32 devices in a mesh: expert: 16 (over z, x, core), tensor: 2 (over y).
Axes of the slice: x: 2, y: 2, z: 4, core: 2. Of those that a mesh axis runs over, the one named last changes fastest.
Arguments:
- tokens: bfloat16 [256, 7168], P('expert', 'tensor'), may hold values from -6 to 6
- expert_ids: int32 [256, 8], P('expert'), may hold values from 0 to 7, as said below
- route_weights: float32 [256, 8], P('expert'), may hold values from 0.05 to 1
- gate_weight: bfloat16 [16, 512, 7168], P('expert', 'tensor'), may hold values from -0.0625 to 0.0625
- up_weight: bfloat16 [16, 512, 7168], P('expert', 'tensor'), may hold values from -0.0625 to 0.0625
- down_weight: bfloat16 [16, 512, 7168], P('expert', 'tensor'), may hold values from -0.1875 to 0.1875
Outputs:
- mixed: bfloat16 [256, 7168], P('expert', 'tensor')
The draws below stay inside these ranges and needn't reach their ends.
Inputs may be any that keep to these rules, and one draw needn't show every extreme that they name: `expert_ids`: each row holds 8 different experts. One expert, the same for all tokens, is named by exactly 16 of the 16 tokens of every block of 16 consecutive tokens; every other expert by at most 16 tokens of a block.
All inputs are finite; a program needn't handle non-finite values.
Results may differ from the reference program's by a relative error of at most 0.015.
Values may be sent and summed in bfloat16 or wider, within the bound.
A program may use at most 64 MiB of HBM per device.

```python
import math
import jax
import jax.numpy as jnp
from jax import lax

D = 7168
TOP = 8
FF = 1024
TOK_DEV = 16
EXPERTS = 8
TOKENS = 256
CAP = 16
N_TENSOR = 2


def draw_expert_ids(key, part):
    hot_expert = jax.random.randint(jax.random.fold_in(key, 7), (), 0, EXPERTS)
    block_keys = jax.random.split(jax.random.fold_in(key, 11), TOKENS // TOK_DEV)
    column = jnp.arange(TOP, dtype=jnp.int32)

    def one_block(block_key):
        key_order = jax.random.fold_in(block_key, 1)
        key_others = jax.random.fold_in(block_key, 2)
        key_columns = jax.random.fold_in(block_key, 3)
        position = jax.random.permutation(key_order, TOK_DEV).astype(jnp.int32)
        others = jax.random.permutation(key_others, EXPERTS - 1).astype(jnp.int32)
        others = others + (others >= hot_expert).astype(jnp.int32)
        is_hot = position < CAP
        offset = jnp.where(is_hot, position * (TOP - 1), CAP * (TOP - 1) + (position - CAP) * TOP)
        shifted = is_hot.astype(jnp.int32)
        index_table = jnp.mod(offset[:, None] + column[None, :] - shifted[:, None], EXPERTS - 1)
        rows = others[index_table]
        rows = jnp.where(is_hot[:, None] & (column[None, :] == 0), hot_expert, rows)
        scores = jax.random.randint(key_columns, (TOK_DEV, TOP), 0, 1 << 20) * TOP + column[None, :]
        order = jnp.argsort(scores, axis=1)
        return jnp.take_along_axis(rows, order, axis=1)
    result = jax.vmap(one_block)(block_keys)
    return result.reshape(TOKENS, TOP).astype(jnp.int32)


def block_scale(stream_key, dims, pieces, smallest, top_value):
    level, own = 1.0, jax.random.fold_in(stream_key, 6)
    for dim, parts in pieces:
        heights = jnp.exp(jax.random.uniform(jax.random.fold_in(own, dim), (parts,), jnp.float32, smallest / len(pieces), top_value / len(pieces)))
        level = level * jnp.repeat(heights, dims[dim] // parts).reshape([-1 if axis == dim else 1 for axis in range(len(dims))])
    return level


def noise(stream_key, dims, width, limit, cuts=(), held_as=jnp.bfloat16):
    values = jax.random.normal(stream_key, dims, jnp.float32) * width
    if len(cuts) > 0:
        values = block_scale(stream_key, dims, cuts, -0.22, 0.18) * values
    return jnp.clip(values, min=-limit, max=limit).astype(held_as)


def setup_inputs(seed: int = 0) -> dict:
    key_of = jax.random.split(jax.random.key(seed), 7)
    return {
        "tokens": noise(key_of[0], (TOKENS, D), 1.0, 6.0, ((0, 16), (1, 2))),
        "expert_ids": draw_expert_ids(jax.random.fold_in(key_of[6], 71), 0),
        "route_weights": jnp.clip(jnp.exp(math.log(1.0) - 2.9957323 * jax.random.uniform(key_of[2], (TOKENS, TOP), jnp.float32) ** block_scale(key_of[2], (TOKENS, TOP), ((0, 16),), -0.2, 0.2)), 0.05, 1.0),
        "gate_weight": noise(key_of[3], (2 * EXPERTS, FF // 2, D), D ** -0.5, 0.0625, ((0, 16), (1, 2))),
        "up_weight": noise(key_of[4], (2 * EXPERTS, FF // 2, D), D ** -0.5, 0.0625, ((0, 16), (1, 2))),
        "down_weight": noise(key_of[5], (2 * EXPERTS, FF // 2, D), FF ** -0.5, 0.1875, ((0, 16), (1, 2))),
    }


def reference(tokens, expert_ids, route_weights, gate_weight, up_weight, down_weight):
    block_count = TOKENS // TOK_DEV
    slot_count = block_count * CAP
    unit_count = FF // (2 * N_TENSOR)
    expert_range = jnp.arange(EXPERTS, dtype=jnp.int32)
    onehot = jnp.sum((expert_ids[:, :, None] == expert_range[None, None, :]).astype(jnp.int32), axis=1)
    onehot_blocks = onehot.reshape(block_count, TOK_DEV, EXPERTS)
    earlier_count = (jnp.cumsum(onehot_blocks, axis=1) - onehot_blocks).reshape(TOKENS, EXPERTS)
    slot_rank = jnp.take_along_axis(earlier_count, expert_ids, axis=1)
    token_range = jnp.arange(TOKENS, dtype=jnp.int32)
    slot_index = (token_range // TOK_DEV)[:, None] * CAP + slot_rank
    token_table = jnp.full((EXPERTS, slot_count), TOKENS, dtype=jnp.int32)
    token_table = token_table.at[expert_ids, slot_index].set(jnp.broadcast_to(token_range[:, None], expert_ids.shape))
    padded = jnp.concatenate([tokens, jnp.zeros((1, D), jnp.bfloat16)], axis=0)

    def run_expert(expert):
        expert_rows = padded[token_table[expert]]
        halves = []
        for half in range(2):
            entry = 2 * expert + half
            gate_act = jnp.dot(expert_rows, gate_weight[entry].T, preferred_element_type=jnp.float32)
            up_act = jnp.dot(expert_rows, up_weight[entry].T, preferred_element_type=jnp.float32)
            hidden = (jax.nn.silu(gate_act) * up_act).astype(jnp.bfloat16)
            hidden_groups = hidden.reshape(slot_count, N_TENSOR, unit_count).astype(jnp.float32)
            down_groups = down_weight[entry].reshape(N_TENSOR, unit_count, D).astype(jnp.float32)
            group_terms = jnp.einsum("rgf,gfd->grd", hidden_groups, down_groups).astype(jnp.bfloat16)
            group_terms = lax.optimization_barrier(group_terms)
            halves.append(jnp.sum(group_terms.astype(jnp.float32), axis=0).astype(jnp.bfloat16))
        return jnp.stack(halves, axis=0)

    half_out = lax.map(run_expert, expert_range)
    picked = half_out[expert_ids, 0, slot_index].astype(jnp.float32) + half_out[expert_ids, 1, slot_index].astype(jnp.float32)
    mixed = jnp.sum(route_weights[:, :, None] * picked, axis=1)
    return mixed.astype(jnp.bfloat16)
```

```python
import functools

import jax
import jax.numpy as jnp
from jax import lax
from jax.experimental import pallas as pl
from jax.experimental.pallas import tpu as pltpu
from jax.sharding import PartitionSpec as P

LANES = 128


def rows_times(rows, weight):
    return lax.dot_general(
        rows, weight, (((1,), (1,)), ((), ())), preferred_element_type=jnp.float32
    )


def sparse_body(tokens, expert_ids, route_weights, gate_weight, up_weight, down_weight):
    devices_wide = lax.axis_size("expert")
    experts = devices_wide // 2
    tok_count = expert_ids.shape[0]
    per_token = expert_ids.shape[1]
    capacity = min(tok_count, tok_count * per_token // experts)
    slot_count = experts * capacity
    arrived_count = devices_wide * capacity
    expert_range = jnp.arange(experts, dtype=jnp.int32)
    onehot = jnp.sum(
        (expert_ids[:, :, None] == expert_range[None, None, :]).astype(jnp.int32), axis=1
    )
    token_range = jnp.arange(tok_count, dtype=jnp.int32)
    earlier = token_range[None, :, None] < token_range[:, None, None]
    earlier_count = jnp.sum(jnp.where(earlier, onehot[None, :, :], 0), axis=1)
    slot_rank = jnp.take_along_axis(earlier_count, expert_ids, axis=1)
    slot_of = expert_ids * capacity + slot_rank
    slot_range = jnp.arange(slot_count, dtype=jnp.int32)
    select = jnp.any(slot_of[None, :, :] == slot_range[:, None, None], axis=2).astype(jnp.bfloat16)
    weight_gate = gate_weight[0]
    weight_up = up_weight[0]
    weight_out = down_weight[0]
    whole_rows = lax.all_gather(tokens, "tensor", axis=1, tiled=True)
    packed = jnp.dot(select, whole_rows, preferred_element_type=jnp.float32).astype(jnp.bfloat16)
    packed = packed.reshape(experts, capacity, whole_rows.shape[1])
    arrived = lax.all_to_all(
        jnp.repeat(packed, 2, axis=0), "expert", split_axis=0, concat_axis=0, tiled=True
    ).reshape(arrived_count, -1)
    gate_act = rows_times(arrived, weight_gate)
    up_act = rows_times(arrived, weight_up)
    hidden = (jax.nn.silu(gate_act) * up_act).astype(jnp.bfloat16)
    columns = lax.all_to_all(weight_out, "tensor", split_axis=1, concat_axis=0, tiled=True)
    unit_count = hidden.shape[1]
    shard_piece = lax.all_gather(hidden, "tensor", axis=1, tiled=True)
    groups = shard_piece.shape[1] // unit_count
    weight_rows = columns
    weight_rows = weight_rows.reshape(groups, unit_count, columns.shape[1])
    grouped = shard_piece.reshape(shard_piece.shape[0], groups, unit_count)
    group_terms = jnp.einsum(
        "rgf,gfd->grd", grouped, weight_rows, preferred_element_type=jnp.float32
    ).astype(jnp.bfloat16)
    group_terms = lax.optimization_barrier(group_terms)
    half_out = jnp.sum(group_terms.astype(jnp.float32), axis=0).astype(jnp.bfloat16)
    returned = lax.all_to_all(
        half_out.reshape(devices_wide, capacity, -1),
        "expert",
        split_axis=0,
        concat_axis=0,
        tiled=True,
    )
    returned = returned.reshape(experts, 2, capacity, -1).astype(jnp.float32)
    combined = (returned[:, 0] + returned[:, 1]).reshape(slot_count, -1)
    picked = combined[slot_of]
    mixed_out = jnp.sum(route_weights[:, :, None] * picked, axis=1)
    return mixed_out.astype(jnp.bfloat16)


OWN, FIRST, SECOND, DIAGONAL = range(4)


def fused_kernel(
    widths, late, tok_hbm, ids_ref, rw_ref, gate_hbm, up_hbm, down_hbm, out_ref, *scratch
):
    pieces = len(widths)
    rows = scratch[:pieces]
    (
        gate, up, down, hid, part, diag_buf, first_buf, second_buf, relay_buf, owner_buf,
        late_buf, late_relay, late_diag, late_owner,
        load_sem, row_sem, gz_send, gr_send, ga_send, gb_send, gc_send,
        down_send, down_recv, hid_send, hid_recv,
        rd_sem, ra_sem, rb_sem, rr_sem, rz_send, rz_recv, rc_sem,
        lz_send, lz_recv, ld_sem, la_send, lb_send, lc_send, lo_recv,
    ) = scratch[pieces:]
    nz = rows[0].shape[3]
    me, y = lax.axis_index("expert"), lax.axis_index("tensor")
    c = lax.rem(me, 2)
    x = lax.rem(me // 2, 2)
    z = me // 4
    oc, ox, oy = 1 - c, 1 - x, 1 - y
    tok, wide = out_ref.shape
    half = wide // 2
    early = half - late
    units = gate.shape[0]
    experts = 2 * nz
    blocks = 4 * nz
    count = blocks * tok
    top = ids_ref.shape[0]
    last = pieces - 1
    strip = 2 * LANES
    starts = [sum(widths[:p]) for p in range(pieces)]
    wide_f, narrow = jnp.float32, jnp.bfloat16
    middle = (z == 1) | (z == 2)
    side = jnp.where(lax.rem(z, 2) == 0, z + 1, z - 1)
    far_mid = jnp.where(z < 2, 2, 1)
    far_end = jnp.where(z < 2, 3, 0)
    near = [z, side, far_mid, far_end]
    columns = [
        (x, y),
        (jnp.where(c == 0, ox, x), jnp.where(c == 0, y, oy)),
        (jnp.where(c == 0, x, ox), jnp.where(c == 0, oy, y)),
        (ox, oy),
    ]

    def dev(zz, xx, cc, yy):
        return ((zz * 2 + xx) * 2 + cc, yy)

    def beside(col, cc):
        xx, yy = columns[col]
        return dev(z, xx, cc, yy)

    dev_a, dev_b, dev_c = beside(FIRST, c), beside(SECOND, c), dev(z, x, oc, y)

    def remote(src, dst, send, recv, to):
        return pltpu.make_async_remote_copy(
            src_ref=src, dst_ref=dst, send_sem=send, recv_sem=recv,
            device_id=to, device_id_type=pl.DeviceIdType.MESH,
        )

    tok_loads = [
        pltpu.make_async_copy(
            tok_hbm.at[:, pl.ds(starts[p], widths[p])],
            rows[p].at[y, c, x, z, :, pl.ds(0, widths[p])],
            load_sem.at[p],
        )
        for p in range(pieces)
    ]
    gate_load = pltpu.make_async_copy(gate_hbm.at[0], gate, load_sem.at[pieces])
    up_load = pltpu.make_async_copy(up_hbm.at[0], up, load_sem.at[pieces + 1])

    def down_rows(cc, yy):
        return (
            down_hbm.at[0, :, pl.ds(pl.multiple_of((2 * yy + cc) * half, LANES), half)],
            down.at[yy, pl.ds(pl.multiple_of(c * units, units), units)],
        )

    down_loads = [
        pltpu.make_async_copy(*down_rows(c, yy), load_sem.at[pieces + 2 + yy]) for yy in range(2)
    ]
    for load in tok_loads + [gate_load, up_load] + down_loads:
        load.start()
    ids = ids_ref[...].astype(wide_f).T
    weights = rw_ref[...].T
    lane = lax.broadcasted_iota(jnp.int32, (tok, LANES), 1)
    which = lax.rem(lane, experts).astype(wide_f)
    spread = jnp.zeros((tok, LANES), wide_f)
    for j in range(top):
        spread = jnp.where(ids[:, j : j + 1] == which, weights[:, j : j + 1], spread)
    first = spread.astype(narrow).astype(wide_f)
    rest = spread - first
    second = rest.astype(narrow).astype(wide_f)
    third = rest - second
    parts = jnp.where(lane < experts, first, jnp.where(lane < 2 * experts, second, third))
    parts = jnp.where(lane < 3 * experts, parts, 0.0)
    rows[0][y, c, x, z, :, widths[0] :] = parts.astype(narrow)

    barrier = pltpu.get_barrier_semaphore()
    partners = [dev(zz, x, cc, y) for zz in near[1:] for cc in (c, oc)]
    partners += [beside(col, cc) for col in (FIRST, SECOND) for cc in (c, oc)] + [dev_c]
    for to in partners:
        pl.semaphore_signal(barrier, inc=1, device_id=to, device_id_type=pl.DeviceIdType.MESH)
    for load in tok_loads:
        load.wait()
    pl.semaphore_wait(barrier, len(partners))

    def row_copy(p, yy, cc, xx, zz, send, to):
        ref = rows[p].at[yy, cc, xx, zz]
        return remote(ref, ref, send, row_sem.at[p, yy, cc, xx, zz], to)

    def z_copy(p, col, k):
        xx, yy = columns[col]
        return row_copy(p, yy, c, xx, z, gz_send.at[p, col, k], dev(near[k], x, c, y))

    def relay_copy(p, col):
        xx, yy = columns[col]
        return row_copy(p, yy, c, xx, far_end, gr_send.at[p, col], dev(side, x, c, y))

    def a_copy(p, zz):
        return row_copy(p, y, c, x, zz, ga_send.at[p, zz], dev_a)

    def b_copy(p, col, zz):
        xx, yy = columns[col]
        return row_copy(p, yy, c, xx, zz, gb_send.at[p, col, zz], dev_b)

    def c_copy(p, col, zz):
        xx, yy = columns[col]
        return row_copy(p, yy, c, xx, zz, gc_send.at[p, yy, xx, zz], dev_c)

    def in_middle(action):
        @pl.when(middle)
        def _():
            action()

    def at_ends(action):
        @pl.when(jnp.logical_not(middle))
        def _():
            action()

    def to_planes(p, col):
        z_copy(p, col, 1).start()
        z_copy(p, col, 2).start()
        in_middle(lambda: z_copy(p, col, 3).start())

    def column_sends(p, zz):
        a_copy(p, zz).start()
        b_copy(p, OWN, zz).start()

    def arrive(p, col, k):
        zz = near[k]
        c_copy(p, col, zz).wait_recv()
        if k == 3 and (col == OWN or p == last):
            in_middle(lambda: relay_copy(p, col).start())
        if p == last and k == 0:
            if col == FIRST:
                b_copy(p, FIRST, zz).start()
            to_planes(p, col)
        if p < last:
            if col == OWN:
                column_sends(p, zz)
            elif col == FIRST:
                b_copy(p, FIRST, zz).start()
        c_copy(p, col, zz).start()

    def from_core(p, yy):
        def step(k, carry):
            xx, zz = k // nz, lax.rem(k, nz)
            ref = rows[p].at[yy, oc, xx, zz]
            remote(ref, ref, gc_send.at[p, yy, xx, zz], row_sem.at[p, yy, oc, xx, zz], dev_c).wait_recv()
            return carry

        lax.fori_loop(0, 2 * nz, step, 0)

    contract = (((1,), (1,)), ((), ()))

    def share(p, yy):
        from_core(p, yy)
        block = rows[p][yy, :, :, :, :, : widths[p]].reshape(count, widths[p])
        cols = pl.ds(pl.multiple_of(yy * wide + starts[p], LANES), widths[p])
        g = lax.dot_general(block, gate[:, cols], contract, preferred_element_type=wide_f)
        u = lax.dot_general(block, up[:, cols], contract, preferred_element_type=wide_f)
        return g, u

    column_sends(last, z)
    for p in range(last):
        to_planes(p, OWN)
        column_sends(p, z)
    to_planes(last, OWN)
    for p in range(pieces):
        c_copy(p, OWN, z).start()
    down_copies = []
    for yy in range(2):
        src, dst = down_rows(oc, yy)
        down_copies.append(remote(src, dst, down_send.at[yy], down_recv.at[yy], dev_c))
    for copy in down_copies:
        copy.start()

    loads_waited = False
    sums = None
    for step in gather_order(last):
        if step[0] == "share":
            if not loads_waited:
                gate_load.wait()
                up_load.wait()
                loads_waited = True
            g, u = share(step[1], y if step[2] == 0 else oy)
            sums = (g, u) if sums is None else (sums[0] + g, sums[1] + u)
        else:
            arrive(*step)
    gate_act, up_act = sums
    lanes = lax.broadcasted_iota(jnp.int32, (count, LANES), 1)
    mine = (lax.rem(lanes, experts) == me // 2) & (lanes < 3 * experts)
    kept = rows[0][0, :, :, :, :, widths[0] :].reshape(count, LANES).astype(wide_f)
    scale = jnp.sum(jnp.where(mine, kept, 0.0), axis=1, keepdims=True)
    hid_cols = pl.ds(pl.multiple_of(c * units, units), units)
    hid[:, hid_cols] = (jax.nn.silu(gate_act) * up_act * scale).astype(narrow)
    hid_copy = remote(hid.at[:, hid_cols], hid.at[:, hid_cols], hid_send, hid_recv, dev_c)
    hid_copy.start()
    for load in down_loads:
        load.wait()
    for copy in down_copies:
        copy.wait_recv()
    hid_copy.wait_recv()

    def project(yy, begin, end):
        def step(k, carry):
            cols = pl.ds(pl.multiple_of(k * strip, LANES), strip)
            term = jnp.dot(hid[...], down[yy, :, cols], preferred_element_type=wide_f)
            part[yy, :, :, :, :, cols] = term.astype(narrow).reshape(2, 2, nz, tok, strip)
            return carry

        lax.fori_loop(begin, end, step, 0)

    soon, later = pl.ds(0, early), pl.ds(early, late)

    def part_at(col, zz, cols, cc=slice(None)):
        xx, yy = columns[col]
        return part.at[yy, cc, xx, zz, :, cols]

    def add_into(ref, buf):
        ref[...] = (ref[...].astype(wide_f) + buf[...].astype(wide_f)).astype(narrow)

    def rd(zz):
        return remote(part_at(DIAGONAL, zz, soon), diag_buf.at[zz], rd_sem.at[0, zz], rd_sem.at[1, zz], dev_b)

    def rb(zz):
        return remote(part_at(SECOND, zz, soon), second_buf.at[zz], rb_sem.at[0, zz], rb_sem.at[1, zz], dev_b)

    def ra(zz):
        return remote(part_at(FIRST, zz, soon), first_buf.at[zz], ra_sem.at[0, zz], ra_sem.at[1, zz], dev_a)

    def rr():
        return remote(part_at(OWN, far_end, soon), relay_buf, rr_sem.at[0], rr_sem.at[1], dev(side, x, c, y))

    def rz(k, cc):
        zz = near[k]
        return remote(
            part_at(OWN, zz, soon, cc), owner_buf.at[c, z], rz_send.at[cc, k], rz_recv.at[c, z], dev(zz, x, cc, y)
        )

    def rc():
        return remote(part_at(OWN, z, soon, oc), owner_buf.at[c, z], rc_sem, rz_recv.at[c, z], dev_c)

    def from_plane(j, zz):
        ref = owner_buf.at[j, zz]
        remote(ref, ref, rz_send.at[0, 0], rz_recv.at[j, zz], dev_c).wait_recv()

    def plane(zz):
        return part.at[:, :, :, zz, :, later]

    def lz(k):
        return remote(plane(near[k]), late_buf.at[z], lz_send.at[k], lz_recv.at[z], dev(near[k], x, c, y))

    def lr():
        return remote(plane(far_end), late_relay, lz_send.at[3], lz_recv.at[nz], dev(side, x, c, y))

    def from_late(k, buf):
        remote(buf, buf, lz_send.at[0], lz_recv.at[near[k]], dev_c).wait_recv()

    def ld():
        return remote(part_at(DIAGONAL, z, later), late_diag, ld_sem.at[0], ld_sem.at[1], dev_b)

    def la(cc):
        return remote(
            part_at(FIRST, z, later, cc), late_owner.at[c, 0], la_send.at[cc], lo_recv.at[c, 0], beside(FIRST, cc)
        )

    def lb(cc):
        return remote(
            part_at(SECOND, z, later, cc), late_owner.at[c, 1], lb_send.at[cc], lo_recv.at[c, 1], beside(SECOND, cc)
        )

    def lc():
        return remote(part_at(OWN, z, later, oc), late_owner.at[c, 2], lc_send, lo_recv.at[c, 2], dev_c)

    def from_late_owner(j, s):
        ref = late_owner.at[j, s]
        remote(ref, ref, lc_send, lo_recv.at[j, s], dev_c).wait_recv()

    order = [3, 2, 1, 0]

    for yy in range(2):
        project(yy, early // strip, half // strip)
    at_ends(lambda: lr().start())
    lz(2).start()
    lz(1).start()
    for yy in range(2):
        project(yy, 0, early // strip)
    for k in order:
        rd(near[k]).start()
    for k in order:
        rb(near[k]).start()

    def turn(k):
        zz = near[k]
        rd(zz).wait_recv()
        add_into(part_at(FIRST, zz, soon), diag_buf.at[zz])
        ra(zz).start()

    def column_sum(k):
        zz = near[k]
        ra(zz).wait_recv()
        rb(zz).wait_recv()
        own = part_at(OWN, zz, soon)
        total = own[...].astype(wide_f) + first_buf[zz].astype(wide_f) + second_buf[zz].astype(wide_f)
        own[...] = total.astype(narrow)

    def home(k):
        column_sum(k)
        if k == 3:
            at_ends(lambda: rr().start())
        elif k == 0:
            rc().start()
        else:
            for cc in range(2):
                rz(k, cc).start()

    def relay_home():
        rr().wait_recv()
        add_into(part_at(OWN, far_end, soon), relay_buf)
        for cc in range(2):
            rz(3, cc).start()

    def late_pass():
        lr().wait_recv()
        add_into(plane(far_end), late_relay)
        lz(3).start()

    def late_sum():
        from_late(1, late_buf.at[side])
        from_late(2, late_buf.at[far_mid])
        target = plane(z)
        total = target[...].astype(wide_f) + late_buf[side].astype(wide_f) + late_buf[far_mid].astype(wide_f)
        target[...] = total.astype(narrow)

    turn(3)
    in_middle(late_pass)
    turn(2)
    turn(1)
    turn(0)
    home(3)
    late_sum()
    in_middle(lambda: (from_late(3, late_buf.at[far_end]), add_into(plane(z), late_buf.at[far_end])))
    ld().start()
    for cc in range(2):
        lb(cc).start()
    lc().start()
    home(2)
    in_middle(relay_home)
    home(1)
    ld().wait_recv()
    add_into(part_at(FIRST, z, later), late_diag)
    for cc in range(2):
        la(cc).start()
    home(0)

    for s in range(3):
        from_late_owner(oc, s)
    for s in range(2):
        from_late_owner(c, s)
    late_mine = part_at(OWN, z, later, c)[...]
    for j, own in ((c, True), (oc, False)):
        total = late_owner[j, 0].astype(wide_f) + late_owner[j, 1].astype(wide_f)
        total = total + (late_mine if own else late_owner[j, 2]).astype(wide_f)
        out_ref[:, pl.ds(pl.multiple_of(j * half + early, LANES), late)] = total.astype(narrow)
    for j, own in ((c, True), (oc, False)):
        if not own:
            from_plane(j, z)
        from_plane(j, side)
        from_plane(j, far_mid)
        total = owner_buf[j, side].astype(wide_f) + owner_buf[j, far_mid].astype(wide_f)
        total = total + (part_at(OWN, z, soon, c)[...] if own else owner_buf[j, z]).astype(wide_f)
        at = pl.ds(pl.multiple_of(j * half, LANES), early)

        @pl.when(middle)
        def _():
            from_plane(j, far_end)
            out_ref[:, at] = (total + owner_buf[j, far_end].astype(wide_f)).astype(narrow)

        @pl.when(jnp.logical_not(middle))
        def _():
            out_ref[:, at] = total.astype(narrow)

    for p in range(pieces):
        reach = 4 if p == last else 1
        for col in range(reach):
            z_copy(p, col, 1).wait_send()
            z_copy(p, col, 2).wait_send()
        in_middle(lambda: [c.wait_send() for col in range(reach) for c in (z_copy(p, col, 3), relay_copy(p, col))])
        if p == last:
            a_copy(p, z).wait_send()
            b_copy(p, OWN, z).wait_send()
            b_copy(p, FIRST, z).wait_send()

    def drain(zz, carry):
        for p in range(pieces):
            for col in range(4):
                c_copy(p, col, zz).wait_send()
            if p < last:
                a_copy(p, zz).wait_send()
                b_copy(p, OWN, zz).wait_send()
                b_copy(p, FIRST, zz).wait_send()
        for copy in (rd(zz), rb(zz), ra(zz)):
            copy.wait_send()
        return carry

    lax.fori_loop(0, nz, drain, 0)
    for cc in range(2):
        for copy in (rz(1, cc), rz(2, cc), la(cc), lb(cc)):
            copy.wait_send()
    for copy in [rc(), lz(1), lz(2), ld(), lc(), hid_copy] + down_copies:
        copy.wait_send()
    in_middle(lambda: [copy.wait_send() for copy in (rz(3, 0), rz(3, 1), lz(3))])
    at_ends(lambda: [copy.wait_send() for copy in (rr(), lr())])


def gather_order(last):
    steps = []
    for p in range(last):
        for k in range(1, 4):
            steps.append((p, OWN, k))
            steps.append((p, FIRST, k - 1))
            if p == 0 and k == 1:
                steps += [(last, FIRST, 0), (last, SECOND, 0)]
            if p == 0 and k == 2:
                steps.append((last, DIAGONAL, 0))
        steps.append((p, FIRST, 3))
        steps += [(p, col, k) for k in range(4) for col in (SECOND, DIAGONAL)]
        steps += [("share", p, 0), ("share", p, 1)]
        if p == last - 2:
            steps += [(last, col, k) for k in range(1, 4) for col in range(4)]
            steps += [("share", last, 0), ("share", last, 1)]
    return steps


def fused_body(tokens, expert_ids, route_weights, gate_weight, up_weight, down_weight):
    nz = lax.axis_size("expert") // 4
    tok, wide = tokens.shape
    half = wide // 2
    units = gate_weight.shape[1]
    bf16 = jnp.bfloat16
    tiles = wide // (2 * LANES)
    ahead = max(1, tiles * 3 // 14)
    others = tiles - ahead
    widths = [2 * LANES * n for n in ((others + 2) // 3, (others + 1) // 3, others // 3, ahead)]
    late = LANES * max(1, half // LANES * 3 // 14)
    pieces = len(widths)
    early = half - late
    vmem = pl.BlockSpec(memory_space=pltpu.VMEM)
    anywhere = pl.BlockSpec(memory_space=pl.ANY)
    sems = pltpu.SemaphoreType.DMA
    spare = [LANES] + [0] * (pieces - 1)
    return pl.pallas_call(
        functools.partial(fused_kernel, widths, late),
        out_shape=jax.ShapeDtypeStruct((tok, wide), bf16),
        in_specs=[anywhere, vmem, vmem] + [anywhere] * 3,
        out_specs=vmem,
        scratch_shapes=[pltpu.VMEM((2, 2, 2, nz, tok, w + s), bf16) for w, s in zip(widths, spare)]
        + [
            pltpu.VMEM((units, 2 * wide), bf16),
            pltpu.VMEM((units, 2 * wide), bf16),
            pltpu.VMEM((2, 2 * units, half), bf16),
            pltpu.VMEM((4 * nz * tok, 2 * units), bf16),
            pltpu.VMEM((2, 2, 2, nz, tok, half), bf16),
        ]
        + [pltpu.VMEM((nz, 2, tok, early), bf16)] * 3
        + [
            pltpu.VMEM((2, tok, early), bf16),
            pltpu.VMEM((2, nz, tok, early), bf16),
            pltpu.VMEM((nz, 2, 2, 2, tok, late), bf16),
            pltpu.VMEM((2, 2, 2, tok, late), bf16),
            pltpu.VMEM((2, tok, late), bf16),
            pltpu.VMEM((2, 3, tok, late), bf16),
            sems((pieces + 4,)),
            sems((pieces, 2, 2, 2, nz)),
            sems((pieces, 4, 4)),
            sems((pieces, 4)),
            sems((pieces, nz)),
            sems((pieces, 2, nz)),
            sems((pieces, 2, 2, nz)),
            sems((2,)),
            sems((2,)),
            sems,
            sems,
            sems((2, nz)),
            sems((2, nz)),
            sems((2, nz)),
            sems((2,)),
            sems((2, 4)),
            sems((2, nz)),
            sems,
            sems((4,)),
            sems((nz + 1,)),
            sems((2,)),
            sems((2,)),
            sems((2,)),
            sems,
            sems((2, 3)),
        ],
        compiler_params=pltpu.CompilerParams(
            collective_id=0, has_side_effects=True, vmem_limit_bytes=60 * 2**20
        ),
    )(tokens, expert_ids.T, route_weights.T, gate_weight, up_weight, down_weight)


def body(*args):
    every = args[1].shape[1] == lax.axis_size("expert") // 2
    tok, wide = args[0].shape
    even = lax.axis_size("tensor") == 2 and lax.axis_size("expert") == 16
    fits = tok % 16 == 0 and wide % 512 == 0 and 3 * args[1].shape[1] <= LANES
    if every and even and fits:
        return fused_body(*args)
    return sparse_body(*args)


def solution(mesh):
    placed = (
        P("expert", "tensor"),
        P("expert", None),
        P("expert", None),
        P("expert", "tensor", None),
        P("expert", "tensor", None),
        P("expert", "tensor", None),
    )
    return jax.shard_map(
        body, mesh=mesh, in_specs=placed, out_specs=P("expert", "tensor"), check_vma=False
    )
```

```python
import functools

import jax
import jax.numpy as jnp
from jax import lax
from jax.experimental import pallas as pl
from jax.experimental.pallas import tpu as pltpu
from jax.sharding import PartitionSpec as P

LANES = 128


def rows_times(rows, weight):
    return lax.dot_general(
        rows, weight, (((1,), (1,)), ((), ())), preferred_element_type=jnp.float32
    )


def sparse_body(tokens, expert_ids, route_weights, gate_weight, up_weight, down_weight):
    devices_wide = lax.axis_size("expert")
    experts = devices_wide // 2
    tok_count = expert_ids.shape[0]
    per_token = expert_ids.shape[1]
    capacity = min(tok_count, tok_count * per_token // experts)
    slot_count = experts * capacity
    arrived_count = devices_wide * capacity
    expert_range = jnp.arange(experts, dtype=jnp.int32)
    onehot = jnp.sum(
        (expert_ids[:, :, None] == expert_range[None, None, :]).astype(jnp.int32), axis=1
    )
    token_range = jnp.arange(tok_count, dtype=jnp.int32)
    earlier = token_range[None, :, None] < token_range[:, None, None]
    earlier_count = jnp.sum(jnp.where(earlier, onehot[None, :, :], 0), axis=1)
    slot_rank = jnp.take_along_axis(earlier_count, expert_ids, axis=1)
    slot_of = expert_ids * capacity + slot_rank
    slot_range = jnp.arange(slot_count, dtype=jnp.int32)
    select = jnp.any(slot_of[None, :, :] == slot_range[:, None, None], axis=2).astype(jnp.bfloat16)
    weight_gate = gate_weight[0]
    weight_up = up_weight[0]
    weight_out = down_weight[0]
    whole_rows = lax.all_gather(tokens, "tensor", axis=1, tiled=True)
    packed = jnp.dot(select, whole_rows, preferred_element_type=jnp.float32).astype(jnp.bfloat16)
    packed = packed.reshape(experts, capacity, whole_rows.shape[1])
    arrived = lax.all_to_all(
        jnp.repeat(packed, 2, axis=0), "expert", split_axis=0, concat_axis=0, tiled=True
    ).reshape(arrived_count, -1)
    gate_act = rows_times(arrived, weight_gate)
    up_act = rows_times(arrived, weight_up)
    hidden = (jax.nn.silu(gate_act) * up_act).astype(jnp.bfloat16)
    columns = lax.all_to_all(weight_out, "tensor", split_axis=1, concat_axis=0, tiled=True)
    unit_count = hidden.shape[1]
    shard_piece = lax.all_gather(hidden, "tensor", axis=1, tiled=True)
    groups = shard_piece.shape[1] // unit_count
    weight_rows = columns
    weight_rows = weight_rows.reshape(groups, unit_count, columns.shape[1])
    grouped = shard_piece.reshape(shard_piece.shape[0], groups, unit_count)
    group_terms = jnp.einsum(
        "rgf,gfd->grd", grouped, weight_rows, preferred_element_type=jnp.float32
    ).astype(jnp.bfloat16)
    group_terms = lax.optimization_barrier(group_terms)
    half_out = jnp.sum(group_terms.astype(jnp.float32), axis=0).astype(jnp.bfloat16)
    returned = lax.all_to_all(
        half_out.reshape(devices_wide, capacity, -1),
        "expert",
        split_axis=0,
        concat_axis=0,
        tiled=True,
    )
    returned = returned.reshape(experts, 2, capacity, -1).astype(jnp.float32)
    combined = (returned[:, 0] + returned[:, 1]).reshape(slot_count, -1)
    picked = combined[slot_of]
    mixed_out = jnp.sum(route_weights[:, :, None] * picked, axis=1)
    return mixed_out.astype(jnp.bfloat16)


OWN, FIRST, SECOND, DIAGONAL = range(4)
HERE, SIDE, FAR_MID, FAR_END = range(4)
GATHER = (
    ('a', 2), ('zn', 0), ('bd', 0, 0), ('a', 0), ('a', 1), ('zf', 0), ('bd', 1, 0), ('bd', 2, 0), ('zf', 1),
    ('own', 0, 1), ('zn', 1), ('first', 2, 0), ('bd', 0, 1), ('first', 1, 0), ('own', 0, 2), ('first', 0, 0),
    ('own', 1, 2), ('here',), ('own', 1, 1), ('first', 0, 1), ('bd', 0, 2), ('bd', 1, 2), ('bd', 1, 1), ('own', 0, 3),
    ('bd', 0, 3), ('first', 0, 2), ('own', 1, 3), ('bd', 1, 3), ('plane', 1), ('first', 0, 3), ('cs', 0),
    ('first', 1, 1), ('cf', 0), ('plane', 2), ('first', 1, 2), ('co', 0), ('co', 1), ('cs', 1), ('first', 1, 3),
    ('cf', 1), ('plane', 3), ('cd', 0), ('share', 0, 0), ('cd', 1), ('share', 1, 0), ('share', 2, 1), ('share', 2, 0),
    ('share', 0, 1), ('share', 1, 1),
)
SCATTER = (
    ('downL',), ('lz', 3), ('down', 0), ('rd', 3, 0), ('down', 1), ('rd', 1, 1), ('rd', 3, 1), ('rd', 1, 0),
    ('lz', 2), ('rb', 2, 0), ('rb', 3, 1), ('rd', 2, 0), ('rd', 2, 1), ('rd', 0, 1), ('lz', 1), ('turn', 3, 0),
    ('rb', 1, 0), ('rb', 3, 0), ('lrelay',), ('turn', 2, 0), ('rd', 0, 0), ('turn', 3, 1), ('turn', 0, 1),
    ('turn', 1, 0), ('home', 3, 0), ('turn', 2, 1), ('rb', 0, 1), ('rb', 1, 1), ('home', 2, 0), ('rb', 0, 0),
    ('rb', 2, 1), ('home', 3, 1), ('turn', 1, 1), ('turn', 0, 0), ('lsum',), ('ld',), ('relay', 0), ('home', 1, 0),
    ('relay', 1), ('home', 2, 1), ('lb',), ('home', 0, 1), ('home', 1, 1), ('lc',), ('home', 0, 0), ('lturn',),
)


def fused_kernel(
    widths, cuts, tok_hbm, ids_hbm, rw_hbm, gate_hbm, up_hbm, down_hbm, out_ref, *scratch
):
    pieces, splits = len(widths), len(cuts) - 1
    rows, scratch = scratch[:pieces], scratch[pieces:]
    parts, scratch = scratch[: splits + 1], scratch[splits + 1 :]
    diag_bufs, scratch = scratch[:splits], scratch[splits:]
    first_bufs, scratch = scratch[:splits], scratch[splits:]
    second_bufs, scratch = scratch[:splits], scratch[splits:]
    relay_bufs, scratch = scratch[:splits], scratch[splits:]
    owner_bufs, scratch = scratch[:splits], scratch[splits:]
    (
        gate, up, down, hid, ids_buf, rw_buf, late_buf, late_relay, late_diag, late_owner,
        load_sem, own_recv, first_recv, side_recv, plane_recv, core_recv, gz_send, gr_send, ga_send, gb_send, gc_send,
        down_send, down_recv, hid_send, hid_recv,
        rd_send, rd_recv, ra_send, ra_recv, rb_send, rb_recv, rr_send, rr_recv, rz_send, rz_recv, rc_send,
        lz_send, lz_recv, lr_send, lr_recv, ld_send, ld_recv, la_send, lb_send, lc_send, lo_recv,
    ) = scratch
    nz = rows[0].shape[2]
    me, y = lax.axis_index("expert"), lax.axis_index("tensor")
    c = lax.rem(me, 2)
    x = lax.rem(me // 2, 2)
    z = me // 4
    oc, ox, oy = 1 - c, 1 - x, 1 - y
    tok, wide = out_ref.shape
    half = wide // 2
    units = gate.shape[0]
    experts = 2 * nz
    count = 4 * nz * tok
    top = ids_hbm.shape[0]
    last = pieces - 1
    starts = [sum(widths[:p]) for p in range(pieces)]
    wide_f, narrow = jnp.float32, jnp.bfloat16
    middle = (z > 0) & (z < nz - 1)
    side = jnp.where(lax.rem(z, 2) == 0, z + 1, z - 1)
    low = z < nz // 2
    near = [z, side, jnp.where(low, nz // 2, nz // 2 - 1), jnp.where(low, nz - 1, 0)]
    far_end = near[FAR_END]
    columns = [
        (x, y),
        (jnp.where(c == 0, ox, x), jnp.where(c == 0, y, oy)),
        (jnp.where(c == 0, x, ox), jnp.where(c == 0, oy, y)),
        (ox, oy),
    ]

    def dev(zz, xx, cc, yy):
        return ((zz * 2 + xx) * 2 + cc, yy)

    def beside(col, cc):
        xx, yy = columns[col]
        return dev(z, xx, cc, yy)

    dev_a, dev_b, dev_c = beside(FIRST, c), beside(SECOND, c), dev(z, x, oc, y)
    dev_side = dev(side, x, c, y)

    def in_middle(action):
        @pl.when(middle)
        def _():
            action()

    def at_ends(action):
        @pl.when(jnp.logical_not(middle))
        def _():
            action()

    def remote(src, dst, send, recv, to):
        return pltpu.make_async_remote_copy(
            src_ref=src, dst_ref=dst, send_sem=send, recv_sem=recv,
            device_id=to, device_id_type=pl.DeviceIdType.MESH,
        )

    barrier = pltpu.get_barrier_semaphore()

    def greet(to):
        pl.semaphore_signal(barrier, inc=1, device_id=to, device_id_type=pl.DeviceIdType.MESH)

    partners = [dev(near[k], x, cc, y) for k in (FAR_MID, SIDE) for cc in (c, oc)]
    partners += [beside(col, cc) for col in (FIRST, SECOND) for cc in (c, oc)] + [dev_c]

    @pl.when(middle)
    def _():
        for cc in (c, oc):
            greet(dev(far_end, x, cc, y))

    for to in partners:
        greet(to)
    small_loads = [
        pltpu.make_async_copy(ids_hbm, ids_buf, load_sem.at[0]),
        pltpu.make_async_copy(rw_hbm, rw_buf, load_sem.at[1]),
    ]
    tok_loads = [
        pltpu.make_async_copy(
            tok_hbm.at[:, pl.ds(starts[p], widths[p])],
            rows[p].at[y, x, z, c, :, pl.ds(0, widths[p])],
            load_sem.at[2 + p],
        )
        for p in range(pieces)
    ]
    gate_load = pltpu.make_async_copy(gate_hbm.at[0], gate, load_sem.at[pieces + 2])
    up_load = pltpu.make_async_copy(up_hbm.at[0], up, load_sem.at[pieces + 3])

    def down_rows(cc, yy):
        return (
            down_hbm.at[0, :, pl.ds(pl.multiple_of((2 * yy + cc) * half, LANES), half)],
            down.at[yy, pl.ds(pl.multiple_of(c * units, units), units)],
        )

    down_loads = [
        pltpu.make_async_copy(*down_rows(c, yy), load_sem.at[pieces + 4 + yy]) for yy in range(2)
    ]
    for load in small_loads + tok_loads + [gate_load, up_load] + down_loads:
        load.start()
    for load in small_loads:
        load.wait()
    ids = ids_buf[...].astype(wide_f).T
    weights = rw_buf[...].T
    lane = lax.broadcasted_iota(jnp.int32, (tok, LANES), 1)
    which = lax.rem(lane, experts).astype(wide_f)
    spread = jnp.zeros((tok, LANES), wide_f)
    for j in range(top):
        spread = jnp.where(ids[:, j : j + 1] == which, weights[:, j : j + 1], spread)
    first = spread.astype(narrow).astype(wide_f)
    rest = spread - first
    second = rest.astype(narrow).astype(wide_f)
    third = rest - second
    terms = jnp.where(lane < experts, first, jnp.where(lane < 2 * experts, second, third))
    terms = jnp.where(lane < 3 * experts, terms, 0.0)
    rows[0][y, x, z, c, :, widths[0] :] = terms.astype(narrow)
    for load in tok_loads:
        load.wait()
    pl.semaphore_wait(barrier, len(partners) + 2 * middle.astype(jnp.int32))

    def column(p, col, cc=c):
        xx, yy = columns[col]
        return rows[p].at[yy, xx, :, cc]

    def cell(p, col, zz):
        xx, yy = columns[col]
        return rows[p].at[yy, xx, zz, c]

    def layer(zz, cc=c):
        return rows[last].at[:, :, zz, cc]

    def same(ref, send, recv, to):
        return remote(ref, ref, send, recv, to)

    def over_z(k):
        return dev(near[k], x, c, y)

    def z_copy(p, k):
        return same(cell(p, OWN, z), gz_send.at[p, k - 1], own_recv.at[p, z], over_z(k))

    def relay_copy(p):
        return same(cell(p, OWN, far_end), gr_send.at[p], own_recv.at[p, far_end], dev_side)

    def a_copy(p, zz):
        return same(cell(p, OWN, zz), ga_send.at[p], first_recv.at[p, zz], dev_a)

    def b_copy(p, zz):
        return same(cell(p, OWN, zz), gb_send.at[p, 0], side_recv.at[p, 0], dev_b)

    def d_copy(p, zz):
        return same(cell(p, FIRST, zz), gb_send.at[p, 1], side_recv.at[p, 1], dev_b)

    def c_copy(p, col):
        _, yy = columns[col]
        return same(column(p, col), gc_send.at[p, col], core_recv.at[p, yy], dev_c)

    def layer_copy(k):
        return same(layer(z), gz_send.at[last, k - 1], plane_recv.at[z], over_z(k))

    def layer_relay():
        return same(layer(far_end), gr_send.at[last], plane_recv.at[far_end], dev_side)

    def layer_core(zz):
        return same(layer(zz), gc_send.at[last, 0], core_recv.at[last, 0], dev_c)

    def landed(ref, recv):
        same(ref, gr_send.at[last], recv, dev_c).wait_recv()

    def left(ref, send):
        same(ref, send, core_recv.at[last, 0], dev_c).wait_send()

    def to_far(copy):
        copy(FAR_MID).start()

        @pl.when(middle)
        def _():
            copy(FAR_END).start()

    def own(p, k):
        landed(cell(p, OWN, near[k]), own_recv.at[p, near[k]])
        if k == FAR_END:
            in_middle(lambda: relay_copy(p).start())
        a_copy(p, near[k]).start()

    def first_block(p, k):
        landed(cell(p, FIRST, near[k]), first_recv.at[p, near[k]])
        d_copy(p, near[k]).start()

    def sideways(p, j):
        landed(column(p, SECOND + j), side_recv.at[p, j])
        c_copy(p, SECOND + j).start()

    def here():
        for j in range(2):
            landed(cell(last, SECOND + j, z), side_recv.at[last, j])
        to_far(layer_copy)
        layer_copy(SIDE).start()
        layer_core(z).start()

    def layer_in(k):
        landed(layer(near[k]), plane_recv.at[near[k]])
        if k == FAR_END:
            in_middle(lambda: layer_relay().start())
        layer_core(near[k]).start()

    contract = (((1,), (1,)), ((), ()))
    sums, layers_in = [], []

    def share(p, turn_of):
        yy = oy if turn_of else y
        if p < last:
            landed(rows[p].at[yy, :, :, oc], core_recv.at[p, yy])
        elif not layers_in:
            landed(rows[p].at[:, :, :, oc], core_recv.at[p, 0])
            layers_in.append(p)
        if not sums:
            gate_load.wait()
            up_load.wait()
        block = rows[p][yy, :, :, :, :, : widths[p]].reshape(count, widths[p])
        cols = pl.ds(pl.multiple_of(yy * wide + starts[p], LANES), widths[p])
        g = lax.dot_general(block, gate[:, cols], contract, preferred_element_type=wide_f)
        u = lax.dot_general(block, up[:, cols], contract, preferred_element_type=wide_f)
        sums.append((g, u) if not sums else (sums[-1][0] + g, sums[-1][1] + u))

    gather = {
        "zn": lambda p: z_copy(p, SIDE).start(),
        "zf": lambda p: to_far(functools.partial(z_copy, p)),
        "a": lambda p: a_copy(p, z).start(),
        "bd": lambda p, k: b_copy(p, near[k]).start(),
        "own": own,
        "first": first_block,
        "co": lambda p: c_copy(p, OWN).start(),
        "cf": lambda p: c_copy(p, FIRST).start(),
        "cs": lambda p: sideways(p, 0),
        "cd": lambda p: sideways(p, 1),
        "here": here,
        "plane": layer_in,
        "share": share,
    }
    down_copies = []
    for yy in range(2):
        src, dst = down_rows(oc, yy)
        down_copies.append(remote(src, dst, down_send.at[yy], down_recv.at[yy], dev_c))
    started = False
    for name, *where in GATHER:
        if name == "own" and not started:
            for copy in down_copies:
                copy.start()
            started = True
        gather[name](*where)
    gate_act, up_act = sums[-1]
    lanes = lax.broadcasted_iota(jnp.int32, (count, LANES), 1)
    mine = (lax.rem(lanes, experts) == me // 2) & (lanes < 3 * experts)
    kept = rows[0][0, :, :, :, :, widths[0] :].reshape(count, LANES).astype(wide_f)
    scale = jnp.sum(jnp.where(mine, kept, 0.0), axis=1, keepdims=True)
    hid_cols = pl.ds(pl.multiple_of(c * units, units), units)
    hid[:, hid_cols] = (jax.nn.silu(gate_act) * up_act * scale).astype(narrow)
    hid_copy = remote(hid.at[:, hid_cols], hid.at[:, hid_cols], hid_send, hid_recv, dev_c)
    hid_copy.start()
    for load in down_loads:
        load.wait()
    for copy in down_copies:
        copy.wait_recv()
    hid_copy.wait_recv()

    def project(r):
        begin, end = cuts[r], cuts[r + 1] if r < splits else half
        for yy in range(2):
            term = jnp.dot(hid[...], down[yy, :, begin:end], preferred_element_type=wide_f)
            parts[r][yy] = term.astype(narrow).reshape(2, nz, 2, tok, end - begin)

    def block(r, col, zz):
        xx, yy = columns[col]
        return parts[r].at[yy, xx, zz]

    def total(*terms):
        out = terms[0].astype(wide_f)
        for term in terms[1:]:
            out = out + term.astype(wide_f)
        return out

    def rd(k, r):
        zz = near[k]
        return remote(block(r, DIAGONAL, zz), diag_bufs[r].at[zz], rd_send.at[r], rd_recv.at[r, zz], dev_b)

    def rb(k, r):
        zz = near[k]
        return remote(block(r, SECOND, zz), second_bufs[r].at[zz], rb_send.at[r], rb_recv.at[r, zz], dev_b)

    def ra(k, r):
        zz = near[k]
        return remote(block(r, FIRST, zz), first_bufs[r].at[zz], ra_send.at[r], ra_recv.at[r, zz], dev_a)

    def rr(r):
        return remote(block(r, OWN, far_end), relay_bufs[r], rr_send.at[r], rr_recv.at[r], dev_side)

    def rz(k, r, cc):
        zz = near[k]
        return remote(
            block(r, OWN, zz).at[cc], owner_bufs[r].at[c, z], rz_send.at[r, k - 1], rz_recv.at[r, c], dev(zz, x, cc, y)
        )

    def rc(r):
        return remote(block(r, OWN, z).at[oc], owner_bufs[r].at[c, z], rc_send.at[r], rz_recv.at[r, c], dev_c)

    def landed_slots(ref, slots, recv):
        landed(ref.at[pl.ds(0, slots)], recv)

    def plane(zz):
        return parts[splits].at[:, :, zz]

    def lz(k):
        return remote(plane(near[k]), late_buf.at[z], lz_send.at[k - 1], lz_recv, over_z(k))

    def lr():
        return remote(plane(far_end), late_relay, lr_send, lr_recv, dev_side)

    def ld():
        return remote(block(splits, DIAGONAL, z), late_diag, ld_send, ld_recv, dev_b)

    def la(cc):
        return remote(
            block(splits, FIRST, z).at[cc], late_owner.at[c, 0], la_send, lo_recv.at[c], beside(FIRST, cc)
        )

    def lb(cc):
        return remote(
            block(splits, SECOND, z).at[cc], late_owner.at[c, 1], lb_send, lo_recv.at[c], beside(SECOND, cc)
        )

    def lc():
        return remote(block(splits, OWN, z).at[oc], late_owner.at[c, 2], lc_send, lo_recv.at[c], dev_c)

    def send_late(k):
        if k == FAR_END:
            at_ends(lambda: lr().start())
        else:
            lz(k).start()

    def turn(k, r):
        rd(k, r).wait_recv()
        ref = block(r, FIRST, near[k])
        ref[...] = total(ref[...], diag_bufs[r][near[k]]).astype(narrow)
        ra(k, r).start()

    def home(k, r):
        ra(k, r).wait_recv()
        rb(k, r).wait_recv()
        ref = block(r, OWN, near[k])
        ref[...] = total(ref[...], first_bufs[r][near[k]], second_bufs[r][near[k]]).astype(narrow)
        if k == FAR_END:
            at_ends(lambda: rr(r).start())
        elif k == HERE:
            rc(r).start()
        else:
            for cc in range(2):
                rz(k, r, cc).start()

    def relay(r):
        @pl.when(middle)
        def _():
            rr(r).wait_recv()
            ref = block(r, OWN, far_end)
            ref[...] = total(ref[...], relay_bufs[r][...]).astype(narrow)
            for cc in range(2):
                rz(FAR_END, r, cc).start()

    def late_pass():
        @pl.when(middle)
        def _():
            lr().wait_recv()
            ref = plane(far_end)
            ref[...] = total(ref[...], late_relay[...]).astype(narrow)
            lz(FAR_END).start()

    def late_sum():
        ref = plane(z)

        @pl.when(middle)
        def _():
            landed_slots(late_buf, nz - 1, lz_recv)
            ref[...] = total(ref[...], late_buf[side], late_buf[near[FAR_MID]], late_buf[far_end]).astype(narrow)

        @pl.when(jnp.logical_not(middle))
        def _():
            landed_slots(late_buf, nz - 2, lz_recv)
            ref[...] = total(ref[...], late_buf[side], late_buf[near[FAR_MID]]).astype(narrow)

    def late_turn():
        ld().wait_recv()
        ref = block(splits, FIRST, z)
        ref[...] = total(ref[...], late_diag[...]).astype(narrow)
        for cc in range(2):
            la(cc).start()

    def late_out(j):
        core, mine_too = (oc, late_owner.at[oc, 2]) if j else (c, block(splits, OWN, z).at[c])
        landed_slots(late_owner.at[core], 2 + j, lo_recv.at[core])
        at = pl.ds(pl.multiple_of(core * half + cuts[splits], LANES), half - cuts[splits])
        out_ref[:, at] = total(mine_too[...], late_owner[core, 0], late_owner[core, 1]).astype(narrow)

    def out(r, j):
        bufs = owner_bufs[r]
        core, mine_too = (oc, bufs.at[oc, z]) if j else (c, block(r, OWN, z).at[c])
        at = pl.ds(pl.multiple_of(core * half + cuts[r], LANES), cuts[r + 1] - cuts[r])

        @pl.when(middle)
        def _():
            landed_slots(bufs.at[core], nz - 1 + j, rz_recv.at[r, core])
            sums = [bufs[core, near[k]] for k in (SIDE, FAR_MID, FAR_END)]
            out_ref[:, at] = total(mine_too[...], *sums).astype(narrow)

        @pl.when(jnp.logical_not(middle))
        def _():
            landed_slots(bufs.at[core], nz - 2 + j, rz_recv.at[r, core])
            sums = [bufs[core, near[k]] for k in (SIDE, FAR_MID)]
            out_ref[:, at] = total(mine_too[...], *sums).astype(narrow)

    scatter = {
        "downL": lambda: project(splits),
        "down": project,
        "lz": send_late,
        "rd": lambda k, r: rd(k, r).start(),
        "rb": lambda k, r: rb(k, r).start(),
        "turn": turn,
        "home": home,
        "relay": relay,
        "lrelay": late_pass,
        "lsum": late_sum,
        "ld": lambda: ld().start(),
        "lb": lambda: [lb(cc).start() for cc in range(2)],
        "lc": lambda: lc().start(),
        "lturn": late_turn,
    }
    for name, *where in SCATTER:
        scatter[name](*where)
    for r in range(splits):
        for j in range(2):
            out(r, j)
    for j in range(2):
        late_out(j)

    for p in range(last):
        z_copy(p, SIDE).wait_send()
        z_copy(p, FAR_MID).wait_send()
        left(column(p, OWN), ga_send.at[p])
        left(column(p, OWN), gb_send.at[p, 0])
        left(column(p, FIRST), gb_send.at[p, 1])
        for col in range(4):
            c_copy(p, col).wait_send()
    a_copy(last, z).wait_send()
    b_copy(last, z).wait_send()
    d_copy(last, z).wait_send()
    layer_copy(SIDE).wait_send()
    layer_copy(FAR_MID).wait_send()
    left(rows[last].at[:, :, :, c], gc_send.at[last, 0])
    for r in range(splits):
        left(first_bufs[r], ra_send.at[r])
        left(diag_bufs[r], rd_send.at[r])
        left(second_bufs[r], rb_send.at[r])
        left(relay_bufs[r], rz_send.at[r, SIDE - 1])
        left(relay_bufs[r], rz_send.at[r, FAR_MID - 1])
        rc(r).wait_send()
    left(late_diag, la_send)
    left(late_diag, lb_send)
    for copy in [lz(SIDE), lz(FAR_MID), ld(), lc(), hid_copy] + down_copies:
        copy.wait_send()

    @pl.when(middle)
    def _():
        for p in range(last):
            z_copy(p, FAR_END).wait_send()
            relay_copy(p).wait_send()
        layer_copy(FAR_END).wait_send()
        layer_relay().wait_send()
        lz(FAR_END).wait_send()
        for r in range(splits):
            left(relay_bufs[r], rz_send.at[r, FAR_END - 1])

    @pl.when(jnp.logical_not(middle))
    def _():
        lr().wait_send()
        for r in range(splits):
            rr(r).wait_send()


def fused_body(tokens, expert_ids, route_weights, gate_weight, up_weight, down_weight):
    nz = lax.axis_size("expert") // 4
    tok, wide = tokens.shape
    half = wide // 2
    units = gate_weight.shape[1]
    bf16 = jnp.bfloat16
    tiles = wide // (2 * LANES)
    ahead = max(1, tiles * 3 // 14)
    others = tiles - ahead
    widths = [2 * LANES * n for n in (others // 2, others - others // 2, ahead)]
    lanes = half // LANES
    late = max(1, lanes * 2 // 7)
    cuts = [0, LANES * (lanes * 3 // 7), half - LANES * late]
    splits = len(cuts) - 1
    spans = [b - a for a, b in zip(cuts, cuts[1:])]
    pieces = len(widths)
    vmem = pl.BlockSpec(memory_space=pltpu.VMEM)
    anywhere = pl.BlockSpec(memory_space=pl.ANY)
    sems = pltpu.SemaphoreType.DMA
    spare = [LANES] + [0] * (pieces - 1)
    last = half - cuts[-1]
    return pl.pallas_call(
        functools.partial(fused_kernel, widths, cuts),
        out_shape=jax.ShapeDtypeStruct((tok, wide), bf16),
        in_specs=[anywhere] * 6,
        out_specs=vmem,
        scratch_shapes=[pltpu.VMEM((2, 2, nz, 2, tok, w + s), bf16) for w, s in zip(widths, spare)]
        + [pltpu.VMEM((2, 2, nz, 2, tok, w), bf16) for w in spans + [last]]
        + [pltpu.VMEM((nz, 2, tok, w), bf16) for _ in range(3) for w in spans]
        + [pltpu.VMEM((2, tok, w), bf16) for w in spans]
        + [pltpu.VMEM((2, nz, tok, w), bf16) for w in spans]
        + [
            pltpu.VMEM((units, 2 * wide), bf16),
            pltpu.VMEM((units, 2 * wide), bf16),
            pltpu.VMEM((2, 2 * units, half), bf16),
            pltpu.VMEM((4 * nz * tok, 2 * units), bf16),
            pltpu.VMEM(expert_ids.shape[::-1], expert_ids.dtype),
            pltpu.VMEM(route_weights.shape[::-1], route_weights.dtype),
            pltpu.VMEM((nz, 2, 2, 2, tok, last), bf16),
            pltpu.VMEM((2, 2, 2, tok, last), bf16),
            pltpu.VMEM((2, tok, last), bf16),
            pltpu.VMEM((2, 3, tok, last), bf16),
            sems((pieces + 6,)),
            sems((pieces, nz)),
            sems((pieces, nz)),
            sems((pieces, 2)),
            sems((nz,)),
            sems((pieces, 2)),
            sems((pieces, 3)),
            sems((pieces,)),
            sems((pieces,)),
            sems((pieces, 2)),
            sems((pieces, 4)),
            sems((2,)),
            sems((2,)),
            sems,
            sems,
        ]
        + [sems((splits,)), sems((splits, nz))] * 3
        + [
            sems((splits,)),
            sems((splits,)),
            sems((splits, 3)),
            sems((splits, 2)),
            sems((splits,)),
            sems((3,)),
            sems,
            sems,
            sems,
            sems,
            sems,
            sems,
            sems,
            sems,
            sems((2,)),
        ],
        compiler_params=pltpu.CompilerParams(
            collective_id=0, has_side_effects=True, vmem_limit_bytes=60 * 2**20
        ),
    )(tokens, expert_ids.T, route_weights.T, gate_weight, up_weight, down_weight)


def body(*args):
    every = args[1].shape[1] == lax.axis_size("expert") // 2
    tok, wide = args[0].shape
    even = lax.axis_size("tensor") == 2 and lax.axis_size("expert") == 16
    fits = tok % 16 == 0 and wide % 512 == 0 and 3 * args[1].shape[1] <= LANES
    if every and even and fits:
        return fused_body(*args)
    return sparse_body(*args)


def solution(mesh):
    placed = (
        P("expert", "tensor"),
        P("expert", None),
        P("expert", None),
        P("expert", "tensor", None),
        P("expert", "tensor", None),
        P("expert", "tensor", None),
    )
    return jax.shard_map(
        body, mesh=mesh, in_specs=placed, out_specs=P("expert", "tensor"), check_vma=False
    )
```

```python
import functools

import jax
import jax.numpy as jnp
from jax import lax
from jax.experimental import pallas as pl
from jax.experimental.pallas import tpu as pltpu
from jax.sharding import PartitionSpec as P

LANES = 128


def rows_times(rows, weight):
    return lax.dot_general(
        rows, weight, (((1,), (1,)), ((), ())), preferred_element_type=jnp.float32
    )


def sparse_body(tokens, expert_ids, route_weights, gate_weight, up_weight, down_weight):
    devices_wide = lax.axis_size("expert")
    experts = devices_wide // 2
    tok_count = expert_ids.shape[0]
    per_token = expert_ids.shape[1]
    capacity = min(tok_count, tok_count * per_token // experts)
    slot_count = experts * capacity
    arrived_count = devices_wide * capacity
    expert_range = jnp.arange(experts, dtype=jnp.int32)
    onehot = jnp.sum(
        (expert_ids[:, :, None] == expert_range[None, None, :]).astype(jnp.int32), axis=1
    )
    token_range = jnp.arange(tok_count, dtype=jnp.int32)
    earlier = token_range[None, :, None] < token_range[:, None, None]
    earlier_count = jnp.sum(jnp.where(earlier, onehot[None, :, :], 0), axis=1)
    slot_rank = jnp.take_along_axis(earlier_count, expert_ids, axis=1)
    slot_of = expert_ids * capacity + slot_rank
    slot_range = jnp.arange(slot_count, dtype=jnp.int32)
    select = jnp.any(slot_of[None, :, :] == slot_range[:, None, None], axis=2).astype(jnp.bfloat16)
    weight_gate = gate_weight[0]
    weight_up = up_weight[0]
    weight_out = down_weight[0]
    whole_rows = lax.all_gather(tokens, "tensor", axis=1, tiled=True)
    packed = jnp.dot(select, whole_rows, preferred_element_type=jnp.float32).astype(jnp.bfloat16)
    packed = packed.reshape(experts, capacity, whole_rows.shape[1])
    arrived = lax.all_to_all(
        jnp.repeat(packed, 2, axis=0), "expert", split_axis=0, concat_axis=0, tiled=True
    ).reshape(arrived_count, -1)
    gate_act = rows_times(arrived, weight_gate)
    up_act = rows_times(arrived, weight_up)
    hidden = (jax.nn.silu(gate_act) * up_act).astype(jnp.bfloat16)
    columns = lax.all_to_all(weight_out, "tensor", split_axis=1, concat_axis=0, tiled=True)
    unit_count = hidden.shape[1]
    shard_piece = lax.all_gather(hidden, "tensor", axis=1, tiled=True)
    groups = shard_piece.shape[1] // unit_count
    weight_rows = columns
    weight_rows = weight_rows.reshape(groups, unit_count, columns.shape[1])
    grouped = shard_piece.reshape(shard_piece.shape[0], groups, unit_count)
    group_terms = jnp.einsum(
        "rgf,gfd->grd", grouped, weight_rows, preferred_element_type=jnp.float32
    ).astype(jnp.bfloat16)
    group_terms = lax.optimization_barrier(group_terms)
    half_out = jnp.sum(group_terms.astype(jnp.float32), axis=0).astype(jnp.bfloat16)
    returned = lax.all_to_all(
        half_out.reshape(devices_wide, capacity, -1),
        "expert",
        split_axis=0,
        concat_axis=0,
        tiled=True,
    )
    returned = returned.reshape(experts, 2, capacity, -1).astype(jnp.float32)
    combined = (returned[:, 0] + returned[:, 1]).reshape(slot_count, -1)
    picked = combined[slot_of]
    mixed_out = jnp.sum(route_weights[:, :, None] * picked, axis=1)
    return mixed_out.astype(jnp.bfloat16)


OWN, FIRST, SECOND, DIAGONAL = range(4)
HERE, SIDE, FAR_MID, FAR_END = range(4)
GATHER = (
    ('a', 2), ('zf', 0), ('a', 0), ('zf', 1), ('zn', 1), ('a', 1), ('bd', 2, 0), ('bd', 0, 0), ('zn', 0),
    ('first', 2, 0), ('bd', 1, 0), ('first', 0, 0), ('own', 0, 2), ('bd', 0, 2), ('here',), ('own', 1, 2),
    ('first', 1, 0), ('bd', 1, 2), ('own', 1, 1), ('own', 0, 1), ('bd', 0, 1), ('bd', 1, 1), ('own', 0, 3),
    ('bd', 0, 3), ('own', 1, 3), ('bd', 1, 3), ('plane', 1), ('first', 0, 2), ('plane', 2), ('first', 1, 2),
    ('first', 0, 1), ('co', 1), ('first', 0, 3), ('first', 1, 1), ('co', 0), ('first', 1, 3), ('cs', 0), ('cf', 0),
    ('cf', 1), ('cs', 1), ('plane', 3), ('cd', 0), ('share', 0, 0), ('cd', 1), ('share', 1, 0), ('share', 2, 0),
    ('share', 0, 1), ('share', 2, 1), ('share', 1, 1),
)
SCATTER = (
    ('downL',), ('lz', 3), ('down', 0), ('rd', 3, 0), ('down', 1), ('rb', 3, 1), ('rb', 3, 0), ('rd', 2, 0),
    ('lz', 2), ('lz', 1), ('rb', 1, 1), ('rd', 3, 1), ('rb', 1, 0), ('rd', 1, 0), ('turn', 3, 0), ('rd', 1, 1),
    ('turn', 3, 1), ('rd', 2, 1), ('turn', 2, 0), ('rb', 0, 1), ('rb', 2, 0), ('turn', 1, 0), ('rd', 0, 1),
    ('rd', 0, 0), ('rb', 2, 1), ('lrelay',), ('turn', 1, 1), ('home', 3, 0), ('home', 3, 1), ('turn', 2, 1),
    ('home', 2, 0), ('rb', 0, 0), ('lsum',), ('lc',), ('ld',), ('turn', 0, 0), ('home', 2, 1), ('turn', 0, 1),
    ('home', 1, 0), ('home', 1, 1), ('relay', 0), ('lb',), ('relay', 1), ('lturn',), ('home', 0, 0), ('home', 0, 1),
)


def fused_kernel(
    widths, cuts, tok_hbm, ids_hbm, rw_hbm, gate_hbm, up_hbm, down_hbm, out_ref, *scratch
):
    pieces, splits = len(widths), len(cuts) - 1
    rows, scratch = scratch[:pieces], scratch[pieces:]
    parts, scratch = scratch[: splits + 1], scratch[splits + 1 :]
    diag_bufs, scratch = scratch[:splits], scratch[splits:]
    first_bufs, scratch = scratch[:splits], scratch[splits:]
    second_bufs, scratch = scratch[:splits], scratch[splits:]
    relay_bufs, scratch = scratch[:splits], scratch[splits:]
    owner_bufs, scratch = scratch[:splits], scratch[splits:]
    (
        gate, up, down, hid, ids_buf, rw_buf, late_buf, late_relay, late_diag, late_owner,
        load_sem, own_recv, first_recv, side_recv, plane_recv, core_recv, gz_send, gr_send, ga_send, gb_send, gc_send,
        down_send, down_recv, hid_send, hid_recv,
        rd_send, rd_recv, ra_send, ra_recv, rb_send, rb_recv, rr_send, rr_recv, rz_send, rz_recv, rc_send,
        lz_send, lz_recv, lr_send, lr_recv, ld_send, ld_recv, la_send, lb_send, lc_send, lo_recv,
    ) = scratch
    nz = rows[0].shape[2]
    me, y = lax.axis_index("expert"), lax.axis_index("tensor")
    c = lax.rem(me, 2)
    x = lax.rem(me // 2, 2)
    z = me // 4
    oc, ox, oy = 1 - c, 1 - x, 1 - y
    tok, wide = out_ref.shape
    half = wide // 2
    units = gate.shape[0]
    experts = 2 * nz
    count = 4 * nz * tok
    top = ids_hbm.shape[0]
    last = pieces - 1
    starts = [sum(widths[:p]) for p in range(pieces)]
    wide_f, narrow = jnp.float32, jnp.bfloat16
    middle = (z > 0) & (z < nz - 1)
    side = jnp.where(lax.rem(z, 2) == 0, z + 1, z - 1)
    low = z < nz // 2
    near = [z, side, jnp.where(low, nz // 2, nz // 2 - 1), jnp.where(low, nz - 1, 0)]
    far_end = near[FAR_END]
    columns = [
        (x, y),
        (jnp.where(c == 0, ox, x), jnp.where(c == 0, y, oy)),
        (jnp.where(c == 0, x, ox), jnp.where(c == 0, oy, y)),
        (ox, oy),
    ]

    def dev(zz, xx, cc, yy):
        return ((zz * 2 + xx) * 2 + cc, yy)

    def beside(col, cc):
        xx, yy = columns[col]
        return dev(z, xx, cc, yy)

    dev_a, dev_b, dev_c = beside(FIRST, c), beside(SECOND, c), dev(z, x, oc, y)
    dev_side = dev(side, x, c, y)

    def in_middle(action):
        @pl.when(middle)
        def _():
            action()

    def at_ends(action):
        @pl.when(jnp.logical_not(middle))
        def _():
            action()

    def remote(src, dst, send, recv, to):
        return pltpu.make_async_remote_copy(
            src_ref=src, dst_ref=dst, send_sem=send, recv_sem=recv,
            device_id=to, device_id_type=pl.DeviceIdType.MESH,
        )

    barrier = pltpu.get_barrier_semaphore()

    def greet(to):
        pl.semaphore_signal(barrier, inc=1, device_id=to, device_id_type=pl.DeviceIdType.MESH)

    partners = [dev(near[k], x, cc, y) for k in (FAR_MID, SIDE) for cc in (c, oc)]
    partners += [beside(col, cc) for col in (FIRST, SECOND) for cc in (c, oc)] + [dev_c]

    @pl.when(middle)
    def _():
        for cc in (c, oc):
            greet(dev(far_end, x, cc, y))

    for to in partners:
        greet(to)
    small_loads = [
        pltpu.make_async_copy(ids_hbm, ids_buf, load_sem.at[0]),
        pltpu.make_async_copy(rw_hbm, rw_buf, load_sem.at[1]),
    ]
    tok_loads = [
        pltpu.make_async_copy(
            tok_hbm.at[:, pl.ds(starts[p], widths[p])],
            rows[p].at[y, x, z, c, :, pl.ds(0, widths[p])],
            load_sem.at[2 + p],
        )
        for p in range(pieces)
    ]
    gate_load = pltpu.make_async_copy(gate_hbm.at[0], gate, load_sem.at[pieces + 2])
    up_load = pltpu.make_async_copy(up_hbm.at[0], up, load_sem.at[pieces + 3])

    def down_rows(cc, yy):
        return (
            down_hbm.at[0, :, pl.ds(pl.multiple_of((2 * yy + cc) * half, LANES), half)],
            down.at[yy, pl.ds(pl.multiple_of(c * units, units), units)],
        )

    down_loads = [
        pltpu.make_async_copy(*down_rows(c, yy), load_sem.at[pieces + 4 + yy]) for yy in range(2)
    ]
    for load in small_loads + tok_loads + [gate_load, up_load] + down_loads:
        load.start()
    for load in small_loads:
        load.wait()
    ids = ids_buf[...].astype(wide_f).T
    weights = rw_buf[...].T
    lane = lax.broadcasted_iota(jnp.int32, (tok, LANES), 1)
    which = lax.rem(lane, experts).astype(wide_f)
    spread = jnp.zeros((tok, LANES), wide_f)
    for j in range(top):
        spread = jnp.where(ids[:, j : j + 1] == which, weights[:, j : j + 1], spread)
    first = spread.astype(narrow).astype(wide_f)
    rest = spread - first
    second = rest.astype(narrow).astype(wide_f)
    third = rest - second
    terms = jnp.where(lane < experts, first, jnp.where(lane < 2 * experts, second, third))
    terms = jnp.where(lane < 3 * experts, terms, 0.0)
    rows[0][y, x, z, c, :, widths[0] :] = terms.astype(narrow)
    for load in tok_loads:
        load.wait()
    pl.semaphore_wait(barrier, len(partners) + 2 * middle.astype(jnp.int32))

    def column(p, col, cc=c):
        xx, yy = columns[col]
        return rows[p].at[yy, xx, :, cc]

    def cell(p, col, zz):
        xx, yy = columns[col]
        return rows[p].at[yy, xx, zz, c]

    def layer(zz, cc=c):
        return rows[last].at[:, :, zz, cc]

    def same(ref, send, recv, to):
        return remote(ref, ref, send, recv, to)

    def over_z(k):
        return dev(near[k], x, c, y)

    def z_copy(p, k):
        return same(cell(p, OWN, z), gz_send.at[p, k - 1], own_recv.at[p, z], over_z(k))

    def relay_copy(p):
        return same(cell(p, OWN, far_end), gr_send.at[p], own_recv.at[p, far_end], dev_side)

    def a_copy(p, zz):
        return same(cell(p, OWN, zz), ga_send.at[p], first_recv.at[p, zz], dev_a)

    def b_copy(p, zz):
        return same(cell(p, OWN, zz), gb_send.at[p, 0], side_recv.at[p, 0], dev_b)

    def d_copy(p, zz):
        return same(cell(p, FIRST, zz), gb_send.at[p, 1], side_recv.at[p, 1], dev_b)

    def c_copy(p, col):
        _, yy = columns[col]
        return same(column(p, col), gc_send.at[p, col], core_recv.at[p, yy], dev_c)

    def layer_copy(k):
        return same(layer(z), gz_send.at[last, k - 1], plane_recv.at[z], over_z(k))

    def layer_relay():
        return same(layer(far_end), gr_send.at[last], plane_recv.at[far_end], dev_side)

    def layer_core(zz):
        return same(layer(zz), gc_send.at[last, 0], core_recv.at[last, 0], dev_c)

    def landed(ref, recv):
        same(ref, gr_send.at[last], recv, dev_c).wait_recv()

    def left(ref, send):
        same(ref, send, core_recv.at[last, 0], dev_c).wait_send()

    def to_far(copy):
        copy(FAR_MID).start()

        @pl.when(middle)
        def _():
            copy(FAR_END).start()

    def own(p, k):
        landed(cell(p, OWN, near[k]), own_recv.at[p, near[k]])
        if k == FAR_END:
            in_middle(lambda: relay_copy(p).start())
        a_copy(p, near[k]).start()

    def first_block(p, k):
        landed(cell(p, FIRST, near[k]), first_recv.at[p, near[k]])
        d_copy(p, near[k]).start()

    def sideways(p, j):
        landed(column(p, SECOND + j), side_recv.at[p, j])
        c_copy(p, SECOND + j).start()

    def here():
        for j in range(2):
            landed(cell(last, SECOND + j, z), side_recv.at[last, j])
        to_far(layer_copy)
        layer_copy(SIDE).start()
        layer_core(z).start()

    def layer_in(k):
        landed(layer(near[k]), plane_recv.at[near[k]])
        if k == FAR_END:
            in_middle(lambda: layer_relay().start())
        layer_core(near[k]).start()

    contract = (((1,), (1,)), ((), ()))
    sums, layers_in = [], []

    def share(p, turn_of):
        yy = oy if turn_of else y
        if p < last:
            landed(rows[p].at[yy, :, :, oc], core_recv.at[p, yy])
        elif not layers_in:
            landed(rows[p].at[:, :, :, oc], core_recv.at[p, 0])
            layers_in.append(p)
        if not sums:
            gate_load.wait()
            up_load.wait()
        block = rows[p][yy, :, :, :, :, : widths[p]].reshape(count, widths[p])
        cols = pl.ds(pl.multiple_of(yy * wide + starts[p], LANES), widths[p])
        g = lax.dot_general(block, gate[:, cols], contract, preferred_element_type=wide_f)
        u = lax.dot_general(block, up[:, cols], contract, preferred_element_type=wide_f)
        sums.append((g, u) if not sums else (sums[-1][0] + g, sums[-1][1] + u))

    gather = {
        "zn": lambda p: z_copy(p, SIDE).start(),
        "zf": lambda p: to_far(functools.partial(z_copy, p)),
        "a": lambda p: a_copy(p, z).start(),
        "bd": lambda p, k: b_copy(p, near[k]).start(),
        "own": own,
        "first": first_block,
        "co": lambda p: c_copy(p, OWN).start(),
        "cf": lambda p: c_copy(p, FIRST).start(),
        "cs": lambda p: sideways(p, 0),
        "cd": lambda p: sideways(p, 1),
        "here": here,
        "plane": layer_in,
        "share": share,
    }
    down_copies = []
    for yy in range(2):
        src, dst = down_rows(oc, yy)
        down_copies.append(remote(src, dst, down_send.at[yy], down_recv.at[yy], dev_c))
    started = False
    for name, *where in GATHER:
        if name == "own" and not started:
            for copy in down_copies:
                copy.start()
            started = True
        gather[name](*where)
    gate_act, up_act = sums[-1]
    lanes = lax.broadcasted_iota(jnp.int32, (count, LANES), 1)
    mine = (lax.rem(lanes, experts) == me // 2) & (lanes < 3 * experts)
    kept = rows[0][0, :, :, :, :, widths[0] :].reshape(count, LANES).astype(wide_f)
    scale = jnp.sum(jnp.where(mine, kept, 0.0), axis=1, keepdims=True)
    hid_cols = pl.ds(pl.multiple_of(c * units, units), units)
    hid[:, hid_cols] = (jax.nn.silu(gate_act) * up_act * scale).astype(narrow)
    hid_copy = remote(hid.at[:, hid_cols], hid.at[:, hid_cols], hid_send, hid_recv, dev_c)
    hid_copy.start()
    for load in down_loads:
        load.wait()
    for copy in down_copies:
        copy.wait_recv()
    hid_copy.wait_recv()

    def project(r):
        begin, end = cuts[r], cuts[r + 1] if r < splits else half
        for yy in range(2):
            term = jnp.dot(hid[...], down[yy, :, begin:end], preferred_element_type=wide_f)
            parts[r][yy] = term.astype(narrow).reshape(2, nz, 2, tok, end - begin)

    def block(r, col, zz):
        xx, yy = columns[col]
        return parts[r].at[yy, xx, zz]

    def total(*terms):
        out = terms[0].astype(wide_f)
        for term in terms[1:]:
            out = out + term.astype(wide_f)
        return out

    def rd(k, r):
        zz = near[k]
        return remote(block(r, DIAGONAL, zz), diag_bufs[r].at[zz], rd_send.at[r], rd_recv.at[r, zz], dev_b)

    def rb(k, r):
        zz = near[k]
        return remote(block(r, SECOND, zz), second_bufs[r].at[zz], rb_send.at[r], rb_recv.at[r, zz], dev_b)

    def ra(k, r):
        zz = near[k]
        return remote(block(r, FIRST, zz), first_bufs[r].at[zz], ra_send.at[r], ra_recv.at[r, zz], dev_a)

    def rr(r):
        return remote(block(r, OWN, far_end), relay_bufs[r], rr_send.at[r], rr_recv.at[r], dev_side)

    def rz(k, r, cc):
        zz = near[k]
        return remote(
            block(r, OWN, zz).at[cc], owner_bufs[r].at[c, z], rz_send.at[r, k - 1], rz_recv.at[r, c], dev(zz, x, cc, y)
        )

    def rc(r):
        return remote(block(r, OWN, z).at[oc], owner_bufs[r].at[c, z], rc_send.at[r], rz_recv.at[r, c], dev_c)

    def landed_slots(ref, slots, recv):
        landed(ref.at[pl.ds(0, slots)], recv)

    def plane(zz):
        return parts[splits].at[:, :, zz]

    def lz(k):
        return remote(plane(near[k]), late_buf.at[z], lz_send.at[k - 1], lz_recv, over_z(k))

    def lr():
        return remote(plane(far_end), late_relay, lr_send, lr_recv, dev_side)

    def ld():
        return remote(block(splits, DIAGONAL, z), late_diag, ld_send, ld_recv, dev_b)

    def la(cc):
        return remote(
            block(splits, FIRST, z).at[cc], late_owner.at[c, 0], la_send, lo_recv.at[c], beside(FIRST, cc)
        )

    def lb(cc):
        return remote(
            block(splits, SECOND, z).at[cc], late_owner.at[c, 1], lb_send, lo_recv.at[c], beside(SECOND, cc)
        )

    def lc():
        return remote(block(splits, OWN, z).at[oc], late_owner.at[c, 2], lc_send, lo_recv.at[c], dev_c)

    def send_late(k):
        if k == FAR_END:
            at_ends(lambda: lr().start())
        else:
            lz(k).start()

    def turn(k, r):
        rd(k, r).wait_recv()
        ref = block(r, FIRST, near[k])
        ref[...] = total(ref[...], diag_bufs[r][near[k]]).astype(narrow)
        ra(k, r).start()

    def home(k, r):
        ra(k, r).wait_recv()
        rb(k, r).wait_recv()
        ref = block(r, OWN, near[k])
        ref[...] = total(ref[...], first_bufs[r][near[k]], second_bufs[r][near[k]]).astype(narrow)
        if k == FAR_END:
            at_ends(lambda: rr(r).start())
        elif k == HERE:
            rc(r).start()
        else:
            for cc in range(2):
                rz(k, r, cc).start()

    def relay(r):
        @pl.when(middle)
        def _():
            rr(r).wait_recv()
            ref = block(r, OWN, far_end)
            ref[...] = total(ref[...], relay_bufs[r][...]).astype(narrow)
            for cc in range(2):
                rz(FAR_END, r, cc).start()

    def late_pass():
        @pl.when(middle)
        def _():
            lr().wait_recv()
            ref = plane(far_end)
            ref[...] = total(ref[...], late_relay[...]).astype(narrow)
            lz(FAR_END).start()

    def late_sum():
        ref = plane(z)

        @pl.when(middle)
        def _():
            landed_slots(late_buf, nz - 1, lz_recv)
            ref[...] = total(ref[...], late_buf[side], late_buf[near[FAR_MID]], late_buf[far_end]).astype(narrow)

        @pl.when(jnp.logical_not(middle))
        def _():
            landed_slots(late_buf, nz - 2, lz_recv)
            ref[...] = total(ref[...], late_buf[side], late_buf[near[FAR_MID]]).astype(narrow)

    def late_turn():
        ld().wait_recv()
        ref = block(splits, FIRST, z)
        ref[...] = total(ref[...], late_diag[...]).astype(narrow)
        for cc in range(2):
            la(cc).start()

    def late_out(j):
        core, mine_too = (oc, late_owner.at[oc, 2]) if j else (c, block(splits, OWN, z).at[c])
        landed_slots(late_owner.at[core], 2 + j, lo_recv.at[core])
        at = pl.ds(pl.multiple_of(core * half + cuts[splits], LANES), half - cuts[splits])
        out_ref[:, at] = total(mine_too[...], late_owner[core, 0], late_owner[core, 1]).astype(narrow)

    def out(r, j):
        bufs = owner_bufs[r]
        core, mine_too = (oc, bufs.at[oc, z]) if j else (c, block(r, OWN, z).at[c])
        at = pl.ds(pl.multiple_of(core * half + cuts[r], LANES), cuts[r + 1] - cuts[r])

        @pl.when(middle)
        def _():
            landed_slots(bufs.at[core], nz - 1 + j, rz_recv.at[r, core])
            sums = [bufs[core, near[k]] for k in (SIDE, FAR_MID, FAR_END)]
            out_ref[:, at] = total(mine_too[...], *sums).astype(narrow)

        @pl.when(jnp.logical_not(middle))
        def _():
            landed_slots(bufs.at[core], nz - 2 + j, rz_recv.at[r, core])
            sums = [bufs[core, near[k]] for k in (SIDE, FAR_MID)]
            out_ref[:, at] = total(mine_too[...], *sums).astype(narrow)

    scatter = {
        "downL": lambda: project(splits),
        "down": project,
        "lz": send_late,
        "rd": lambda k, r: rd(k, r).start(),
        "rb": lambda k, r: rb(k, r).start(),
        "turn": turn,
        "home": home,
        "relay": relay,
        "lrelay": late_pass,
        "lsum": late_sum,
        "ld": lambda: ld().start(),
        "lb": lambda: [lb(cc).start() for cc in range(2)],
        "lc": lambda: lc().start(),
        "lturn": late_turn,
    }
    for name, *where in SCATTER:
        scatter[name](*where)
    for r in range(splits):
        for j in range(2):
            out(r, j)
    for j in range(2):
        late_out(j)

    for p in range(last):
        z_copy(p, SIDE).wait_send()
        z_copy(p, FAR_MID).wait_send()
        left(column(p, OWN), ga_send.at[p])
        left(column(p, OWN), gb_send.at[p, 0])
        left(column(p, FIRST), gb_send.at[p, 1])
        for col in range(4):
            c_copy(p, col).wait_send()
    a_copy(last, z).wait_send()
    b_copy(last, z).wait_send()
    d_copy(last, z).wait_send()
    layer_copy(SIDE).wait_send()
    layer_copy(FAR_MID).wait_send()
    left(rows[last].at[:, :, :, c], gc_send.at[last, 0])
    for r in range(splits):
        left(first_bufs[r], ra_send.at[r])
        left(diag_bufs[r], rd_send.at[r])
        left(second_bufs[r], rb_send.at[r])
        left(relay_bufs[r], rz_send.at[r, SIDE - 1])
        left(relay_bufs[r], rz_send.at[r, FAR_MID - 1])
        rc(r).wait_send()
    left(late_diag, la_send)
    left(late_diag, lb_send)
    for copy in [lz(SIDE), lz(FAR_MID), ld(), lc(), hid_copy] + down_copies:
        copy.wait_send()

    @pl.when(middle)
    def _():
        for p in range(last):
            z_copy(p, FAR_END).wait_send()
            relay_copy(p).wait_send()
        layer_copy(FAR_END).wait_send()
        layer_relay().wait_send()
        lz(FAR_END).wait_send()
        for r in range(splits):
            left(relay_bufs[r], rz_send.at[r, FAR_END - 1])

    @pl.when(jnp.logical_not(middle))
    def _():
        lr().wait_send()
        for r in range(splits):
            rr(r).wait_send()


def fused_body(tokens, expert_ids, route_weights, gate_weight, up_weight, down_weight):
    nz = lax.axis_size("expert") // 4
    tok, wide = tokens.shape
    half = wide // 2
    units = gate_weight.shape[1]
    bf16 = jnp.bfloat16
    tiles = wide // (2 * LANES)
    ahead = max(1, tiles * 3 // 14)
    others = tiles - ahead
    widths = [2 * LANES * n for n in (others // 2, others - others // 2, ahead)]
    lanes = half // LANES
    late = max(1, lanes * 2 // 7)
    cuts = [0, LANES * (lanes * 3 // 7), half - LANES * late]
    splits = len(cuts) - 1
    spans = [b - a for a, b in zip(cuts, cuts[1:])]
    pieces = len(widths)
    vmem = pl.BlockSpec(memory_space=pltpu.VMEM)
    anywhere = pl.BlockSpec(memory_space=pl.ANY)
    sems = pltpu.SemaphoreType.DMA
    spare = [LANES] + [0] * (pieces - 1)
    last = half - cuts[-1]
    return pl.pallas_call(
        functools.partial(fused_kernel, widths, cuts),
        out_shape=pltpu.VMEM((tok, wide), bf16),
        in_specs=[anywhere] * 6,
        out_specs=vmem,
        scratch_shapes=[pltpu.VMEM((2, 2, nz, 2, tok, w + s), bf16) for w, s in zip(widths, spare)]
        + [pltpu.VMEM((2, 2, nz, 2, tok, w), bf16) for w in spans + [last]]
        + [pltpu.VMEM((nz, 2, tok, w), bf16) for _ in range(3) for w in spans]
        + [pltpu.VMEM((2, tok, w), bf16) for w in spans]
        + [pltpu.VMEM((2, nz, tok, w), bf16) for w in spans]
        + [
            pltpu.VMEM((units, 2 * wide), bf16),
            pltpu.VMEM((units, 2 * wide), bf16),
            pltpu.VMEM((2, 2 * units, half), bf16),
            pltpu.VMEM((4 * nz * tok, 2 * units), bf16),
            pltpu.VMEM(expert_ids.shape[::-1], expert_ids.dtype),
            pltpu.VMEM(route_weights.shape[::-1], route_weights.dtype),
            pltpu.VMEM((nz, 2, 2, 2, tok, last), bf16),
            pltpu.VMEM((2, 2, 2, tok, last), bf16),
            pltpu.VMEM((2, tok, last), bf16),
            pltpu.VMEM((2, 3, tok, last), bf16),
            sems((pieces + 6,)),
            sems((pieces, nz)),
            sems((pieces, nz)),
            sems((pieces, 2)),
            sems((nz,)),
            sems((pieces, 2)),
            sems((pieces, 3)),
            sems((pieces,)),
            sems((pieces,)),
            sems((pieces, 2)),
            sems((pieces, 4)),
            sems((2,)),
            sems((2,)),
            sems,
            sems,
        ]
        + [sems((splits,)), sems((splits, nz))] * 3
        + [
            sems((splits,)),
            sems((splits,)),
            sems((splits, 3)),
            sems((splits, 2)),
            sems((splits,)),
            sems((3,)),
            sems,
            sems,
            sems,
            sems,
            sems,
            sems,
            sems,
            sems,
            sems((2,)),
        ],
        compiler_params=pltpu.CompilerParams(
            collective_id=0, has_side_effects=True, vmem_limit_bytes=60 * 2**20
        ),
    )(tokens, expert_ids.T, route_weights.T, gate_weight, up_weight, down_weight)


def body(*args):
    every = args[1].shape[1] == lax.axis_size("expert") // 2
    tok, wide = args[0].shape
    even = lax.axis_size("tensor") == 2 and lax.axis_size("expert") == 16
    fits = tok % 16 == 0 and wide % 512 == 0 and 3 * args[1].shape[1] <= LANES
    if every and even and fits:
        return fused_body(*args)
    return sparse_body(*args)


def solution(mesh):
    placed = (
        P("expert", "tensor"),
        P("expert", None),
        P("expert", None),
        P("expert", "tensor", None),
        P("expert", "tensor", None),
        P("expert", "tensor", None),
    )
    return jax.shard_map(
        body, mesh=mesh, in_specs=placed, out_specs=P("expert", "tensor"), check_vma=False
    )
```

```python
import functools

import jax
import jax.numpy as jnp
from jax import lax
from jax.experimental import pallas as pl
from jax.experimental.pallas import tpu as pltpu
from jax.sharding import PartitionSpec as P

LANES = 128


def rows_times(rows, weight):
    return lax.dot_general(
        rows, weight, (((1,), (1,)), ((), ())), preferred_element_type=jnp.float32
    )


def sparse_body(tokens, expert_ids, route_weights, gate_weight, up_weight, down_weight):
    devices_wide = lax.axis_size("expert")
    experts = devices_wide // 2
    tok_count = expert_ids.shape[0]
    per_token = expert_ids.shape[1]
    capacity = min(tok_count, tok_count * per_token // experts)
    slot_count = experts * capacity
    arrived_count = devices_wide * capacity
    expert_range = jnp.arange(experts, dtype=jnp.int32)
    onehot = jnp.sum(
        (expert_ids[:, :, None] == expert_range[None, None, :]).astype(jnp.int32), axis=1
    )
    token_range = jnp.arange(tok_count, dtype=jnp.int32)
    earlier = token_range[None, :, None] < token_range[:, None, None]
    earlier_count = jnp.sum(jnp.where(earlier, onehot[None, :, :], 0), axis=1)
    slot_rank = jnp.take_along_axis(earlier_count, expert_ids, axis=1)
    slot_of = expert_ids * capacity + slot_rank
    slot_range = jnp.arange(slot_count, dtype=jnp.int32)
    select = jnp.any(slot_of[None, :, :] == slot_range[:, None, None], axis=2).astype(jnp.bfloat16)
    weight_gate = gate_weight[0]
    weight_up = up_weight[0]
    weight_out = down_weight[0]
    whole_rows = lax.all_gather(tokens, "tensor", axis=1, tiled=True)
    packed = jnp.dot(select, whole_rows, preferred_element_type=jnp.float32).astype(jnp.bfloat16)
    packed = packed.reshape(experts, capacity, whole_rows.shape[1])
    arrived = lax.all_to_all(
        jnp.repeat(packed, 2, axis=0), "expert", split_axis=0, concat_axis=0, tiled=True
    ).reshape(arrived_count, -1)
    gate_act = rows_times(arrived, weight_gate)
    up_act = rows_times(arrived, weight_up)
    hidden = (jax.nn.silu(gate_act) * up_act).astype(jnp.bfloat16)
    columns = lax.all_to_all(weight_out, "tensor", split_axis=1, concat_axis=0, tiled=True)
    unit_count = hidden.shape[1]
    shard_piece = lax.all_gather(hidden, "tensor", axis=1, tiled=True)
    groups = shard_piece.shape[1] // unit_count
    weight_rows = columns
    weight_rows = weight_rows.reshape(groups, unit_count, columns.shape[1])
    grouped = shard_piece.reshape(shard_piece.shape[0], groups, unit_count)
    group_terms = jnp.einsum(
        "rgf,gfd->grd", grouped, weight_rows, preferred_element_type=jnp.float32
    ).astype(jnp.bfloat16)
    group_terms = lax.optimization_barrier(group_terms)
    half_out = jnp.sum(group_terms.astype(jnp.float32), axis=0).astype(jnp.bfloat16)
    returned = lax.all_to_all(
        half_out.reshape(devices_wide, capacity, -1),
        "expert",
        split_axis=0,
        concat_axis=0,
        tiled=True,
    )
    returned = returned.reshape(experts, 2, capacity, -1).astype(jnp.float32)
    combined = (returned[:, 0] + returned[:, 1]).reshape(slot_count, -1)
    picked = combined[slot_of]
    mixed_out = jnp.sum(route_weights[:, :, None] * picked, axis=1)
    return mixed_out.astype(jnp.bfloat16)


OWN, FIRST, SECOND, DIAGONAL = range(4)
HERE, SIDE, FAR_MID, FAR_END = range(4)
GATHER = (
    ('zn', 1), ('bd', 0, 0), ('zf', 0), ('zn', 0), ('bd', 1, 0), ('a', 3), ('a', 2), ('a', 0), ('bd', 3, 0), ('a', 1),
    ('own', 1, 1), ('zf', 1), ('zn', 2), ('bd', 1, 1), ('own', 0, 2), ('first', 3, 0), ('bd', 2, 0), ('zf', 2),
    ('own', 0, 3), ('bd', 0, 2), ('first', 0, 0), ('bd', 0, 3), ('own', 0, 1), ('bd', 0, 1), ('own', 2, 1),
    ('bd', 2, 1), ('here',), ('own', 1, 2), ('bd', 1, 2), ('own', 2, 2), ('first', 1, 1), ('co', 0), ('own', 1, 3),
    ('bd', 1, 3), ('cs', 0), ('first', 0, 1), ('co', 1), ('bd', 2, 2), ('own', 2, 3), ('bd', 2, 3), ('first', 0, 3),
    ('first', 0, 2), ('cf', 0), ('first', 1, 2), ('first', 2, 1), ('first', 2, 0), ('cs', 1), ('plane', 1), ('co', 2),
    ('first', 1, 3), ('first', 1, 0), ('cf', 1), ('cs', 2), ('first', 2, 2), ('first', 2, 3), ('cf', 2), ('plane', 2),
    ('cd', 0), ('share', 0, 0), ('plane', 3), ('cd', 1), ('share', 1, 0), ('share', 0, 1), ('cd', 2), ('share', 2, 0),
    ('share', 3, 1), ('share', 1, 1), ('share', 3, 0), ('share', 2, 1),
)
SCATTER = (
    ('down', 0), ('rd', 2, 0), ('rd', 3, 0), ('downL',), ('lz', 3), ('lz', 2), ('down', 1), ('rb', 1, 0),
    ('rd', 2, 1), ('rd', 3, 1), ('rd', 1, 1), ('rb', 3, 0), ('turn', 3, 0), ('lz', 1), ('turn', 2, 0), ('rb', 2, 0),
    ('turn', 3, 1), ('rd', 1, 0), ('rb', 3, 1), ('lrelay',), ('turn', 1, 1), ('rd', 0, 0), ('rb', 2, 1), ('rb', 1, 1),
    ('home', 3, 0), ('home', 2, 0), ('rd', 0, 1), ('turn', 2, 1), ('turn', 1, 0), ('home', 3, 1), ('lsum',), ('ld',),
    ('rb', 0, 1), ('rb', 0, 0), ('turn', 0, 0), ('home', 1, 1), ('home', 2, 1), ('relay', 0), ('turn', 0, 1),
    ('home', 1, 0), ('lb',), ('relay', 1), ('lturn',), ('home', 0, 0), ('lc',), ('home', 0, 1),
)


def fused_kernel(
    widths, cuts, tok_hbm, ids_hbm, rw_hbm, gate_hbm, up_hbm, down_hbm, out_ref, *scratch
):
    pieces, splits = len(widths), len(cuts) - 1
    rows, scratch = scratch[:pieces], scratch[pieces:]
    parts, scratch = scratch[: splits + 1], scratch[splits + 1 :]
    diag_bufs, scratch = scratch[:splits], scratch[splits:]
    first_bufs, scratch = scratch[:splits], scratch[splits:]
    second_bufs, scratch = scratch[:splits], scratch[splits:]
    relay_bufs, scratch = scratch[:splits], scratch[splits:]
    owner_bufs, scratch = scratch[:splits], scratch[splits:]
    (
        gate, up, down, hid, ids_buf, rw_buf, late_buf, late_relay, late_diag, late_owner,
        load_sem, own_recv, first_recv, side_recv, plane_recv, core_recv, gz_send, gr_send, ga_send, gb_send, gc_send,
        down_send, down_recv, hid_send, hid_recv,
        rd_send, rd_recv, ra_send, ra_recv, rb_send, rb_recv, rr_send, rr_recv, rz_send, rz_recv, rc_send,
        lz_send, lz_recv, lr_send, lr_recv, ld_send, ld_recv, la_send, lb_send, lc_send, lo_recv,
    ) = scratch
    nz = rows[0].shape[2]
    me, y = lax.axis_index("expert"), lax.axis_index("tensor")
    c = lax.rem(me, 2)
    x = lax.rem(me // 2, 2)
    z = me // 4
    oc, ox, oy = 1 - c, 1 - x, 1 - y
    tok, wide = out_ref.shape
    half = wide // 2
    units = gate.shape[0]
    experts = 2 * nz
    count = 4 * nz * tok
    top = ids_hbm.shape[0]
    last = pieces - 1
    starts = [sum(widths[:p]) for p in range(pieces)]
    wide_f, narrow = jnp.float32, jnp.bfloat16
    middle = (z > 0) & (z < nz - 1)
    side = jnp.where(lax.rem(z, 2) == 0, z + 1, z - 1)
    low = z < nz // 2
    near = [z, side, jnp.where(low, nz // 2, nz // 2 - 1), jnp.where(low, nz - 1, 0)]
    far_end = near[FAR_END]
    columns = [
        (x, y),
        (jnp.where(c == 0, ox, x), jnp.where(c == 0, y, oy)),
        (jnp.where(c == 0, x, ox), jnp.where(c == 0, oy, y)),
        (ox, oy),
    ]

    def dev(zz, xx, cc, yy):
        return ((zz * 2 + xx) * 2 + cc, yy)

    def beside(col, cc):
        xx, yy = columns[col]
        return dev(z, xx, cc, yy)

    dev_a, dev_b, dev_c = beside(FIRST, c), beside(SECOND, c), dev(z, x, oc, y)
    dev_side = dev(side, x, c, y)

    def in_middle(action):
        @pl.when(middle)
        def _():
            action()

    def at_ends(action):
        @pl.when(jnp.logical_not(middle))
        def _():
            action()

    def remote(src, dst, send, recv, to):
        return pltpu.make_async_remote_copy(
            src_ref=src, dst_ref=dst, send_sem=send, recv_sem=recv,
            device_id=to, device_id_type=pl.DeviceIdType.MESH,
        )

    barrier = pltpu.get_barrier_semaphore()

    def greet(to):
        pl.semaphore_signal(barrier, inc=1, device_id=to, device_id_type=pl.DeviceIdType.MESH)

    partners = [dev(near[k], x, cc, y) for k in (FAR_MID, SIDE) for cc in (c, oc)]
    partners += [beside(col, cc) for col in (FIRST, SECOND) for cc in (c, oc)] + [dev_c]

    @pl.when(middle)
    def _():
        for cc in (c, oc):
            greet(dev(far_end, x, cc, y))

    for to in partners:
        greet(to)
    small_loads = [
        pltpu.make_async_copy(ids_hbm, ids_buf, load_sem.at[0]),
        pltpu.make_async_copy(rw_hbm, rw_buf, load_sem.at[1]),
    ]
    tok_loads = [
        pltpu.make_async_copy(
            tok_hbm.at[:, pl.ds(starts[p], widths[p])],
            rows[p].at[y, x, z, c, :, pl.ds(0, widths[p])],
            load_sem.at[2 + p],
        )
        for p in range(pieces)
    ]
    gate_load = pltpu.make_async_copy(gate_hbm.at[0], gate, load_sem.at[pieces + 2])
    up_load = pltpu.make_async_copy(up_hbm.at[0], up, load_sem.at[pieces + 3])

    def down_rows(cc, yy):
        return (
            down_hbm.at[0, :, pl.ds(pl.multiple_of((2 * yy + cc) * half, LANES), half)],
            down.at[yy, pl.ds(pl.multiple_of(c * units, units), units)],
        )

    down_loads = [
        pltpu.make_async_copy(*down_rows(c, yy), load_sem.at[pieces + 4 + yy]) for yy in range(2)
    ]
    for load in small_loads + tok_loads + [gate_load, up_load] + down_loads:
        load.start()
    for load in small_loads:
        load.wait()
    ids = ids_buf[...].astype(wide_f).T
    weights = rw_buf[...].T
    lane = lax.broadcasted_iota(jnp.int32, (tok, LANES), 1)
    which = lax.rem(lane, experts).astype(wide_f)
    spread = jnp.zeros((tok, LANES), wide_f)
    for j in range(top):
        spread = jnp.where(ids[:, j : j + 1] == which, weights[:, j : j + 1], spread)
    first = spread.astype(narrow).astype(wide_f)
    rest = spread - first
    second = rest.astype(narrow).astype(wide_f)
    third = rest - second
    terms = jnp.where(lane < experts, first, jnp.where(lane < 2 * experts, second, third))
    terms = jnp.where(lane < 3 * experts, terms, 0.0)
    rows[0][y, x, z, c, :, widths[0] :] = terms.astype(narrow)
    for load in tok_loads:
        load.wait()
    pl.semaphore_wait(barrier, len(partners) + 2 * middle.astype(jnp.int32))

    def column(p, col, cc=c):
        xx, yy = columns[col]
        return rows[p].at[yy, xx, :, cc]

    def cell(p, col, zz):
        xx, yy = columns[col]
        return rows[p].at[yy, xx, zz, c]

    def layer(zz, cc=c):
        return rows[last].at[:, :, zz, cc]

    def same(ref, send, recv, to):
        return remote(ref, ref, send, recv, to)

    def over_z(k):
        return dev(near[k], x, c, y)

    def z_copy(p, k):
        return same(cell(p, OWN, z), gz_send.at[p, k - 1], own_recv.at[p, z], over_z(k))

    def relay_copy(p):
        return same(cell(p, OWN, far_end), gr_send.at[p], own_recv.at[p, far_end], dev_side)

    def a_copy(p, zz):
        return same(cell(p, OWN, zz), ga_send.at[p], first_recv.at[p, zz], dev_a)

    def b_copy(p, zz):
        return same(cell(p, OWN, zz), gb_send.at[p, 0], side_recv.at[p, 0], dev_b)

    def d_copy(p, zz):
        return same(cell(p, FIRST, zz), gb_send.at[p, 1], side_recv.at[p, 1], dev_b)

    def c_copy(p, col):
        _, yy = columns[col]
        return same(column(p, col), gc_send.at[p], core_recv.at[p, yy], dev_c)

    def layer_copy(k):
        return same(layer(z), gz_send.at[last, k - 1], plane_recv.at[z], over_z(k))

    def layer_relay():
        return same(layer(far_end), gr_send.at[last], plane_recv.at[far_end], dev_side)

    def layer_core(zz):
        return same(layer(zz), gc_send.at[last], core_recv.at[last, 0], dev_c)

    def landed(ref, recv):
        same(ref, gr_send.at[last], recv, dev_c).wait_recv()

    def left(ref, send):
        same(ref, send, core_recv.at[last, 0], dev_c).wait_send()

    def to_far(copy):
        copy(FAR_MID).start()

        @pl.when(middle)
        def _():
            copy(FAR_END).start()

    def own(p, k):
        landed(cell(p, OWN, near[k]), own_recv.at[p, near[k]])
        if k == FAR_END:
            in_middle(lambda: relay_copy(p).start())
        a_copy(p, near[k]).start()

    def first_block(p, k):
        landed(cell(p, FIRST, near[k]), first_recv.at[p, near[k]])
        d_copy(p, near[k]).start()

    def sideways(p, j):
        landed(column(p, SECOND + j), side_recv.at[p, j])
        c_copy(p, SECOND + j).start()

    def here():
        for j in range(2):
            landed(cell(last, SECOND + j, z), side_recv.at[last, j])
        to_far(layer_copy)
        layer_copy(SIDE).start()
        layer_core(z).start()

    def layer_in(k):
        landed(layer(near[k]), plane_recv.at[near[k]])
        if k == FAR_END:
            in_middle(lambda: layer_relay().start())
        layer_core(near[k]).start()

    contract = (((1,), (1,)), ((), ()))
    sums, layers_in = [], []

    def share(p, turn_of):
        yy = oy if turn_of else y
        if p < last:
            landed(rows[p].at[yy, :, :, oc], core_recv.at[p, yy])
        elif not layers_in:
            landed(rows[p].at[:, :, :, oc], core_recv.at[p, 0])
            layers_in.append(p)
        if not sums:
            gate_load.wait()
            up_load.wait()
        block = rows[p][yy, :, :, :, :, : widths[p]].reshape(count, widths[p])
        cols = pl.ds(pl.multiple_of(yy * wide + starts[p], LANES), widths[p])
        g = lax.dot_general(block, gate[:, cols], contract, preferred_element_type=wide_f)
        u = lax.dot_general(block, up[:, cols], contract, preferred_element_type=wide_f)
        sums.append((g, u) if not sums else (sums[-1][0] + g, sums[-1][1] + u))

    gather = {
        "zn": lambda p: z_copy(p, SIDE).start(),
        "zf": lambda p: to_far(functools.partial(z_copy, p)),
        "a": lambda p: a_copy(p, z).start(),
        "bd": lambda p, k: b_copy(p, near[k]).start(),
        "own": own,
        "first": first_block,
        "co": lambda p: c_copy(p, OWN).start(),
        "cf": lambda p: c_copy(p, FIRST).start(),
        "cs": lambda p: sideways(p, 0),
        "cd": lambda p: sideways(p, 1),
        "here": here,
        "plane": layer_in,
        "share": share,
    }
    down_copies = []
    for yy in range(2):
        src, dst = down_rows(oc, yy)
        down_copies.append(remote(src, dst, down_send.at[yy], down_recv.at[yy], dev_c))

    def route_scale():
        lanes = lax.broadcasted_iota(jnp.int32, (count, LANES), 1)
        mine = (lax.rem(lanes, experts) == me // 2) & (lanes < 3 * experts)
        kept = rows[0][0, :, :, :, :, widths[0] :].reshape(count, LANES).astype(wide_f)
        return jnp.sum(jnp.where(mine, kept, 0.0), axis=1, keepdims=True)

    shared = []
    started = False
    for name, *where in GATHER:
        if name == "own" and not started:
            for copy in down_copies:
                copy.start()
            started = True
        gather[name](*where)
        if name == "share" and where[0] == 0:
            shared.append(where)
            if len(shared) == 2:
                scale = route_scale()
    gate_act, up_act = sums[-1]
    hid_cols = pl.ds(pl.multiple_of(c * units, units), units)
    hid_copies = []
    for i in range(2):
        part = slice(i * count // 2, (i + 1) * count // 2)
        act = jax.nn.silu(gate_act[part]) * up_act[part] * scale[part]
        hid[part, hid_cols] = act.astype(narrow)
        ref = hid.at[pl.ds(i * count // 2, count // 2), hid_cols]
        hid_copies.append(remote(ref, ref, hid_send.at[i], hid_recv.at[i], dev_c))
        hid_copies[i].start()
    for load in down_loads:
        load.wait()
    for copy in down_copies:
        copy.wait_recv()
    for copy in hid_copies:
        copy.wait_recv()

    def project(r):
        begin, end = cuts[r], cuts[r + 1] if r < splits else half
        for yy in range(2):
            term = jnp.dot(hid[...], down[yy, :, begin:end], preferred_element_type=wide_f)
            parts[r][yy] = term.astype(narrow).reshape(2, nz, 2, tok, end - begin)

    def block(r, col, zz):
        xx, yy = columns[col]
        return parts[r].at[yy, xx, zz]

    def total(*terms):
        out = terms[0].astype(wide_f)
        for term in terms[1:]:
            out = out + term.astype(wide_f)
        return out

    def rd(k, r):
        zz = near[k]
        return remote(block(r, DIAGONAL, zz), diag_bufs[r].at[zz], rd_send.at[r], rd_recv.at[r, zz], dev_b)

    def rb(k, r):
        zz = near[k]
        return remote(block(r, SECOND, zz), second_bufs[r].at[zz], rb_send.at[r], rb_recv.at[r, zz], dev_b)

    def ra(k, r):
        zz = near[k]
        return remote(block(r, FIRST, zz), first_bufs[r].at[zz], ra_send.at[r], ra_recv.at[r, zz], dev_a)

    def rr(r):
        return remote(block(r, OWN, far_end), relay_bufs[r], rr_send.at[r], rr_recv.at[r], dev_side)

    def rz(k, r, cc):
        zz = near[k]
        return remote(
            block(r, OWN, zz).at[cc], owner_bufs[r].at[c, z], rz_send.at[r, k - 1], rz_recv.at[r, c], dev(zz, x, cc, y)
        )

    def rc(r):
        return remote(block(r, OWN, z).at[oc], owner_bufs[r].at[c, z], rc_send.at[r], rz_recv.at[r, c], dev_c)

    def landed_slots(ref, slots, recv):
        landed(ref.at[pl.ds(0, slots)], recv)

    def plane(zz):
        return parts[splits].at[:, :, zz]

    def lz(k):
        return remote(plane(near[k]), late_buf.at[z], lz_send.at[k - 1], lz_recv, over_z(k))

    def lr():
        return remote(plane(far_end), late_relay, lr_send, lr_recv, dev_side)

    def ld():
        return remote(block(splits, DIAGONAL, z), late_diag, ld_send, ld_recv, dev_b)

    def la(cc):
        return remote(
            block(splits, FIRST, z).at[cc], late_owner.at[c, 0], la_send, lo_recv.at[c], beside(FIRST, cc)
        )

    def lb(cc):
        return remote(
            block(splits, SECOND, z).at[cc], late_owner.at[c, 1], lb_send, lo_recv.at[c], beside(SECOND, cc)
        )

    def lc():
        return remote(block(splits, OWN, z).at[oc], late_owner.at[c, 2], lc_send, lo_recv.at[c], dev_c)

    def send_late(k):
        if k == FAR_END:
            at_ends(lambda: lr().start())
        else:
            lz(k).start()

    def turn(k, r):
        rd(k, r).wait_recv()
        ref = block(r, FIRST, near[k])
        ref[...] = total(ref[...], diag_bufs[r][near[k]]).astype(narrow)
        ra(k, r).start()

    def home(k, r):
        ra(k, r).wait_recv()
        rb(k, r).wait_recv()
        ref = block(r, OWN, near[k])
        ref[...] = total(ref[...], first_bufs[r][near[k]], second_bufs[r][near[k]]).astype(narrow)
        if k == FAR_END:
            at_ends(lambda: rr(r).start())
        elif k == HERE:
            rc(r).start()
        else:
            for cc in range(2):
                rz(k, r, cc).start()

    def relay(r):
        @pl.when(middle)
        def _():
            rr(r).wait_recv()
            ref = block(r, OWN, far_end)
            ref[...] = total(ref[...], relay_bufs[r][...]).astype(narrow)
            for cc in range(2):
                rz(FAR_END, r, cc).start()

    def late_pass():
        @pl.when(middle)
        def _():
            lr().wait_recv()
            ref = plane(far_end)
            ref[...] = total(ref[...], late_relay[...]).astype(narrow)
            lz(FAR_END).start()

    def late_sum():
        ref = plane(z)

        @pl.when(middle)
        def _():
            landed_slots(late_buf, nz - 1, lz_recv)
            ref[...] = total(ref[...], late_buf[side], late_buf[near[FAR_MID]], late_buf[far_end]).astype(narrow)

        @pl.when(jnp.logical_not(middle))
        def _():
            landed_slots(late_buf, nz - 2, lz_recv)
            ref[...] = total(ref[...], late_buf[side], late_buf[near[FAR_MID]]).astype(narrow)

    def late_turn():
        ld().wait_recv()
        ref = block(splits, FIRST, z)
        ref[...] = total(ref[...], late_diag[...]).astype(narrow)
        for cc in range(2):
            la(cc).start()

    def late_out(j):
        core, mine_too = (oc, late_owner.at[oc, 2]) if j else (c, block(splits, OWN, z).at[c])
        landed_slots(late_owner.at[core], 2 + j, lo_recv.at[core])
        at = pl.ds(pl.multiple_of(core * half + cuts[splits], LANES), half - cuts[splits])
        out_ref[:, at] = total(mine_too[...], late_owner[core, 0], late_owner[core, 1]).astype(narrow)

    def out(r, j):
        bufs = owner_bufs[r]
        core, mine_too = (oc, bufs.at[oc, z]) if j else (c, block(r, OWN, z).at[c])
        at = pl.ds(pl.multiple_of(core * half + cuts[r], LANES), cuts[r + 1] - cuts[r])

        @pl.when(middle)
        def _():
            landed_slots(bufs.at[core], nz - 1 + j, rz_recv.at[r, core])
            sums = [bufs[core, near[k]] for k in (SIDE, FAR_MID, FAR_END)]
            out_ref[:, at] = total(mine_too[...], *sums).astype(narrow)

        @pl.when(jnp.logical_not(middle))
        def _():
            landed_slots(bufs.at[core], nz - 2 + j, rz_recv.at[r, core])
            sums = [bufs[core, near[k]] for k in (SIDE, FAR_MID)]
            out_ref[:, at] = total(mine_too[...], *sums).astype(narrow)

    scatter = {
        "downL": lambda: project(splits),
        "down": project,
        "lz": send_late,
        "rd": lambda k, r: rd(k, r).start(),
        "rb": lambda k, r: rb(k, r).start(),
        "turn": turn,
        "home": home,
        "relay": relay,
        "lrelay": late_pass,
        "lsum": late_sum,
        "ld": lambda: ld().start(),
        "lb": lambda: [lb(cc).start() for cc in range(2)],
        "lc": lambda: lc().start(),
        "lturn": late_turn,
    }
    for name, *where in SCATTER:
        scatter[name](*where)
    for r in range(splits):
        for j in range(2):
            out(r, j)
    for j in range(2):
        late_out(j)

    for p in range(last):
        z_copy(p, SIDE).wait_send()
        z_copy(p, FAR_MID).wait_send()
        left(column(p, OWN), ga_send.at[p])
        left(column(p, OWN), gb_send.at[p, 0])
        left(column(p, FIRST), gb_send.at[p, 1])
        left(rows[p].at[:, :, :, c], gc_send.at[p])
    a_copy(last, z).wait_send()
    b_copy(last, z).wait_send()
    d_copy(last, z).wait_send()
    layer_copy(SIDE).wait_send()
    layer_copy(FAR_MID).wait_send()
    left(rows[last].at[:, :, :, c], gc_send.at[last])
    for r in range(splits):
        left(first_bufs[r], ra_send.at[r])
        left(diag_bufs[r], rd_send.at[r])
        left(second_bufs[r], rb_send.at[r])
        left(relay_bufs[r], rz_send.at[r, SIDE - 1])
        left(relay_bufs[r], rz_send.at[r, FAR_MID - 1])
        rc(r).wait_send()
    left(late_diag, la_send)
    left(late_diag, lb_send)
    for copy in [lz(SIDE), lz(FAR_MID), ld(), lc()] + hid_copies + down_copies:
        copy.wait_send()

    @pl.when(middle)
    def _():
        for p in range(last):
            z_copy(p, FAR_END).wait_send()
            relay_copy(p).wait_send()
        layer_copy(FAR_END).wait_send()
        layer_relay().wait_send()
        lz(FAR_END).wait_send()
        for r in range(splits):
            left(relay_bufs[r], rz_send.at[r, FAR_END - 1])

    @pl.when(jnp.logical_not(middle))
    def _():
        lr().wait_send()
        for r in range(splits):
            rr(r).wait_send()


def fused_body(tokens, expert_ids, route_weights, gate_weight, up_weight, down_weight):
    nz = lax.axis_size("expert") // 4
    tok, wide = tokens.shape
    half = wide // 2
    units = gate_weight.shape[1]
    bf16 = jnp.bfloat16
    tiles = wide // (2 * LANES)
    ahead = max(1, tiles * 3 // 14)
    others = tiles - ahead
    widths = [2 * LANES * n for n in ((others + 2) // 3, (others + 1) // 3, others // 3, ahead)]
    lanes = half // LANES
    late = max(1, lanes * 3 // 14)
    cuts = [0, LANES * (lanes * 3 // 7), half - LANES * late]
    splits = len(cuts) - 1
    spans = [b - a for a, b in zip(cuts, cuts[1:])]
    pieces = len(widths)
    vmem = pl.BlockSpec(memory_space=pltpu.VMEM)
    anywhere = pl.BlockSpec(memory_space=pl.ANY)
    sems = pltpu.SemaphoreType.DMA
    spare = [LANES] + [0] * (pieces - 1)
    last = half - cuts[-1]
    return pl.pallas_call(
        functools.partial(fused_kernel, widths, cuts),
        out_shape=pltpu.VMEM((tok, wide), bf16),
        in_specs=[anywhere] * 6,
        out_specs=vmem,
        scratch_shapes=[pltpu.VMEM((2, 2, nz, 2, tok, w + s), bf16) for w, s in zip(widths, spare)]
        + [pltpu.VMEM((2, 2, nz, 2, tok, w), bf16) for w in spans + [last]]
        + [pltpu.VMEM((nz, 2, tok, w), bf16) for _ in range(3) for w in spans]
        + [pltpu.VMEM((2, tok, w), bf16) for w in spans]
        + [pltpu.VMEM((2, nz, tok, w), bf16) for w in spans]
        + [
            pltpu.VMEM((units, 2 * wide), bf16),
            pltpu.VMEM((units, 2 * wide), bf16),
            pltpu.VMEM((2, 2 * units, half), bf16),
            pltpu.VMEM((4 * nz * tok, 2 * units), bf16),
            pltpu.VMEM(expert_ids.shape[::-1], expert_ids.dtype),
            pltpu.VMEM(route_weights.shape[::-1], route_weights.dtype),
            pltpu.VMEM((nz, 2, 2, 2, tok, last), bf16),
            pltpu.VMEM((2, 2, 2, tok, last), bf16),
            pltpu.VMEM((2, tok, last), bf16),
            pltpu.VMEM((2, 3, tok, last), bf16),
            sems((pieces + 6,)),
            sems((pieces - 1, nz)),
            sems((pieces, nz)),
            sems((pieces, 2)),
            sems((nz,)),
            sems((pieces, 2)),
            sems((pieces, 3)),
            sems((pieces,)),
            sems((pieces,)),
            sems((pieces, 2)),
            sems((pieces,)),
            sems((2,)),
            sems((2,)),
            sems((2,)),
            sems((2,)),
        ]
        + [sems((splits,)), sems((splits, nz))] * 3
        + [
            sems((splits,)),
            sems((splits,)),
            sems((splits, 3)),
            sems((splits, 2)),
            sems((splits,)),
            sems((3,)),
            sems,
            sems,
            sems,
            sems,
            sems,
            sems,
            sems,
            sems,
            sems((2,)),
        ],
        compiler_params=pltpu.CompilerParams(
            collective_id=0, has_side_effects=True, vmem_limit_bytes=60 * 2**20
        ),
    )(tokens, expert_ids.T, route_weights.T, gate_weight, up_weight, down_weight)


def body(*args):
    every = args[1].shape[1] == lax.axis_size("expert") // 2
    tok, wide = args[0].shape
    even = lax.axis_size("tensor") == 2 and lax.axis_size("expert") == 16
    fits = tok % 16 == 0 and wide % 512 == 0 and 3 * args[1].shape[1] <= LANES
    if every and even and fits:
        return fused_body(*args)
    return sparse_body(*args)


def solution(mesh):
    placed = (
        P("expert", "tensor"),
        P("expert", None),
        P("expert", None),
        P("expert", "tensor", None),
        P("expert", "tensor", None),
        P("expert", "tensor", None),
    )
    return jax.shard_map(
        body, mesh=mesh, in_specs=placed, out_specs=P("expert", "tensor"), check_vma=False
    )
```

```python
import functools

import jax
import jax.numpy as jnp
from jax import lax
from jax.experimental import pallas as pl
from jax.experimental.pallas import tpu as pltpu
from jax.sharding import PartitionSpec as P

LANES = 128


def rows_times(rows, weight):
    return lax.dot_general(
        rows, weight, (((1,), (1,)), ((), ())), preferred_element_type=jnp.float32
    )


def sparse_body(tokens, expert_ids, route_weights, gate_weight, up_weight, down_weight):
    devices_wide = lax.axis_size("expert")
    experts = devices_wide // 2
    tok_count = expert_ids.shape[0]
    per_token = expert_ids.shape[1]
    capacity = min(tok_count, tok_count * per_token // experts)
    slot_count = experts * capacity
    arrived_count = devices_wide * capacity
    expert_range = jnp.arange(experts, dtype=jnp.int32)
    onehot = jnp.sum(
        (expert_ids[:, :, None] == expert_range[None, None, :]).astype(jnp.int32), axis=1
    )
    token_range = jnp.arange(tok_count, dtype=jnp.int32)
    earlier = token_range[None, :, None] < token_range[:, None, None]
    earlier_count = jnp.sum(jnp.where(earlier, onehot[None, :, :], 0), axis=1)
    slot_rank = jnp.take_along_axis(earlier_count, expert_ids, axis=1)
    slot_of = expert_ids * capacity + slot_rank
    slot_range = jnp.arange(slot_count, dtype=jnp.int32)
    select = jnp.any(slot_of[None, :, :] == slot_range[:, None, None], axis=2).astype(jnp.bfloat16)
    weight_gate = gate_weight[0]
    weight_up = up_weight[0]
    weight_out = down_weight[0]
    whole_rows = lax.all_gather(tokens, "tensor", axis=1, tiled=True)
    packed = jnp.dot(select, whole_rows, preferred_element_type=jnp.float32).astype(jnp.bfloat16)
    packed = packed.reshape(experts, capacity, whole_rows.shape[1])
    arrived = lax.all_to_all(
        jnp.repeat(packed, 2, axis=0), "expert", split_axis=0, concat_axis=0, tiled=True
    ).reshape(arrived_count, -1)
    gate_act = rows_times(arrived, weight_gate)
    up_act = rows_times(arrived, weight_up)
    hidden = (jax.nn.silu(gate_act) * up_act).astype(jnp.bfloat16)
    columns = lax.all_to_all(weight_out, "tensor", split_axis=1, concat_axis=0, tiled=True)
    unit_count = hidden.shape[1]
    shard_piece = lax.all_gather(hidden, "tensor", axis=1, tiled=True)
    groups = shard_piece.shape[1] // unit_count
    weight_rows = columns
    weight_rows = weight_rows.reshape(groups, unit_count, columns.shape[1])
    grouped = shard_piece.reshape(shard_piece.shape[0], groups, unit_count)
    group_terms = jnp.einsum(
        "rgf,gfd->grd", grouped, weight_rows, preferred_element_type=jnp.float32
    ).astype(jnp.bfloat16)
    group_terms = lax.optimization_barrier(group_terms)
    half_out = jnp.sum(group_terms.astype(jnp.float32), axis=0).astype(jnp.bfloat16)
    returned = lax.all_to_all(
        half_out.reshape(devices_wide, capacity, -1),
        "expert",
        split_axis=0,
        concat_axis=0,
        tiled=True,
    )
    returned = returned.reshape(experts, 2, capacity, -1).astype(jnp.float32)
    combined = (returned[:, 0] + returned[:, 1]).reshape(slot_count, -1)
    picked = combined[slot_of]
    mixed_out = jnp.sum(route_weights[:, :, None] * picked, axis=1)
    return mixed_out.astype(jnp.bfloat16)


OWN, FIRST, SECOND, DIAGONAL = range(4)
HERE, SIDE, FAR_MID, FAR_END = range(4)
GATHER = (
    ('zn', 1), ('bd', 0, 0), ('zf', 0), ('zn', 0), ('bd', 1, 0), ('a', 3), ('a', 2), ('a', 0), ('bd', 3, 0), ('a', 1),
    ('own', 1, 1), ('zf', 1), ('zn', 2), ('bd', 1, 1), ('own', 0, 2), ('first', 3, 0), ('bd', 2, 0), ('zf', 2),
    ('bd', 0, 2), ('own', 0, 3), ('first', 0, 0), ('bd', 0, 3), ('own', 0, 1), ('bd', 0, 1), ('own', 2, 1),
    ('bd', 2, 1), ('here',), ('own', 1, 2), ('bd', 1, 2), ('own', 2, 2), ('first', 1, 1), ('co', 0), ('own', 1, 3),
    ('bd', 1, 3), ('cs', 0), ('first', 0, 1), ('co', 1), ('bd', 2, 2), ('own', 2, 3), ('bd', 2, 3), ('first', 0, 3),
    ('first', 0, 2), ('cf', 0), ('first', 1, 2), ('first', 2, 1), ('first', 2, 0), ('cs', 1), ('plane', 1), ('co', 2),
    ('first', 1, 3), ('first', 1, 0), ('cf', 1), ('cs', 2), ('first', 2, 2), ('first', 2, 3), ('cf', 2), ('plane', 2),
    ('cd', 0), ('share', 0, 0), ('plane', 3), ('cd', 1), ('share', 1, 0), ('share', 0, 1), ('cd', 2), ('share', 2, 0),
    ('share', 3, 1), ('share', 1, 1), ('share', 3, 0), ('share', 2, 1),
)
SCATTER = (
    ('down', 0), ('rd', 2, 0), ('rd', 3, 0), ('downL',), ('lz', 3), ('lz', 2), ('down', 1), ('rb', 1, 0),
    ('rd', 2, 1), ('rd', 3, 1), ('rd', 1, 1), ('rb', 3, 0), ('turn', 3, 0), ('lz', 1), ('turn', 2, 0), ('rb', 2, 0),
    ('turn', 3, 1), ('rd', 1, 0), ('rb', 3, 1), ('lrelay',), ('turn', 1, 1), ('rd', 0, 0), ('rb', 2, 1), ('rb', 1, 1),
    ('home', 3, 0), ('home', 2, 0), ('rd', 0, 1), ('turn', 2, 1), ('turn', 1, 0), ('home', 3, 1), ('lsum',), ('ld',),
    ('rb', 0, 1), ('rb', 0, 0), ('turn', 0, 0), ('home', 1, 1), ('home', 2, 1), ('relay', 0), ('turn', 0, 1),
    ('home', 1, 0), ('lb',), ('relay', 1), ('lturn',), ('home', 0, 0), ('lc',), ('home', 0, 1),
)


def fused_kernel(
    widths, cuts, tok_hbm, ids_hbm, rw_hbm, gate_hbm, up_hbm, down_hbm, out_ref, *scratch
):
    pieces, splits = len(widths), len(cuts) - 1
    rows, scratch = scratch[:pieces], scratch[pieces:]
    parts, scratch = scratch[: splits + 1], scratch[splits + 1 :]
    diag_bufs, scratch = scratch[:splits], scratch[splits:]
    first_bufs, scratch = scratch[:splits], scratch[splits:]
    second_bufs, scratch = scratch[:splits], scratch[splits:]
    relay_bufs, scratch = scratch[:splits], scratch[splits:]
    owner_bufs, scratch = scratch[:splits], scratch[splits:]
    (
        gate, up, down, hid, ids_buf, rw_buf, late_buf, late_relay, late_diag, late_owner,
        load_sem, own_recv, first_recv, side_recv, plane_recv, core_recv, gz_send, gr_send, ga_send, gb_send, gc_send,
        down_send, down_recv, hid_send, hid_recv,
        rd_send, rd_recv, ra_send, ra_recv, rb_send, rb_recv, rr_send, rr_recv, rz_send, rz_recv, rc_send,
        lz_send, lz_recv, lr_send, lr_recv, ld_send, ld_recv, la_send, lb_send, lc_send, lo_recv,
    ) = scratch
    nz = rows[0].shape[2]
    me, y = lax.axis_index("expert"), lax.axis_index("tensor")
    c = lax.rem(me, 2)
    x = lax.rem(me // 2, 2)
    z = me // 4
    oc, ox, oy = 1 - c, 1 - x, 1 - y
    tok, wide = out_ref.shape
    half = wide // 2
    units = gate.shape[0]
    experts = 2 * nz
    count = 4 * nz * tok
    top = ids_hbm.shape[0]
    last = pieces - 1
    starts = [sum(widths[:p]) for p in range(pieces)]
    wide_f, narrow = jnp.float32, jnp.bfloat16
    middle = (z > 0) & (z < nz - 1)
    side = jnp.where(lax.rem(z, 2) == 0, z + 1, z - 1)
    low = z < nz // 2
    near = [z, side, jnp.where(low, nz // 2, nz // 2 - 1), jnp.where(low, nz - 1, 0)]
    far_end = near[FAR_END]
    columns = [
        (x, y),
        (jnp.where(c == 0, ox, x), jnp.where(c == 0, y, oy)),
        (jnp.where(c == 0, x, ox), jnp.where(c == 0, oy, y)),
        (ox, oy),
    ]

    def dev(zz, xx, cc, yy):
        return ((zz * 2 + xx) * 2 + cc, yy)

    def beside(col, cc):
        xx, yy = columns[col]
        return dev(z, xx, cc, yy)

    dev_a, dev_b, dev_c = beside(FIRST, c), beside(SECOND, c), dev(z, x, oc, y)
    dev_side = dev(side, x, c, y)

    def in_middle(action):
        @pl.when(middle)
        def _():
            action()

    def at_ends(action):
        @pl.when(jnp.logical_not(middle))
        def _():
            action()

    def remote(src, dst, send, recv, to):
        return pltpu.make_async_remote_copy(
            src_ref=src, dst_ref=dst, send_sem=send, recv_sem=recv,
            device_id=to, device_id_type=pl.DeviceIdType.MESH,
        )

    barrier = pltpu.get_barrier_semaphore()

    def greet(to):
        pl.semaphore_signal(barrier, inc=1, device_id=to, device_id_type=pl.DeviceIdType.MESH)

    partners = [dev(near[k], x, cc, y) for k in (FAR_MID, SIDE) for cc in (c, oc)]
    partners += [beside(col, cc) for col in (FIRST, SECOND) for cc in (c, oc)] + [dev_c]

    @pl.when(middle)
    def _():
        for cc in (c, oc):
            greet(dev(far_end, x, cc, y))

    for to in partners:
        greet(to)
    small_loads = [
        pltpu.make_async_copy(ids_hbm, ids_buf, load_sem.at[0]),
        pltpu.make_async_copy(rw_hbm, rw_buf, load_sem.at[1]),
    ]
    tok_loads = [
        pltpu.make_async_copy(
            tok_hbm.at[:, pl.ds(starts[p], widths[p])],
            rows[p].at[y, x, z, c, :, pl.ds(0, widths[p])],
            load_sem.at[2 + p],
        )
        for p in range(pieces)
    ]
    gate_load = pltpu.make_async_copy(gate_hbm.at[0], gate, load_sem.at[pieces + 2])
    up_load = pltpu.make_async_copy(up_hbm.at[0], up, load_sem.at[pieces + 3])

    def down_rows(cc, yy):
        return (
            down_hbm.at[0, :, pl.ds(pl.multiple_of((2 * yy + cc) * half, LANES), half)],
            down.at[yy, pl.ds(pl.multiple_of(c * units, units), units)],
        )

    down_loads = [
        pltpu.make_async_copy(*down_rows(c, yy), load_sem.at[pieces + 4 + yy]) for yy in range(2)
    ]
    for load in small_loads + tok_loads + [gate_load, up_load] + down_loads:
        load.start()
    for load in small_loads:
        load.wait()
    ids = ids_buf[...].astype(wide_f).T
    weights = rw_buf[...].T
    lane = lax.broadcasted_iota(jnp.int32, (tok, LANES), 1)
    which = lax.rem(lane, experts).astype(wide_f)
    spread = jnp.zeros((tok, LANES), wide_f)
    for j in range(top):
        spread = jnp.where(ids[:, j : j + 1] == which, weights[:, j : j + 1], spread)
    first = spread.astype(narrow).astype(wide_f)
    rest = spread - first
    second = rest.astype(narrow).astype(wide_f)
    third = rest - second
    terms = jnp.where(lane < experts, first, jnp.where(lane < 2 * experts, second, third))
    terms = jnp.where(lane < 3 * experts, terms, 0.0)
    rows[0][y, x, z, c, :, widths[0] :] = terms.astype(narrow)
    for load in tok_loads:
        load.wait()
    pl.semaphore_wait(barrier, len(partners) + 2 * middle.astype(jnp.int32))

    def column(p, col, cc=c):
        xx, yy = columns[col]
        return rows[p].at[yy, xx, :, cc]

    def cell(p, col, zz):
        xx, yy = columns[col]
        return rows[p].at[yy, xx, zz, c]

    def layer(zz, cc=c):
        return rows[last].at[:, :, zz, cc]

    def same(ref, send, recv, to):
        return remote(ref, ref, send, recv, to)

    def over_z(k):
        return dev(near[k], x, c, y)

    def z_copy(p, k):
        return same(cell(p, OWN, z), gz_send.at[p, k - 1], own_recv.at[p, z], over_z(k))

    def relay_copy(p):
        return same(cell(p, OWN, far_end), gr_send.at[p], own_recv.at[p, far_end], dev_side)

    def a_copy(p, zz):
        return same(cell(p, OWN, zz), ga_send.at[p], first_recv.at[p, zz], dev_a)

    def b_copy(p, zz):
        return same(cell(p, OWN, zz), gb_send.at[p, 0], side_recv.at[p, 0], dev_b)

    def d_copy(p, zz):
        return same(cell(p, FIRST, zz), gb_send.at[p, 1], side_recv.at[p, 1], dev_b)

    def c_copy(p, col):
        _, yy = columns[col]
        return same(column(p, col), gc_send.at[p], core_recv.at[p, yy], dev_c)

    def layer_copy(k):
        return same(layer(z), gz_send.at[last, k - 1], plane_recv.at[z], over_z(k))

    def layer_relay():
        return same(layer(far_end), gr_send.at[last], plane_recv.at[far_end], dev_side)

    def layer_core(zz):
        return same(layer(zz), gc_send.at[last], core_recv.at[last, 0], dev_c)

    def landed(ref, recv):
        same(ref, gr_send.at[last], recv, dev_c).wait_recv()

    def left(ref, send):
        same(ref, send, core_recv.at[last, 0], dev_c).wait_send()

    def to_far(copy):
        copy(FAR_MID).start()

        @pl.when(middle)
        def _():
            copy(FAR_END).start()

    def own(p, k):
        landed(cell(p, OWN, near[k]), own_recv.at[p, near[k]])
        if k == FAR_END:
            in_middle(lambda: relay_copy(p).start())
        a_copy(p, near[k]).start()

    def first_block(p, k):
        landed(cell(p, FIRST, near[k]), first_recv.at[p, near[k]])
        d_copy(p, near[k]).start()

    def sideways(p, j):
        landed(column(p, SECOND + j), side_recv.at[p, j])
        c_copy(p, SECOND + j).start()

    def here():
        for j in range(2):
            landed(cell(last, SECOND + j, z), side_recv.at[last, j])
        to_far(layer_copy)
        layer_copy(SIDE).start()
        layer_core(z).start()

    def layer_in(k):
        landed(layer(near[k]), plane_recv.at[near[k]])
        if k == FAR_END:
            in_middle(lambda: layer_relay().start())
        layer_core(near[k]).start()

    contract = (((1,), (1,)), ((), ()))
    sums, layers_in = [], []

    def share(p, turn_of):
        yy = oy if turn_of else y
        if p < last:
            landed(rows[p].at[yy, :, :, oc], core_recv.at[p, yy])
        elif not layers_in:
            landed(rows[p].at[:, :, :, oc], core_recv.at[p, 0])
            layers_in.append(p)
        if not sums:
            gate_load.wait()
            up_load.wait()
        block = rows[p][yy, :, :, :, :, : widths[p]].reshape(count, widths[p])
        cols = pl.ds(pl.multiple_of(yy * wide + starts[p], LANES), widths[p])
        g = lax.dot_general(block, gate[:, cols], contract, preferred_element_type=wide_f)
        u = lax.dot_general(block, up[:, cols], contract, preferred_element_type=wide_f)
        sums.append((g, u) if not sums else (sums[-1][0] + g, sums[-1][1] + u))

    gather = {
        "zn": lambda p: z_copy(p, SIDE).start(),
        "zf": lambda p: to_far(functools.partial(z_copy, p)),
        "a": lambda p: a_copy(p, z).start(),
        "bd": lambda p, k: b_copy(p, near[k]).start(),
        "own": own,
        "first": first_block,
        "co": lambda p: c_copy(p, OWN).start(),
        "cf": lambda p: c_copy(p, FIRST).start(),
        "cs": lambda p: sideways(p, 0),
        "cd": lambda p: sideways(p, 1),
        "here": here,
        "plane": layer_in,
        "share": share,
    }
    down_copies = []
    for yy in range(2):
        src, dst = down_rows(oc, yy)
        down_copies.append(remote(src, dst, down_send.at[yy], down_recv.at[yy], dev_c))

    def route_scale():
        lanes = lax.broadcasted_iota(jnp.int32, (count, LANES), 1)
        mine = (lax.rem(lanes, experts) == me // 2) & (lanes < 3 * experts)
        kept = rows[0][0, :, :, :, :, widths[0] :].reshape(count, LANES).astype(wide_f)
        return jnp.sum(jnp.where(mine, kept, 0.0), axis=1, keepdims=True)

    shared = []
    started = False
    for name, *where in GATHER:
        if name == "own" and not started:
            for copy in down_copies:
                copy.start()
            started = True
        gather[name](*where)
        if name == "share" and where[0] == 0:
            shared.append(where)
            if len(shared) == 2:
                scale = route_scale()
    gate_act, up_act = sums[-1]
    hid_cols = pl.ds(pl.multiple_of(c * units, units), units)
    hid_copies = []
    for i in range(2):
        part = slice(i * count // 2, (i + 1) * count // 2)
        act = jax.nn.silu(gate_act[part]) * up_act[part] * scale[part]
        hid[part, hid_cols] = act.astype(narrow)
        ref = hid.at[pl.ds(i * count // 2, count // 2), hid_cols]
        hid_copies.append(remote(ref, ref, hid_send.at[i], hid_recv.at[i], dev_c))
        hid_copies[i].start()
    for load in down_loads:
        load.wait()
    for copy in down_copies:
        copy.wait_recv()
    for copy in hid_copies:
        copy.wait_recv()

    def project(r):
        begin, end = cuts[r], cuts[r + 1] if r < splits else half
        for yy in range(2):
            term = jnp.dot(hid[...], down[yy, :, begin:end], preferred_element_type=wide_f)
            parts[r][yy] = term.astype(narrow).reshape(2, nz, 2, tok, end - begin)

    def block(r, col, zz):
        xx, yy = columns[col]
        return parts[r].at[yy, xx, zz]

    def total(*terms):
        out = terms[0].astype(wide_f)
        for term in terms[1:]:
            out = out + term.astype(wide_f)
        return out

    def rd(k, r):
        zz = near[k]
        return remote(block(r, DIAGONAL, zz), diag_bufs[r].at[zz], rd_send.at[r], rd_recv.at[r, zz], dev_b)

    def rb(k, r):
        zz = near[k]
        return remote(block(r, SECOND, zz), second_bufs[r].at[zz], rb_send.at[r], rb_recv.at[r, zz], dev_b)

    def ra(k, r):
        zz = near[k]
        return remote(block(r, FIRST, zz), first_bufs[r].at[zz], ra_send.at[r], ra_recv.at[r, zz], dev_a)

    def rr(r):
        return remote(block(r, OWN, far_end), relay_bufs[r], rr_send.at[r], rr_recv.at[r], dev_side)

    def rz(k, r, cc):
        zz = near[k]
        return remote(
            block(r, OWN, zz).at[cc], owner_bufs[r].at[c, z], rz_send.at[r, k - 1], rz_recv.at[r, c], dev(zz, x, cc, y)
        )

    def rc(r):
        return remote(block(r, OWN, z).at[oc], owner_bufs[r].at[c, z], rc_send.at[r], rz_recv.at[r, c], dev_c)

    def landed_slots(ref, slots, recv):
        landed(ref.at[pl.ds(0, slots)], recv)

    def plane(zz):
        return parts[splits].at[:, :, zz]

    def lz(k):
        return remote(plane(near[k]), late_buf.at[z], lz_send.at[k - 1], lz_recv, over_z(k))

    def lr():
        return remote(plane(far_end), late_relay, lr_send, lr_recv, dev_side)

    def ld():
        return remote(block(splits, DIAGONAL, z), late_diag, ld_send, ld_recv, dev_b)

    def la(cc):
        return remote(
            block(splits, FIRST, z).at[cc], late_owner.at[c, 0], la_send, lo_recv.at[c], beside(FIRST, cc)
        )

    def lb(cc):
        return remote(
            block(splits, SECOND, z).at[cc], late_owner.at[c, 1], lb_send, lo_recv.at[c], beside(SECOND, cc)
        )

    def lc():
        return remote(block(splits, OWN, z).at[oc], late_owner.at[c, 2], lc_send, lo_recv.at[c], dev_c)

    def send_late(k):
        if k == FAR_END:
            at_ends(lambda: lr().start())
        else:
            lz(k).start()

    def turn(k, r):
        rd(k, r).wait_recv()
        ref = block(r, FIRST, near[k])
        ref[...] = total(ref[...], diag_bufs[r][near[k]]).astype(narrow)
        ra(k, r).start()

    def home(k, r):
        ra(k, r).wait_recv()
        rb(k, r).wait_recv()
        ref = block(r, OWN, near[k])
        ref[...] = total(ref[...], first_bufs[r][near[k]], second_bufs[r][near[k]]).astype(narrow)
        if k == FAR_END:
            at_ends(lambda: rr(r).start())
        elif k == HERE:
            rc(r).start()
        else:
            for cc in range(2):
                rz(k, r, cc).start()

    def relay(r):
        @pl.when(middle)
        def _():
            rr(r).wait_recv()
            ref = block(r, OWN, far_end)
            ref[...] = total(ref[...], relay_bufs[r][...]).astype(narrow)
            for cc in range(2):
                rz(FAR_END, r, cc).start()

    def late_pass():
        @pl.when(middle)
        def _():
            lr().wait_recv()
            ref = plane(far_end)
            ref[...] = total(ref[...], late_relay[...]).astype(narrow)
            lz(FAR_END).start()

    def late_sum():
        ref = plane(z)

        @pl.when(middle)
        def _():
            landed_slots(late_buf, nz - 1, lz_recv)
            ref[...] = total(ref[...], late_buf[side], late_buf[near[FAR_MID]], late_buf[far_end]).astype(narrow)

        @pl.when(jnp.logical_not(middle))
        def _():
            landed_slots(late_buf, nz - 2, lz_recv)
            ref[...] = total(ref[...], late_buf[side], late_buf[near[FAR_MID]]).astype(narrow)

    def late_turn():
        ld().wait_recv()
        ref = block(splits, FIRST, z)
        ref[...] = total(ref[...], late_diag[...]).astype(narrow)
        for cc in range(2):
            la(cc).start()

    def late_out(j):
        core, mine_too = (oc, late_owner.at[oc, 2]) if j else (c, block(splits, OWN, z).at[c])
        landed_slots(late_owner.at[core], 2 + j, lo_recv.at[core])
        at = pl.ds(pl.multiple_of(core * half + cuts[splits], LANES), half - cuts[splits])
        out_ref[:, at] = total(mine_too[...], late_owner[core, 0], late_owner[core, 1]).astype(narrow)

    def out(r, j):
        bufs = owner_bufs[r]
        core, mine_too = (oc, bufs.at[oc, z]) if j else (c, block(r, OWN, z).at[c])
        at = pl.ds(pl.multiple_of(core * half + cuts[r], LANES), cuts[r + 1] - cuts[r])

        @pl.when(middle)
        def _():
            landed_slots(bufs.at[core], nz - 1 + j, rz_recv.at[r, core])
            sums = [bufs[core, near[k]] for k in (SIDE, FAR_MID, FAR_END)]
            out_ref[:, at] = total(mine_too[...], *sums).astype(narrow)

        @pl.when(jnp.logical_not(middle))
        def _():
            landed_slots(bufs.at[core], nz - 2 + j, rz_recv.at[r, core])
            sums = [bufs[core, near[k]] for k in (SIDE, FAR_MID)]
            out_ref[:, at] = total(mine_too[...], *sums).astype(narrow)

    scatter = {
        "downL": lambda: project(splits),
        "down": project,
        "lz": send_late,
        "rd": lambda k, r: rd(k, r).start(),
        "rb": lambda k, r: rb(k, r).start(),
        "turn": turn,
        "home": home,
        "relay": relay,
        "lrelay": late_pass,
        "lsum": late_sum,
        "ld": lambda: ld().start(),
        "lb": lambda: [lb(cc).start() for cc in range(2)],
        "lc": lambda: lc().start(),
        "lturn": late_turn,
    }
    for name, *where in SCATTER:
        scatter[name](*where)
    for r in range(splits):
        for j in range(2):
            out(r, j)
    for j in range(2):
        late_out(j)

    for p in range(last):
        z_copy(p, SIDE).wait_send()
        z_copy(p, FAR_MID).wait_send()
        left(column(p, OWN), ga_send.at[p])
        left(column(p, OWN), gb_send.at[p, 0])
        left(column(p, FIRST), gb_send.at[p, 1])
        left(rows[p].at[:, :, :, c], gc_send.at[p])
    a_copy(last, z).wait_send()
    b_copy(last, z).wait_send()
    d_copy(last, z).wait_send()
    layer_copy(SIDE).wait_send()
    layer_copy(FAR_MID).wait_send()
    left(rows[last].at[:, :, :, c], gc_send.at[last])
    for r in range(splits):
        left(first_bufs[r], ra_send.at[r])
        left(diag_bufs[r], rd_send.at[r])
        left(second_bufs[r], rb_send.at[r])
        left(relay_bufs[r], rz_send.at[r, SIDE - 1])
        left(relay_bufs[r], rz_send.at[r, FAR_MID - 1])
        rc(r).wait_send()
    left(late_diag, la_send)
    left(late_diag, lb_send)
    for copy in [lz(SIDE), lz(FAR_MID), ld(), lc()] + hid_copies + down_copies:
        copy.wait_send()

    @pl.when(middle)
    def _():
        for p in range(last):
            z_copy(p, FAR_END).wait_send()
            relay_copy(p).wait_send()
        layer_copy(FAR_END).wait_send()
        layer_relay().wait_send()
        lz(FAR_END).wait_send()
        for r in range(splits):
            left(relay_bufs[r], rz_send.at[r, FAR_END - 1])

    @pl.when(jnp.logical_not(middle))
    def _():
        lr().wait_send()
        for r in range(splits):
            rr(r).wait_send()


def fused_body(tokens, expert_ids, route_weights, gate_weight, up_weight, down_weight):
    nz = lax.axis_size("expert") // 4
    tok, wide = tokens.shape
    half = wide // 2
    units = gate_weight.shape[1]
    bf16 = jnp.bfloat16
    tiles = wide // (2 * LANES)
    ahead = max(1, tiles * 3 // 14)
    others = tiles - ahead
    widths = [2 * LANES * n for n in ((others + 2) // 3, (others + 1) // 3, others // 3, ahead)]
    lanes = half // LANES
    late = max(1, lanes * 3 // 14)
    cuts = [0, LANES * (lanes * 3 // 7), half - LANES * late]
    splits = len(cuts) - 1
    spans = [b - a for a, b in zip(cuts, cuts[1:])]
    pieces = len(widths)
    vmem = pl.BlockSpec(memory_space=pltpu.VMEM)
    anywhere = pl.BlockSpec(memory_space=pl.ANY)
    sems = pltpu.SemaphoreType.DMA
    spare = [LANES] + [0] * (pieces - 1)
    last = half - cuts[-1]
    return pl.pallas_call(
        functools.partial(fused_kernel, widths, cuts),
        out_shape=pltpu.VMEM((tok, wide), bf16),
        in_specs=[anywhere] * 6,
        out_specs=vmem,
        scratch_shapes=[pltpu.VMEM((2, 2, nz, 2, tok, w + s), bf16) for w, s in zip(widths, spare)]
        + [pltpu.VMEM((2, 2, nz, 2, tok, w), bf16) for w in spans + [last]]
        + [pltpu.VMEM((nz, 2, tok, w), bf16) for _ in range(3) for w in spans]
        + [pltpu.VMEM((2, tok, w), bf16) for w in spans]
        + [pltpu.VMEM((2, nz, tok, w), bf16) for w in spans]
        + [
            pltpu.VMEM((units, 2 * wide), bf16),
            pltpu.VMEM((units, 2 * wide), bf16),
            pltpu.VMEM((2, 2 * units, half), bf16),
            pltpu.VMEM((4 * nz * tok, 2 * units), bf16),
            pltpu.VMEM(expert_ids.shape[::-1], expert_ids.dtype),
            pltpu.VMEM(route_weights.shape[::-1], route_weights.dtype),
            pltpu.VMEM((nz, 2, 2, 2, tok, last), bf16),
            pltpu.VMEM((2, 2, 2, tok, last), bf16),
            pltpu.VMEM((2, tok, last), bf16),
            pltpu.VMEM((2, 3, tok, last), bf16),
            sems((pieces + 6,)),
            sems((pieces - 1, nz)),
            sems((pieces, nz)),
            sems((pieces, 2)),
            sems((nz,)),
            sems((pieces, 2)),
            sems((pieces, 3)),
            sems((pieces,)),
            sems((pieces,)),
            sems((pieces, 2)),
            sems((pieces,)),
            sems((2,)),
            sems((2,)),
            sems((2,)),
            sems((2,)),
        ]
        + [sems((splits,)), sems((splits, nz))] * 3
        + [
            sems((splits,)),
            sems((splits,)),
            sems((splits, 3)),
            sems((splits, 2)),
            sems((splits,)),
            sems((3,)),
            sems,
            sems,
            sems,
            sems,
            sems,
            sems,
            sems,
            sems,
            sems((2,)),
        ],
        compiler_params=pltpu.CompilerParams(
            collective_id=0, has_side_effects=True, vmem_limit_bytes=60 * 2**20
        ),
    )(tokens, expert_ids.T, route_weights.T, gate_weight, up_weight, down_weight)


def body(*args):
    every = args[1].shape[1] == lax.axis_size("expert") // 2
    tok, wide = args[0].shape
    even = lax.axis_size("tensor") == 2 and lax.axis_size("expert") == 16
    fits = tok % 16 == 0 and wide % 512 == 0 and 3 * args[1].shape[1] <= LANES
    if every and even and fits:
        return fused_body(*args)
    return sparse_body(*args)


def solution(mesh):
    placed = (
        P("expert", "tensor"),
        P("expert", None),
        P("expert", None),
        P("expert", "tensor", None),
        P("expert", "tensor", None),
        P("expert", "tensor", None),
    )
    return jax.shard_map(
        body, mesh=mesh, in_specs=placed, out_specs=P("expert", "tensor"), check_vma=False
    )
```

```python
import functools

import jax
import jax.numpy as jnp
from jax import lax
from jax.experimental import pallas as pl
from jax.experimental.pallas import tpu as pltpu
from jax.sharding import PartitionSpec as P

LANES = 128


def rows_times(rows, weight):
    return lax.dot_general(
        rows, weight, (((1,), (1,)), ((), ())), preferred_element_type=jnp.float32
    )


def sparse_body(tokens, expert_ids, route_weights, gate_weight, up_weight, down_weight):
    devices_wide = lax.axis_size("expert")
    experts = devices_wide // 2
    tok_count = expert_ids.shape[0]
    per_token = expert_ids.shape[1]
    capacity = min(tok_count, tok_count * per_token // experts)
    slot_count = experts * capacity
    arrived_count = devices_wide * capacity
    expert_range = jnp.arange(experts, dtype=jnp.int32)
    onehot = jnp.sum(
        (expert_ids[:, :, None] == expert_range[None, None, :]).astype(jnp.int32), axis=1
    )
    token_range = jnp.arange(tok_count, dtype=jnp.int32)
    earlier = token_range[None, :, None] < token_range[:, None, None]
    earlier_count = jnp.sum(jnp.where(earlier, onehot[None, :, :], 0), axis=1)
    slot_rank = jnp.take_along_axis(earlier_count, expert_ids, axis=1)
    slot_of = expert_ids * capacity + slot_rank
    slot_range = jnp.arange(slot_count, dtype=jnp.int32)
    select = jnp.any(slot_of[None, :, :] == slot_range[:, None, None], axis=2).astype(jnp.bfloat16)
    weight_gate = gate_weight[0]
    weight_up = up_weight[0]
    weight_out = down_weight[0]
    whole_rows = lax.all_gather(tokens, "tensor", axis=1, tiled=True)
    packed = jnp.dot(select, whole_rows, preferred_element_type=jnp.float32).astype(jnp.bfloat16)
    packed = packed.reshape(experts, capacity, whole_rows.shape[1])
    arrived = lax.all_to_all(
        jnp.repeat(packed, 2, axis=0), "expert", split_axis=0, concat_axis=0, tiled=True
    ).reshape(arrived_count, -1)
    gate_act = rows_times(arrived, weight_gate)
    up_act = rows_times(arrived, weight_up)
    hidden = (jax.nn.silu(gate_act) * up_act).astype(jnp.bfloat16)
    columns = lax.all_to_all(weight_out, "tensor", split_axis=1, concat_axis=0, tiled=True)
    unit_count = hidden.shape[1]
    shard_piece = lax.all_gather(hidden, "tensor", axis=1, tiled=True)
    groups = shard_piece.shape[1] // unit_count
    weight_rows = columns
    weight_rows = weight_rows.reshape(groups, unit_count, columns.shape[1])
    grouped = shard_piece.reshape(shard_piece.shape[0], groups, unit_count)
    group_terms = jnp.einsum(
        "rgf,gfd->grd", grouped, weight_rows, preferred_element_type=jnp.float32
    ).astype(jnp.bfloat16)
    group_terms = lax.optimization_barrier(group_terms)
    half_out = jnp.sum(group_terms.astype(jnp.float32), axis=0).astype(jnp.bfloat16)
    returned = lax.all_to_all(
        half_out.reshape(devices_wide, capacity, -1),
        "expert",
        split_axis=0,
        concat_axis=0,
        tiled=True,
    )
    returned = returned.reshape(experts, 2, capacity, -1).astype(jnp.float32)
    combined = (returned[:, 0] + returned[:, 1]).reshape(slot_count, -1)
    picked = combined[slot_of]
    mixed_out = jnp.sum(route_weights[:, :, None] * picked, axis=1)
    return mixed_out.astype(jnp.bfloat16)


OWN, FIRST, SECOND, DIAGONAL = range(4)
HERE, SIDE, FAR_MID, FAR_END = range(4)
GATHER = (
    ('zn', 1), ('bd', 0, 0), ('zf', 0), ('zn', 0), ('bd', 1, 0), ('a', 3), ('a', 2), ('a', 0), ('bd', 3, 0), ('a', 1),
    ('own', 1, 1), ('zf', 1), ('zn', 2), ('bd', 1, 1), ('own', 0, 2), ('first', 3, 0), ('bd', 2, 0), ('zf', 2),
    ('bd', 0, 2), ('own', 0, 3), ('first', 0, 0), ('bd', 0, 3), ('own', 0, 1), ('bd', 0, 1), ('own', 2, 1),
    ('bd', 2, 1), ('here',), ('own', 1, 2), ('bd', 1, 2), ('own', 2, 2), ('first', 1, 1), ('co', 0), ('own', 1, 3),
    ('bd', 1, 3), ('cs', 0), ('first', 0, 1), ('co', 1), ('bd', 2, 2), ('own', 2, 3), ('bd', 2, 3), ('first', 0, 3),
    ('first', 0, 2), ('cf', 0), ('first', 1, 2), ('first', 2, 1), ('first', 2, 0), ('cs', 1), ('plane', 1), ('co', 2),
    ('first', 1, 3), ('first', 1, 0), ('cf', 1), ('cs', 2), ('first', 2, 2), ('first', 2, 3), ('cf', 2), ('plane', 2),
    ('cd', 0), ('share', 0, 0), ('plane', 3), ('cd', 1), ('share', 1, 0), ('share', 0, 1), ('cd', 2), ('share', 2, 0),
    ('share', 3, 1), ('share', 1, 1), ('share', 3, 0), ('share', 2, 1),
)
SCATTER = (
    ('down', 0, 1), ('down', 0, 0), ('rd', 2, 0), ('rd', 3, 0), ('downL',), ('lz', 3), ('lz', 2), ('down', 1, 1),
    ('down', 1, 0), ('rb', 1, 0),
    ('rd', 2, 1), ('rd', 3, 1), ('rd', 1, 1), ('rb', 3, 0), ('turn', 3, 0), ('lz', 1), ('turn', 2, 0), ('rb', 2, 0),
    ('turn', 3, 1), ('rd', 1, 0), ('rb', 3, 1), ('lrelay',), ('turn', 1, 1), ('rd', 0, 0), ('rb', 2, 1), ('rb', 1, 1),
    ('home', 3, 0), ('home', 2, 0), ('rd', 0, 1), ('turn', 2, 1), ('turn', 1, 0), ('home', 3, 1), ('lsum',), ('ld',),
    ('rb', 0, 1), ('rb', 0, 0), ('turn', 0, 0), ('home', 1, 1), ('home', 2, 1), ('relay', 0), ('turn', 0, 1),
    ('home', 1, 0), ('lb',), ('relay', 1), ('lturn',), ('home', 0, 0), ('lc',), ('home', 0, 1),
)


def fused_kernel(
    widths, cuts, tok_hbm, ids_hbm, rw_hbm, gate_hbm, up_hbm, down_hbm, out_ref, *scratch
):
    pieces, splits = len(widths), len(cuts) - 1
    rows, scratch = scratch[:pieces], scratch[pieces:]
    parts, scratch = scratch[: splits + 1], scratch[splits + 1 :]
    diag_bufs, scratch = scratch[:splits], scratch[splits:]
    first_bufs, scratch = scratch[:splits], scratch[splits:]
    second_bufs, scratch = scratch[:splits], scratch[splits:]
    relay_bufs, scratch = scratch[:splits], scratch[splits:]
    owner_bufs, scratch = scratch[:splits], scratch[splits:]
    (
        gate, up, down, hid, ids_buf, rw_buf, late_buf, late_relay, late_diag, late_owner,
        load_sem, own_recv, first_recv, side_recv, plane_recv, core_recv, gz_send, gr_send, ga_send, gb_send, gc_send,
        down_send, down_recv, hid_send, hid_recv,
        rd_send, rd_recv, ra_send, ra_recv, rb_send, rb_recv, rr_send, rr_recv, rz_send, rz_recv, rc_send,
        lz_send, lz_recv, lr_send, lr_recv, ld_send, ld_recv, la_send, lb_send, lc_send, lo_recv,
    ) = scratch
    nz = rows[0].shape[2]
    me, y = lax.axis_index("expert"), lax.axis_index("tensor")
    c = lax.rem(me, 2)
    x = lax.rem(me // 2, 2)
    z = me // 4
    oc, ox, oy = 1 - c, 1 - x, 1 - y
    tok, wide = out_ref.shape
    half = wide // 2
    units = gate.shape[0]
    experts = 2 * nz
    count = 4 * nz * tok
    top = ids_hbm.shape[0]
    last = pieces - 1
    starts = [sum(widths[:p]) for p in range(pieces)]
    wide_f, narrow = jnp.float32, jnp.bfloat16
    middle = (z > 0) & (z < nz - 1)
    side = jnp.where(lax.rem(z, 2) == 0, z + 1, z - 1)
    low = z < nz // 2
    near = [z, side, jnp.where(low, nz // 2, nz // 2 - 1), jnp.where(low, nz - 1, 0)]
    far_end = near[FAR_END]
    columns = [
        (x, y),
        (jnp.where(c == 0, ox, x), jnp.where(c == 0, y, oy)),
        (jnp.where(c == 0, x, ox), jnp.where(c == 0, oy, y)),
        (ox, oy),
    ]

    def dev(zz, xx, cc, yy):
        return ((zz * 2 + xx) * 2 + cc, yy)

    def beside(col, cc):
        xx, yy = columns[col]
        return dev(z, xx, cc, yy)

    dev_a, dev_b, dev_c = beside(FIRST, c), beside(SECOND, c), dev(z, x, oc, y)
    dev_side = dev(side, x, c, y)

    def in_middle(action):
        @pl.when(middle)
        def _():
            action()

    def at_ends(action):
        @pl.when(jnp.logical_not(middle))
        def _():
            action()

    def remote(src, dst, send, recv, to):
        return pltpu.make_async_remote_copy(
            src_ref=src, dst_ref=dst, send_sem=send, recv_sem=recv,
            device_id=to, device_id_type=pl.DeviceIdType.MESH,
        )

    barrier = pltpu.get_barrier_semaphore()

    def greet(to):
        pl.semaphore_signal(barrier, inc=1, device_id=to, device_id_type=pl.DeviceIdType.MESH)

    partners = [dev(near[k], x, cc, y) for k in (FAR_MID, SIDE) for cc in (c, oc)]
    partners += [beside(col, cc) for col in (FIRST, SECOND) for cc in (c, oc)] + [dev_c]

    @pl.when(middle)
    def _():
        for cc in (c, oc):
            greet(dev(far_end, x, cc, y))

    for to in partners:
        greet(to)
    small_loads = [
        pltpu.make_async_copy(ids_hbm, ids_buf, load_sem.at[0]),
        pltpu.make_async_copy(rw_hbm, rw_buf, load_sem.at[1]),
    ]
    tok_loads = [
        pltpu.make_async_copy(
            tok_hbm.at[:, pl.ds(starts[p], widths[p])],
            rows[p].at[y, x, z, c, :, pl.ds(0, widths[p])],
            load_sem.at[2 + p],
        )
        for p in range(pieces)
    ]
    gate_load = pltpu.make_async_copy(gate_hbm.at[0], gate, load_sem.at[pieces + 2])
    up_load = pltpu.make_async_copy(up_hbm.at[0], up, load_sem.at[pieces + 3])

    def down_rows(cc, yy):
        return (
            down_hbm.at[0, :, pl.ds(pl.multiple_of((2 * yy + cc) * half, LANES), half)],
            down.at[yy, pl.ds(pl.multiple_of(c * units, units), units)],
        )

    down_loads = [
        pltpu.make_async_copy(*down_rows(c, yy), load_sem.at[pieces + 4 + yy]) for yy in range(2)
    ]
    for load in small_loads + tok_loads + [gate_load, up_load] + down_loads:
        load.start()
    for load in small_loads:
        load.wait()
    ids = ids_buf[...].astype(wide_f).T
    weights = rw_buf[...].T
    lane = lax.broadcasted_iota(jnp.int32, (tok, LANES), 1)
    which = lax.rem(lane, experts).astype(wide_f)
    spread = jnp.zeros((tok, LANES), wide_f)
    for j in range(top):
        spread = jnp.where(ids[:, j : j + 1] == which, weights[:, j : j + 1], spread)
    first = spread.astype(narrow).astype(wide_f)
    rest = spread - first
    second = rest.astype(narrow).astype(wide_f)
    third = rest - second
    terms = jnp.where(lane < experts, first, jnp.where(lane < 2 * experts, second, third))
    terms = jnp.where(lane < 3 * experts, terms, 0.0)
    rows[0][y, x, z, c, :, widths[0] :] = terms.astype(narrow)
    for load in tok_loads:
        load.wait()
    pl.semaphore_wait(barrier, len(partners) + 2 * middle.astype(jnp.int32))

    def column(p, col, cc=c):
        xx, yy = columns[col]
        return rows[p].at[yy, xx, :, cc]

    def cell(p, col, zz):
        xx, yy = columns[col]
        return rows[p].at[yy, xx, zz, c]

    def layer(zz, cc=c):
        return rows[last].at[:, :, zz, cc]

    def same(ref, send, recv, to):
        return remote(ref, ref, send, recv, to)

    def over_z(k):
        return dev(near[k], x, c, y)

    def z_copy(p, k):
        return same(cell(p, OWN, z), gz_send.at[p], own_recv.at[p, z], over_z(k))

    def relay_copy(p):
        return same(cell(p, OWN, far_end), gr_send.at[p], own_recv.at[p, far_end], dev_side)

    def a_copy(p, zz):
        return same(cell(p, OWN, zz), ga_send.at[p], first_recv.at[p, zz], dev_a)

    def b_copy(p, zz):
        return same(cell(p, OWN, zz), gb_send.at[p, 0], side_recv.at[p, 0], dev_b)

    def d_copy(p, zz):
        return same(cell(p, FIRST, zz), gb_send.at[p, 1], side_recv.at[p, 1], dev_b)

    def c_copy(p, col):
        _, yy = columns[col]
        return same(column(p, col), gc_send.at[p], core_recv.at[p, yy], dev_c)

    def layer_copy(k):
        return same(layer(z), gz_send.at[last], plane_recv.at[z], over_z(k))

    def layer_relay():
        return same(layer(far_end), gr_send.at[last], plane_recv.at[far_end], dev_side)

    def layer_core(zz):
        return same(layer(zz), gc_send.at[last], core_recv.at[last, 0], dev_c)

    def landed(ref, recv):
        same(ref, gr_send.at[last], recv, dev_c).wait_recv()

    def left(ref, send):
        same(ref, send, core_recv.at[last, 0], dev_c).wait_send()

    def to_far(copy):
        copy(FAR_MID).start()

        @pl.when(middle)
        def _():
            copy(FAR_END).start()

    def own(p, k):
        landed(cell(p, OWN, near[k]), own_recv.at[p, near[k]])
        if k == FAR_END:
            in_middle(lambda: relay_copy(p).start())
        a_copy(p, near[k]).start()

    def first_block(p, k):
        landed(cell(p, FIRST, near[k]), first_recv.at[p, near[k]])
        d_copy(p, near[k]).start()

    def sideways(p, j):
        landed(column(p, SECOND + j), side_recv.at[p, j])
        c_copy(p, SECOND + j).start()

    def here():
        for j in range(2):
            landed(cell(last, SECOND + j, z), side_recv.at[last, j])
        to_far(layer_copy)
        layer_copy(SIDE).start()
        layer_core(z).start()

    def layer_in(k):
        landed(layer(near[k]), plane_recv.at[near[k]])
        if k == FAR_END:
            in_middle(lambda: layer_relay().start())
        layer_core(near[k]).start()

    contract = (((1,), (1,)), ((), ()))
    sums, layers_in = [], []

    def share(p, turn_of):
        yy = oy if turn_of else y
        if p < last:
            landed(rows[p].at[yy, :, :, oc], core_recv.at[p, yy])
        elif not layers_in:
            landed(rows[p].at[:, :, :, oc], core_recv.at[p, 0])
            layers_in.append(p)
        if not sums:
            gate_load.wait()
            up_load.wait()
        block = rows[p][yy, :, :, :, :, : widths[p]].reshape(count, widths[p])
        cols = pl.ds(pl.multiple_of(yy * wide + starts[p], LANES), widths[p])
        g = lax.dot_general(block, gate[:, cols], contract, preferred_element_type=wide_f)
        u = lax.dot_general(block, up[:, cols], contract, preferred_element_type=wide_f)
        sums.append((g, u) if not sums else (sums[-1][0] + g, sums[-1][1] + u))

    gather = {
        "zn": lambda p: z_copy(p, SIDE).start(),
        "zf": lambda p: to_far(functools.partial(z_copy, p)),
        "a": lambda p: a_copy(p, z).start(),
        "bd": lambda p, k: b_copy(p, near[k]).start(),
        "own": own,
        "first": first_block,
        "co": lambda p: c_copy(p, OWN).start(),
        "cf": lambda p: c_copy(p, FIRST).start(),
        "cs": lambda p: sideways(p, 0),
        "cd": lambda p: sideways(p, 1),
        "here": here,
        "plane": layer_in,
        "share": share,
    }
    down_copies = []
    for yy in range(2):
        src, dst = down_rows(oc, yy)
        down_copies.append(remote(src, dst, down_send.at[yy], down_recv.at[yy], dev_c))

    def route_scale():
        lanes = lax.broadcasted_iota(jnp.int32, (count, LANES), 1)
        mine = (lax.rem(lanes, experts) == me // 2) & (lanes < 3 * experts)
        kept = rows[0][0, :, :, :, :, widths[0] :].reshape(count, LANES).astype(wide_f)
        return jnp.sum(jnp.where(mine, kept, 0.0), axis=1, keepdims=True)

    shared = []
    started = False
    for name, *where in GATHER:
        if name == "own" and not started:
            for copy in down_copies:
                copy.start()
            started = True
        gather[name](*where)
        if name == "share" and where[0] == 0:
            shared.append(where)
            if len(shared) == 2:
                scale = route_scale()
    gate_act, up_act = sums[-1]
    hid_cols = pl.ds(pl.multiple_of(c * units, units), units)
    hid_copies = []
    for i in range(2):
        part = slice(i * count // 2, (i + 1) * count // 2)
        act = jax.nn.silu(gate_act[part]) * up_act[part] * scale[part]
        hid[part, hid_cols] = act.astype(narrow)
        ref = hid.at[pl.ds(i * count // 2, count // 2), hid_cols]
        hid_copies.append(remote(ref, ref, hid_send.at[i], hid_recv.at[i], dev_c))
        hid_copies[i].start()
    for load in down_loads:
        load.wait()

    def span(r):
        return slice(cuts[r], cuts[r + 1] if r < splits else half)

    def half_term(r, j, core):
        at = pl.ds(pl.multiple_of(core * units, units), units)
        return jnp.dot(hid[:, at], down[oy if j else y, at, span(r)], preferred_element_type=wide_f)

    ahead = {key: half_term(*key, c) for key in [(0, 1), (0, 0)]}
    for copy in down_copies:
        copy.wait_recv()
    for copy in hid_copies:
        copy.wait_recv()

    def project(r, j):
        yy = oy if j else y
        if (r, j) in ahead:
            term = ahead[r, j] + half_term(r, j, oc)
        else:
            term = jnp.dot(hid[...], down[yy, :, span(r)], preferred_element_type=wide_f)
        parts[r][yy] = term.astype(narrow).reshape(2, nz, 2, tok, term.shape[1])

    def block(r, col, zz):
        xx, yy = columns[col]
        return parts[r].at[yy, xx, zz]

    def total(*terms):
        out = terms[0].astype(wide_f)
        for term in terms[1:]:
            out = out + term.astype(wide_f)
        return out

    def rd(k, r):
        zz = near[k]
        return remote(block(r, DIAGONAL, zz), diag_bufs[r].at[zz], rd_send.at[r], rd_recv.at[r, zz], dev_b)

    def rb(k, r):
        zz = near[k]
        return remote(block(r, SECOND, zz), second_bufs[r].at[zz], rb_send.at[r], rb_recv.at[r, zz], dev_b)

    def ra(k, r):
        zz = near[k]
        return remote(block(r, FIRST, zz), first_bufs[r].at[zz], ra_send.at[r], ra_recv.at[r, zz], dev_a)

    def rr(r):
        return remote(block(r, OWN, far_end), relay_bufs[r], rr_send.at[r], rr_recv.at[r], dev_side)

    def rz(k, r, cc):
        zz = near[k]
        return remote(
            block(r, OWN, zz).at[cc], owner_bufs[r].at[c, z], rz_send.at[r], rz_recv.at[r, c], dev(zz, x, cc, y)
        )

    def rc(r):
        return remote(block(r, OWN, z).at[oc], owner_bufs[r].at[c, z], rc_send.at[r], rz_recv.at[r, c], dev_c)

    def landed_slots(ref, slots, recv):
        landed(ref.at[pl.ds(0, slots)], recv)

    def plane(zz):
        return parts[splits].at[:, :, zz]

    def lz(k):
        return remote(plane(near[k]), late_buf.at[z], lz_send, lz_recv, over_z(k))

    def lr():
        return remote(plane(far_end), late_relay, lr_send, lr_recv, dev_side)

    def ld():
        return remote(block(splits, DIAGONAL, z), late_diag, ld_send, ld_recv, dev_b)

    def la(cc):
        return remote(
            block(splits, FIRST, z).at[cc], late_owner.at[c, 0], la_send, lo_recv.at[c], beside(FIRST, cc)
        )

    def lb(cc):
        return remote(
            block(splits, SECOND, z).at[cc], late_owner.at[c, 1], lb_send, lo_recv.at[c], beside(SECOND, cc)
        )

    def lc():
        return remote(block(splits, OWN, z).at[oc], late_owner.at[c, 2], lc_send, lo_recv.at[c], dev_c)

    def send_late(k):
        if k == FAR_END:
            at_ends(lambda: lr().start())
        else:
            lz(k).start()

    def turn(k, r):
        rd(k, r).wait_recv()
        ref = block(r, FIRST, near[k])
        ref[...] = total(ref[...], diag_bufs[r][near[k]]).astype(narrow)
        ra(k, r).start()

    def home(k, r):
        ra(k, r).wait_recv()
        rb(k, r).wait_recv()
        ref = block(r, OWN, near[k])
        ref[...] = total(ref[...], first_bufs[r][near[k]], second_bufs[r][near[k]]).astype(narrow)
        if k == FAR_END:
            at_ends(lambda: rr(r).start())
        elif k == HERE:
            rc(r).start()
        else:
            for cc in range(2):
                rz(k, r, cc).start()

    def relay(r):
        @pl.when(middle)
        def _():
            rr(r).wait_recv()
            ref = block(r, OWN, far_end)
            ref[...] = total(ref[...], relay_bufs[r][...]).astype(narrow)
            for cc in range(2):
                rz(FAR_END, r, cc).start()

    def late_pass():
        @pl.when(middle)
        def _():
            lr().wait_recv()
            ref = plane(far_end)
            ref[...] = total(ref[...], late_relay[...]).astype(narrow)
            lz(FAR_END).start()

    def late_sum():
        ref = plane(z)

        @pl.when(middle)
        def _():
            landed_slots(late_buf, nz - 1, lz_recv)
            ref[...] = total(ref[...], late_buf[side], late_buf[near[FAR_MID]], late_buf[far_end]).astype(narrow)

        @pl.when(jnp.logical_not(middle))
        def _():
            landed_slots(late_buf, nz - 2, lz_recv)
            ref[...] = total(ref[...], late_buf[side], late_buf[near[FAR_MID]]).astype(narrow)

    def late_turn():
        ld().wait_recv()
        ref = block(splits, FIRST, z)
        ref[...] = total(ref[...], late_diag[...]).astype(narrow)
        for cc in range(2):
            la(cc).start()

    def late_out(j):
        core, mine_too = (oc, late_owner.at[oc, 2]) if j else (c, block(splits, OWN, z).at[c])
        landed_slots(late_owner.at[core], 2 + j, lo_recv.at[core])
        at = pl.ds(pl.multiple_of(core * half + cuts[splits], LANES), half - cuts[splits])
        out_ref[:, at] = total(mine_too[...], late_owner[core, 0], late_owner[core, 1]).astype(narrow)

    def out(r, j):
        bufs = owner_bufs[r]
        core, mine_too = (oc, bufs.at[oc, z]) if j else (c, block(r, OWN, z).at[c])
        at = pl.ds(pl.multiple_of(core * half + cuts[r], LANES), cuts[r + 1] - cuts[r])

        @pl.when(middle)
        def _():
            landed_slots(bufs.at[core], nz - 1 + j, rz_recv.at[r, core])
            sums = [bufs[core, near[k]] for k in (SIDE, FAR_MID, FAR_END)]
            out_ref[:, at] = total(mine_too[...], *sums).astype(narrow)

        @pl.when(jnp.logical_not(middle))
        def _():
            landed_slots(bufs.at[core], nz - 2 + j, rz_recv.at[r, core])
            sums = [bufs[core, near[k]] for k in (SIDE, FAR_MID)]
            out_ref[:, at] = total(mine_too[...], *sums).astype(narrow)

    scatter = {
        "downL": lambda: [project(splits, j) for j in (1, 0)],
        "down": project,
        "lz": send_late,
        "rd": lambda k, r: rd(k, r).start(),
        "rb": lambda k, r: rb(k, r).start(),
        "turn": turn,
        "home": home,
        "relay": relay,
        "lrelay": late_pass,
        "lsum": late_sum,
        "ld": lambda: ld().start(),
        "lb": lambda: [lb(cc).start() for cc in range(2)],
        "lc": lambda: lc().start(),
        "lturn": late_turn,
    }
    for name, *where in SCATTER:
        scatter[name](*where)
    for r in range(splits):
        for j in range(2):
            out(r, j)
    for j in range(2):
        late_out(j)

    for p in range(last):
        left(column(p, OWN), ga_send.at[p])
        left(column(p, OWN), gb_send.at[p, 0])
        left(column(p, FIRST), gb_send.at[p, 1])
        left(rows[p].at[:, :, :, c], gc_send.at[p])
    a_copy(last, z).wait_send()
    b_copy(last, z).wait_send()
    d_copy(last, z).wait_send()
    left(rows[last].at[:, :, :, c], gc_send.at[last])
    for r in range(splits):
        left(first_bufs[r], ra_send.at[r])
        left(diag_bufs[r], rd_send.at[r])
        left(second_bufs[r], rb_send.at[r])
        rc(r).wait_send()
    left(late_diag, la_send)
    left(late_diag, lb_send)
    for copy in [ld(), lc()] + hid_copies + down_copies:
        copy.wait_send()

    @pl.when(middle)
    def _():
        for p in range(last):
            left(column(p, OWN).at[pl.ds(0, nz - 1)], gz_send.at[p])
            relay_copy(p).wait_send()
        left(rows[last].at[:, :, pl.ds(0, nz - 1), c], gz_send.at[last])
        layer_relay().wait_send()
        left(late_buf.at[pl.ds(0, nz - 1)], lz_send)
        for r in range(splits):
            left(owner_bufs[r].at[:, pl.ds(0, nz - 1)], rz_send.at[r])

    @pl.when(jnp.logical_not(middle))
    def _():
        lr().wait_send()
        for p in range(last):
            left(column(p, OWN).at[pl.ds(0, nz - 2)], gz_send.at[p])
        left(rows[last].at[:, :, pl.ds(0, nz - 2), c], gz_send.at[last])
        left(late_buf.at[pl.ds(0, nz - 2)], lz_send)
        for r in range(splits):
            rr(r).wait_send()
            left(owner_bufs[r].at[:, pl.ds(0, nz - 2)], rz_send.at[r])


def fused_body(tokens, expert_ids, route_weights, gate_weight, up_weight, down_weight):
    nz = lax.axis_size("expert") // 4
    tok, wide = tokens.shape
    half = wide // 2
    units = gate_weight.shape[1]
    bf16 = jnp.bfloat16
    tiles = wide // (2 * LANES)
    ahead = max(1, tiles * 3 // 14)
    others = tiles - ahead
    widths = [2 * LANES * n for n in ((others + 2) // 3, (others + 1) // 3, others // 3, ahead)]
    lanes = half // LANES
    late = max(1, lanes * 3 // 14)
    cuts = [0, LANES * (lanes * 3 // 7), half - LANES * late]
    splits = len(cuts) - 1
    spans = [b - a for a, b in zip(cuts, cuts[1:])]
    pieces = len(widths)
    vmem = pl.BlockSpec(memory_space=pltpu.VMEM)
    anywhere = pl.BlockSpec(memory_space=pl.ANY)
    sems = pltpu.SemaphoreType.DMA
    spare = [LANES] + [0] * (pieces - 1)
    last = half - cuts[-1]
    return pl.pallas_call(
        functools.partial(fused_kernel, widths, cuts),
        out_shape=pltpu.VMEM((tok, wide), bf16),
        in_specs=[anywhere] * 6,
        out_specs=vmem,
        scratch_shapes=[pltpu.VMEM((2, 2, nz, 2, tok, w + s), bf16) for w, s in zip(widths, spare)]
        + [pltpu.VMEM((2, 2, nz, 2, tok, w), bf16) for w in spans + [last]]
        + [pltpu.VMEM((nz, 2, tok, w), bf16) for _ in range(3) for w in spans]
        + [pltpu.VMEM((2, tok, w), bf16) for w in spans]
        + [pltpu.VMEM((2, nz, tok, w), bf16) for w in spans]
        + [
            pltpu.VMEM((units, 2 * wide), bf16),
            pltpu.VMEM((units, 2 * wide), bf16),
            pltpu.VMEM((2, 2 * units, half), bf16),
            pltpu.VMEM((4 * nz * tok, 2 * units), bf16),
            pltpu.VMEM(expert_ids.shape[::-1], expert_ids.dtype),
            pltpu.VMEM(route_weights.shape[::-1], route_weights.dtype),
            pltpu.VMEM((nz, 2, 2, 2, tok, last), bf16),
            pltpu.VMEM((2, 2, 2, tok, last), bf16),
            pltpu.VMEM((2, tok, last), bf16),
            pltpu.VMEM((2, 3, tok, last), bf16),
            sems((pieces + 6,)),
            sems((pieces - 1, nz)),
            sems((pieces, nz)),
            sems((pieces, 2)),
            sems((nz,)),
            sems((pieces, 2)),
            sems((pieces,)),
            sems((pieces,)),
            sems((pieces,)),
            sems((pieces, 2)),
            sems((pieces,)),
            sems((2,)),
            sems((2,)),
            sems((2,)),
            sems((2,)),
        ]
        + [sems((splits,)), sems((splits, nz))] * 3
        + [
            sems((splits,)),
            sems((splits,)),
            sems((splits,)),
            sems((splits, 2)),
            sems((splits,)),
            sems,
            sems,
            sems,
            sems,
            sems,
            sems,
            sems,
            sems,
            sems,
            sems((2,)),
        ],
        compiler_params=pltpu.CompilerParams(
            collective_id=0, has_side_effects=True, vmem_limit_bytes=60 * 2**20
        ),
    )(tokens, expert_ids.T, route_weights.T, gate_weight, up_weight, down_weight)


def body(*args):
    every = args[1].shape[1] == lax.axis_size("expert") // 2
    tok, wide = args[0].shape
    even = lax.axis_size("tensor") == 2 and lax.axis_size("expert") == 16
    fits = tok % 16 == 0 and wide % 512 == 0 and 3 * args[1].shape[1] <= LANES
    if every and even and fits:
        return fused_body(*args)
    return sparse_body(*args)


def solution(mesh):
    placed = (
        P("expert", "tensor"),
        P("expert", None),
        P("expert", None),
        P("expert", "tensor", None),
        P("expert", "tensor", None),
        P("expert", "tensor", None),
    )
    return jax.shard_map(
        body, mesh=mesh, in_specs=placed, out_specs=P("expert", "tensor"), check_vma=False
    )
```

```python
import functools

import jax
import jax.numpy as jnp
from jax import lax
from jax.experimental import pallas as pl
from jax.experimental.pallas import tpu as pltpu
from jax.sharding import PartitionSpec as P

LANES = 128


def rows_times(rows, weight):
    return lax.dot_general(
        rows, weight, (((1,), (1,)), ((), ())), preferred_element_type=jnp.float32
    )


def sparse_body(tokens, expert_ids, route_weights, gate_weight, up_weight, down_weight):
    devices_wide = lax.axis_size("expert")
    experts = devices_wide // 2
    tok_count = expert_ids.shape[0]
    per_token = expert_ids.shape[1]
    capacity = min(tok_count, tok_count * per_token // experts)
    slot_count = experts * capacity
    arrived_count = devices_wide * capacity
    expert_range = jnp.arange(experts, dtype=jnp.int32)
    onehot = jnp.sum(
        (expert_ids[:, :, None] == expert_range[None, None, :]).astype(jnp.int32), axis=1
    )
    token_range = jnp.arange(tok_count, dtype=jnp.int32)
    earlier = token_range[None, :, None] < token_range[:, None, None]
    earlier_count = jnp.sum(jnp.where(earlier, onehot[None, :, :], 0), axis=1)
    slot_rank = jnp.take_along_axis(earlier_count, expert_ids, axis=1)
    slot_of = expert_ids * capacity + slot_rank
    slot_range = jnp.arange(slot_count, dtype=jnp.int32)
    select = jnp.any(slot_of[None, :, :] == slot_range[:, None, None], axis=2).astype(jnp.bfloat16)
    weight_gate = gate_weight[0]
    weight_up = up_weight[0]
    weight_out = down_weight[0]
    whole_rows = lax.all_gather(tokens, "tensor", axis=1, tiled=True)
    packed = jnp.dot(select, whole_rows, preferred_element_type=jnp.float32).astype(jnp.bfloat16)
    packed = packed.reshape(experts, capacity, whole_rows.shape[1])
    arrived = lax.all_to_all(
        jnp.repeat(packed, 2, axis=0), "expert", split_axis=0, concat_axis=0, tiled=True
    ).reshape(arrived_count, -1)
    gate_act = rows_times(arrived, weight_gate)
    up_act = rows_times(arrived, weight_up)
    hidden = (jax.nn.silu(gate_act) * up_act).astype(jnp.bfloat16)
    columns = lax.all_to_all(weight_out, "tensor", split_axis=1, concat_axis=0, tiled=True)
    unit_count = hidden.shape[1]
    shard_piece = lax.all_gather(hidden, "tensor", axis=1, tiled=True)
    groups = shard_piece.shape[1] // unit_count
    weight_rows = columns
    weight_rows = weight_rows.reshape(groups, unit_count, columns.shape[1])
    grouped = shard_piece.reshape(shard_piece.shape[0], groups, unit_count)
    group_terms = jnp.einsum(
        "rgf,gfd->grd", grouped, weight_rows, preferred_element_type=jnp.float32
    ).astype(jnp.bfloat16)
    group_terms = lax.optimization_barrier(group_terms)
    half_out = jnp.sum(group_terms.astype(jnp.float32), axis=0).astype(jnp.bfloat16)
    returned = lax.all_to_all(
        half_out.reshape(devices_wide, capacity, -1),
        "expert",
        split_axis=0,
        concat_axis=0,
        tiled=True,
    )
    returned = returned.reshape(experts, 2, capacity, -1).astype(jnp.float32)
    combined = (returned[:, 0] + returned[:, 1]).reshape(slot_count, -1)
    picked = combined[slot_of]
    mixed_out = jnp.sum(route_weights[:, :, None] * picked, axis=1)
    return mixed_out.astype(jnp.bfloat16)


OWN, FIRST, SECOND, DIAGONAL = range(4)
HERE, SIDE, FAR_MID, FAR_END = range(4)
GATHER = (
    ('zn', 1), ('bd', 0, 0), ('zf', 0), ('zn', 0), ('bd', 1, 0), ('a', 3), ('a', 2), ('a', 0), ('bd', 3, 0), ('a', 1),
    ('own', 1, 1), ('zf', 1), ('zn', 2), ('bd', 1, 1), ('own', 0, 2), ('first', 3, 0), ('bd', 2, 0), ('zf', 2),
    ('bd', 0, 2), ('own', 0, 3), ('first', 0, 0), ('bd', 0, 3), ('own', 0, 1), ('bd', 0, 1), ('own', 2, 1),
    ('bd', 2, 1), ('here',), ('own', 1, 2), ('bd', 1, 2), ('own', 2, 2), ('first', 1, 1), ('co', 0), ('own', 1, 3),
    ('bd', 1, 3), ('cs', 0), ('first', 0, 1), ('co', 1), ('bd', 2, 2), ('own', 2, 3), ('bd', 2, 3), ('first', 0, 3),
    ('first', 0, 2), ('cf', 0), ('first', 1, 2), ('first', 2, 1), ('first', 2, 0), ('cs', 1), ('plane', 1), ('co', 2),
    ('first', 1, 3), ('first', 1, 0), ('cf', 1), ('cs', 2), ('first', 2, 2), ('first', 2, 3), ('cf', 2), ('plane', 2),
    ('cd', 0), ('share', 0, 0), ('plane', 3), ('cd', 1), ('share', 1, 0), ('share', 0, 1), ('cd', 2), ('share', 2, 0),
    ('share', 3, 1), ('share', 1, 1), ('share', 3, 0), ('share', 2, 1),
)
SCATTER = (
    ('down', 0), ('rd', 2, 0), ('rd', 3, 0), ('downL',), ('lz', 3), ('lz', 2), ('down', 1), ('rb', 1, 0),
    ('rd', 2, 1), ('rd', 3, 1), ('rd', 1, 1), ('rb', 3, 0), ('turn', 3, 0), ('lz', 1), ('turn', 2, 0), ('rb', 2, 0),
    ('turn', 3, 1), ('rd', 1, 0), ('rb', 3, 1), ('lrelay',), ('turn', 1, 1), ('rd', 0, 0), ('rb', 2, 1), ('rb', 1, 1),
    ('home', 3, 0), ('home', 2, 0), ('rd', 0, 1), ('turn', 2, 1), ('turn', 1, 0), ('home', 3, 1), ('lsum',), ('ld',),
    ('rb', 0, 1), ('rb', 0, 0), ('turn', 0, 0), ('home', 1, 1), ('home', 2, 1), ('relay', 0), ('turn', 0, 1),
    ('home', 1, 0), ('lb',), ('relay', 1), ('lturn',), ('lc',), ('home', 0, 0), ('home', 0, 1),
)


def fused_kernel(
    widths, cuts, tok_hbm, ids_hbm, rw_hbm, gate_hbm, up_hbm, down_hbm, out_ref, *scratch
):
    pieces, splits = len(widths), len(cuts) - 1
    rows, scratch = scratch[:pieces], scratch[pieces:]
    parts, scratch = scratch[: splits + 1], scratch[splits + 1 :]
    diag_bufs, scratch = scratch[:splits], scratch[splits:]
    first_bufs, scratch = scratch[:splits], scratch[splits:]
    second_bufs, scratch = scratch[:splits], scratch[splits:]
    relay_bufs, scratch = scratch[:splits], scratch[splits:]
    owner_bufs, scratch = scratch[:splits], scratch[splits:]
    (
        gate, up, down, hid, ids_buf, rw_buf, late_buf, late_relay, late_diag, late_owner,
        load_sem, own_recv, first_recv, side_recv, plane_recv, core_recv, gz_send, gr_send, ga_send, gb_send, gc_send,
        down_send, down_recv, hid_send, hid_recv,
        rd_send, rd_recv, ra_send, ra_recv, rb_send, rb_recv, rr_send, rr_recv, rz_send, rz_recv, rc_send,
        lz_send, lz_recv, lr_send, lr_recv, ld_send, ld_recv, la_send, lb_send, lc_send, lo_recv,
    ) = scratch
    nz = rows[0].shape[2]
    me, y = lax.axis_index("expert"), lax.axis_index("tensor")
    c = lax.rem(me, 2)
    x = lax.rem(me // 2, 2)
    z = me // 4
    oc, ox, oy = 1 - c, 1 - x, 1 - y
    tok, wide = out_ref.shape
    half = wide // 2
    units = gate.shape[0]
    experts = 2 * nz
    count = 4 * nz * tok
    top = ids_hbm.shape[0]
    last = pieces - 1
    starts = [sum(widths[:p]) for p in range(pieces)]
    wide_f, narrow = jnp.float32, jnp.bfloat16
    middle = (z > 0) & (z < nz - 1)
    side = jnp.where(lax.rem(z, 2) == 0, z + 1, z - 1)
    low = z < nz // 2
    near = [z, side, jnp.where(low, nz // 2, nz // 2 - 1), jnp.where(low, nz - 1, 0)]
    far_end = near[FAR_END]
    columns = [
        (x, y),
        (jnp.where(c == 0, ox, x), jnp.where(c == 0, y, oy)),
        (jnp.where(c == 0, x, ox), jnp.where(c == 0, oy, y)),
        (ox, oy),
    ]

    def dev(zz, xx, cc, yy):
        return ((zz * 2 + xx) * 2 + cc, yy)

    def beside(col, cc):
        xx, yy = columns[col]
        return dev(z, xx, cc, yy)

    dev_a, dev_b, dev_c = beside(FIRST, c), beside(SECOND, c), dev(z, x, oc, y)
    dev_side = dev(side, x, c, y)

    def in_middle(action):
        @pl.when(middle)
        def _():
            action()

    def at_ends(action):
        @pl.when(jnp.logical_not(middle))
        def _():
            action()

    def remote(src, dst, send, recv, to):
        return pltpu.make_async_remote_copy(
            src_ref=src, dst_ref=dst, send_sem=send, recv_sem=recv,
            device_id=to, device_id_type=pl.DeviceIdType.MESH,
        )

    barrier = pltpu.get_barrier_semaphore()

    def greet(to):
        pl.semaphore_signal(barrier, inc=1, device_id=to, device_id_type=pl.DeviceIdType.MESH)

    partners = [dev(near[k], x, cc, y) for k in (FAR_MID, SIDE) for cc in (c, oc)]
    partners += [beside(col, cc) for col in (FIRST, SECOND) for cc in (c, oc)] + [dev_c]

    @pl.when(middle)
    def _():
        for cc in (c, oc):
            greet(dev(far_end, x, cc, y))

    for to in partners:
        greet(to)
    small_loads = [
        pltpu.make_async_copy(ids_hbm, ids_buf, load_sem.at[0]),
        pltpu.make_async_copy(rw_hbm, rw_buf, load_sem.at[1]),
    ]
    tok_loads = [
        pltpu.make_async_copy(
            tok_hbm.at[:, pl.ds(starts[p], widths[p])],
            rows[p].at[y, x, z, c, :, pl.ds(0, widths[p])],
            load_sem.at[2 + p],
        )
        for p in range(pieces)
    ]
    gate_load = pltpu.make_async_copy(gate_hbm.at[0], gate, load_sem.at[pieces + 2])
    up_load = pltpu.make_async_copy(up_hbm.at[0], up, load_sem.at[pieces + 3])

    def down_rows(cc, yy):
        return (
            down_hbm.at[0, :, pl.ds(pl.multiple_of((2 * yy + cc) * half, LANES), half)],
            down.at[yy, pl.ds(pl.multiple_of(c * units, units), units)],
        )

    down_loads = [
        pltpu.make_async_copy(*down_rows(c, yy), load_sem.at[pieces + 4 + yy]) for yy in range(2)
    ]
    for load in small_loads + tok_loads + [gate_load, up_load] + down_loads:
        load.start()
    for load in small_loads:
        load.wait()
    ids = ids_buf[...].astype(wide_f).T
    weights = rw_buf[...].T
    lane = lax.broadcasted_iota(jnp.int32, (tok, LANES), 1)
    which = lax.rem(lane, experts).astype(wide_f)
    spread = jnp.zeros((tok, LANES), wide_f)
    for j in range(top):
        spread = jnp.where(ids[:, j : j + 1] == which, weights[:, j : j + 1], spread)
    first = spread.astype(narrow).astype(wide_f)
    rest = spread - first
    second = rest.astype(narrow).astype(wide_f)
    third = rest - second
    terms = jnp.where(lane < experts, first, jnp.where(lane < 2 * experts, second, third))
    terms = jnp.where(lane < 3 * experts, terms, 0.0)
    rows[0][y, x, z, c, :, widths[0] :] = terms.astype(narrow)
    for load in tok_loads:
        load.wait()
    pl.semaphore_wait(barrier, len(partners) + 2 * middle.astype(jnp.int32))

    def column(p, col, cc=c):
        xx, yy = columns[col]
        return rows[p].at[yy, xx, :, cc]

    def cell(p, col, zz):
        xx, yy = columns[col]
        return rows[p].at[yy, xx, zz, c]

    def layer(zz, cc=c):
        return rows[last].at[:, :, zz, cc]

    def same(ref, send, recv, to):
        return remote(ref, ref, send, recv, to)

    def over_z(k):
        return dev(near[k], x, c, y)

    def z_copy(p, k):
        return same(cell(p, OWN, z), gz_send.at[p, k - 1], own_recv.at[p, z], over_z(k))

    def relay_copy(p):
        return same(cell(p, OWN, far_end), gr_send.at[p], own_recv.at[p, far_end], dev_side)

    def a_copy(p, zz):
        return same(cell(p, OWN, zz), ga_send.at[p], first_recv.at[p, zz], dev_a)

    def b_copy(p, zz):
        return same(cell(p, OWN, zz), gb_send.at[p, 0], side_recv.at[p, 0], dev_b)

    def d_copy(p, zz):
        return same(cell(p, FIRST, zz), gb_send.at[p, 1], side_recv.at[p, 1], dev_b)

    def c_copy(p, col):
        _, yy = columns[col]
        return same(column(p, col), gc_send.at[p], core_recv.at[p, yy], dev_c)

    def layer_copy(k):
        return same(layer(z), gz_send.at[last, k - 1], plane_recv.at[z], over_z(k))

    def layer_relay():
        return same(layer(far_end), gr_send.at[last], plane_recv.at[far_end], dev_side)

    def layer_core(zz):
        return same(layer(zz), gc_send.at[last], core_recv.at[last, 0], dev_c)

    def landed(ref, recv):
        same(ref, gr_send.at[last], recv, dev_c).wait_recv()

    def left(ref, send):
        same(ref, send, core_recv.at[last, 0], dev_c).wait_send()

    def to_far(copy):
        copy(FAR_MID).start()

        @pl.when(middle)
        def _():
            copy(FAR_END).start()

    def own(p, k):
        landed(cell(p, OWN, near[k]), own_recv.at[p, near[k]])
        if k == FAR_END:
            in_middle(lambda: relay_copy(p).start())
        a_copy(p, near[k]).start()

    def first_block(p, k):
        landed(cell(p, FIRST, near[k]), first_recv.at[p, near[k]])
        d_copy(p, near[k]).start()

    def sideways(p, j):
        landed(column(p, SECOND + j), side_recv.at[p, j])
        c_copy(p, SECOND + j).start()

    def here():
        for j in range(2):
            landed(cell(last, SECOND + j, z), side_recv.at[last, j])
        to_far(layer_copy)
        layer_copy(SIDE).start()
        layer_core(z).start()

    def layer_in(k):
        landed(layer(near[k]), plane_recv.at[near[k]])
        if k == FAR_END:
            in_middle(lambda: layer_relay().start())
        layer_core(near[k]).start()

    contract = (((1,), (1,)), ((), ()))
    sums, layers_in = [], []

    def share(p, turn_of):
        yy = oy if turn_of else y
        if p < last:
            landed(rows[p].at[yy, :, :, oc], core_recv.at[p, yy])
        elif not layers_in:
            landed(rows[p].at[:, :, :, oc], core_recv.at[p, 0])
            layers_in.append(p)
        if not sums:
            gate_load.wait()
            up_load.wait()
        block = rows[p][yy, :, :, :, :, : widths[p]].reshape(count, widths[p])
        cols = pl.ds(pl.multiple_of(yy * wide + starts[p], LANES), widths[p])
        g = lax.dot_general(block, gate[:, cols], contract, preferred_element_type=wide_f)
        u = lax.dot_general(block, up[:, cols], contract, preferred_element_type=wide_f)
        sums.append((g, u) if not sums else (sums[-1][0] + g, sums[-1][1] + u))

    gather = {
        "zn": lambda p: z_copy(p, SIDE).start(),
        "zf": lambda p: to_far(functools.partial(z_copy, p)),
        "a": lambda p: a_copy(p, z).start(),
        "bd": lambda p, k: b_copy(p, near[k]).start(),
        "own": own,
        "first": first_block,
        "co": lambda p: c_copy(p, OWN).start(),
        "cf": lambda p: c_copy(p, FIRST).start(),
        "cs": lambda p: sideways(p, 0),
        "cd": lambda p: sideways(p, 1),
        "here": here,
        "plane": layer_in,
        "share": share,
    }
    down_copies = []
    for yy in range(2):
        src, dst = down_rows(oc, yy)
        down_copies.append(remote(src, dst, down_send.at[yy], down_recv.at[yy], dev_c))

    def route_scale():
        lanes = lax.broadcasted_iota(jnp.int32, (count, LANES), 1)
        mine = (lax.rem(lanes, experts) == me // 2) & (lanes < 3 * experts)
        kept = rows[0][0, :, :, :, :, widths[0] :].reshape(count, LANES).astype(wide_f)
        return jnp.sum(jnp.where(mine, kept, 0.0), axis=1, keepdims=True)

    shared = []
    started = False
    for name, *where in GATHER:
        if name == "own" and not started:
            for copy in down_copies:
                copy.start()
            started = True
        gather[name](*where)
        if name == "share" and where[0] == 0:
            shared.append(where)
            if len(shared) == 2:
                scale = route_scale()
    gate_act, up_act = sums[-1]
    hid_cols = pl.ds(pl.multiple_of(c * units, units), units)
    hid_copies = []
    for i in range(2):
        part = slice(i * count // 2, (i + 1) * count // 2)
        act = jax.nn.silu(gate_act[part]) * up_act[part] * scale[part]
        hid[part, hid_cols] = act.astype(narrow)
        ref = hid.at[pl.ds(i * count // 2, count // 2), hid_cols]
        hid_copies.append(remote(ref, ref, hid_send.at[i], hid_recv.at[i], dev_c))
        hid_copies[i].start()
    for load in down_loads:
        load.wait()
    for copy in down_copies:
        copy.wait_recv()
    for copy in hid_copies:
        copy.wait_recv()

    def project(r):
        begin, end = cuts[r], cuts[r + 1] if r < splits else half
        for yy in range(2):
            term = jnp.dot(hid[...], down[yy, :, begin:end], preferred_element_type=wide_f)
            parts[r][yy] = term.astype(narrow).reshape(2, nz, 2, tok, end - begin)

    def block(r, col, zz):
        xx, yy = columns[col]
        return parts[r].at[yy, xx, zz]

    def total(*terms):
        out = terms[0].astype(wide_f)
        for term in terms[1:]:
            out = out + term.astype(wide_f)
        return out

    def rd(k, r):
        zz = near[k]
        return remote(block(r, DIAGONAL, zz), diag_bufs[r].at[zz], rd_send.at[r], rd_recv.at[r, zz], dev_b)

    def rb(k, r):
        zz = near[k]
        return remote(block(r, SECOND, zz), second_bufs[r].at[zz], rb_send.at[r], rb_recv.at[r, zz], dev_b)

    def ra(k, r):
        zz = near[k]
        return remote(block(r, FIRST, zz), first_bufs[r].at[zz], ra_send.at[r], ra_recv.at[r, zz], dev_a)

    def rr(r):
        return remote(block(r, OWN, far_end), relay_bufs[r], rr_send.at[r], rr_recv.at[r], dev_side)

    def rz(k, r, cc):
        zz = near[k]
        return remote(
            block(r, OWN, zz).at[cc], owner_bufs[r].at[c, z], rz_send.at[r, k - 1], rz_recv.at[r, c], dev(zz, x, cc, y)
        )

    def rc(r):
        return remote(block(r, OWN, z).at[oc], owner_bufs[r].at[c, z], rc_send.at[r], rz_recv.at[r, c], dev_c)

    def landed_slots(ref, slots, recv):
        landed(ref.at[pl.ds(0, slots)], recv)

    def plane(zz):
        return parts[splits].at[:, :, zz]

    def lz(k):
        return remote(plane(near[k]), late_buf.at[z], lz_send.at[k - 1], lz_recv, over_z(k))

    def lr():
        return remote(plane(far_end), late_relay, lr_send, lr_recv, dev_side)

    def ld():
        return remote(block(splits, DIAGONAL, z), late_diag, ld_send, ld_recv, dev_b)

    def la(cc):
        return remote(
            block(splits, FIRST, z).at[cc], late_owner.at[c, 0], la_send, lo_recv.at[c], beside(FIRST, cc)
        )

    def lb(cc):
        return remote(
            block(splits, SECOND, z).at[cc], late_owner.at[c, 1], lb_send, lo_recv.at[c], beside(SECOND, cc)
        )

    def lc():
        return remote(block(splits, OWN, z).at[oc], late_owner.at[c, 2], lc_send, lo_recv.at[c], dev_c)

    def send_late(k):
        if k == FAR_END:
            at_ends(lambda: lr().start())
        else:
            lz(k).start()

    def turn(k, r):
        rd(k, r).wait_recv()
        ref = block(r, FIRST, near[k])
        ref[...] = total(ref[...], diag_bufs[r][near[k]]).astype(narrow)
        ra(k, r).start()

    def home(k, r):
        ra(k, r).wait_recv()
        rb(k, r).wait_recv()
        ref = block(r, OWN, near[k])
        ref[...] = total(ref[...], first_bufs[r][near[k]], second_bufs[r][near[k]]).astype(narrow)
        if k == FAR_END:
            at_ends(lambda: rr(r).start())
        elif k == HERE:
            rc(r).start()
        else:
            for cc in range(2):
                rz(k, r, cc).start()

    def relay(r):
        @pl.when(middle)
        def _():
            rr(r).wait_recv()
            ref = block(r, OWN, far_end)
            ref[...] = total(ref[...], relay_bufs[r][...]).astype(narrow)
            for cc in range(2):
                rz(FAR_END, r, cc).start()

    def late_pass():
        @pl.when(middle)
        def _():
            lr().wait_recv()
            ref = plane(far_end)
            ref[...] = total(ref[...], late_relay[...]).astype(narrow)
            lz(FAR_END).start()

    def late_sum():
        ref = plane(z)

        @pl.when(middle)
        def _():
            landed_slots(late_buf, nz - 1, lz_recv)
            ref[...] = total(ref[...], late_buf[side], late_buf[near[FAR_MID]], late_buf[far_end]).astype(narrow)

        @pl.when(jnp.logical_not(middle))
        def _():
            landed_slots(late_buf, nz - 2, lz_recv)
            ref[...] = total(ref[...], late_buf[side], late_buf[near[FAR_MID]]).astype(narrow)

    def late_turn():
        ld().wait_recv()
        ref = block(splits, FIRST, z)
        ref[...] = total(ref[...], late_diag[...]).astype(narrow)
        for cc in range(2):
            la(cc).start()

    def late_out(j):
        core, mine_too = (oc, late_owner.at[oc, 2]) if j else (c, block(splits, OWN, z).at[c])
        landed_slots(late_owner.at[core], 2 + j, lo_recv.at[core])
        at = pl.ds(pl.multiple_of(core * half + cuts[splits], LANES), half - cuts[splits])
        out_ref[:, at] = total(mine_too[...], late_owner[core, 0], late_owner[core, 1]).astype(narrow)

    def out(r, j):
        bufs = owner_bufs[r]
        core, mine_too = (oc, bufs.at[oc, z]) if j else (c, block(r, OWN, z).at[c])
        at = pl.ds(pl.multiple_of(core * half + cuts[r], LANES), cuts[r + 1] - cuts[r])

        @pl.when(middle)
        def _():
            landed_slots(bufs.at[core], nz - 1 + j, rz_recv.at[r, core])
            sums = [bufs[core, near[k]] for k in (SIDE, FAR_MID, FAR_END)]
            out_ref[:, at] = total(mine_too[...], *sums).astype(narrow)

        @pl.when(jnp.logical_not(middle))
        def _():
            landed_slots(bufs.at[core], nz - 2 + j, rz_recv.at[r, core])
            sums = [bufs[core, near[k]] for k in (SIDE, FAR_MID)]
            out_ref[:, at] = total(mine_too[...], *sums).astype(narrow)

    scatter = {
        "downL": lambda: project(splits),
        "down": project,
        "lz": send_late,
        "rd": lambda k, r: rd(k, r).start(),
        "rb": lambda k, r: rb(k, r).start(),
        "turn": turn,
        "home": home,
        "relay": relay,
        "lrelay": late_pass,
        "lsum": late_sum,
        "ld": lambda: ld().start(),
        "lb": lambda: [lb(cc).start() for cc in range(2)],
        "lc": lambda: lc().start(),
        "lturn": late_turn,
    }
    for name, *where in SCATTER:
        scatter[name](*where)
    for r in range(splits):
        for j in range(2):
            out(r, j)
    for j in range(2):
        late_out(j)

    for p in range(last):
        z_copy(p, SIDE).wait_send()
        z_copy(p, FAR_MID).wait_send()
        left(column(p, OWN), ga_send.at[p])
        left(column(p, OWN), gb_send.at[p, 0])
        left(column(p, FIRST), gb_send.at[p, 1])
        left(rows[p].at[:, :, :, c], gc_send.at[p])
    a_copy(last, z).wait_send()
    b_copy(last, z).wait_send()
    d_copy(last, z).wait_send()
    layer_copy(SIDE).wait_send()
    layer_copy(FAR_MID).wait_send()
    left(rows[last].at[:, :, :, c], gc_send.at[last])
    for r in range(splits):
        left(first_bufs[r], ra_send.at[r])
        left(diag_bufs[r], rd_send.at[r])
        left(second_bufs[r], rb_send.at[r])
        left(relay_bufs[r], rz_send.at[r, SIDE - 1])
        left(relay_bufs[r], rz_send.at[r, FAR_MID - 1])
        rc(r).wait_send()
    left(late_diag, la_send)
    left(late_diag, lb_send)
    for copy in [lz(SIDE), lz(FAR_MID), ld(), lc()] + hid_copies + down_copies:
        copy.wait_send()

    @pl.when(middle)
    def _():
        for p in range(last):
            z_copy(p, FAR_END).wait_send()
            relay_copy(p).wait_send()
        layer_copy(FAR_END).wait_send()
        layer_relay().wait_send()
        lz(FAR_END).wait_send()
        for r in range(splits):
            left(relay_bufs[r], rz_send.at[r, FAR_END - 1])

    @pl.when(jnp.logical_not(middle))
    def _():
        lr().wait_send()
        for r in range(splits):
            rr(r).wait_send()


def fused_body(tokens, expert_ids, route_weights, gate_weight, up_weight, down_weight):
    nz = lax.axis_size("expert") // 4
    tok, wide = tokens.shape
    half = wide // 2
    units = gate_weight.shape[1]
    bf16 = jnp.bfloat16
    tiles = wide // (2 * LANES)
    ahead = max(1, tiles * 3 // 14)
    others = tiles - ahead
    widths = [2 * LANES * n for n in ((others + 2) // 3, (others + 1) // 3, others // 3, ahead)]
    lanes = half // LANES
    late = max(1, lanes * 3 // 14)
    cuts = [0, LANES * (lanes * 3 // 7), half - LANES * late]
    splits = len(cuts) - 1
    spans = [b - a for a, b in zip(cuts, cuts[1:])]
    pieces = len(widths)
    vmem = pl.BlockSpec(memory_space=pltpu.VMEM)
    anywhere = pl.BlockSpec(memory_space=pl.ANY)
    sems = pltpu.SemaphoreType.DMA
    spare = [LANES] + [0] * (pieces - 1)
    last = half - cuts[-1]
    return pl.pallas_call(
        functools.partial(fused_kernel, widths, cuts),
        out_shape=pltpu.VMEM((tok, wide), bf16),
        in_specs=[anywhere] * 6,
        out_specs=vmem,
        scratch_shapes=[pltpu.VMEM((2, 2, nz, 2, tok, w + s), bf16) for w, s in zip(widths, spare)]
        + [pltpu.VMEM((2, 2, nz, 2, tok, w), bf16) for w in spans + [last]]
        + [pltpu.VMEM((nz, 2, tok, w), bf16) for _ in range(3) for w in spans]
        + [pltpu.VMEM((2, tok, w), bf16) for w in spans]
        + [pltpu.VMEM((2, nz, tok, w), bf16) for w in spans]
        + [
            pltpu.VMEM((units, 2 * wide), bf16),
            pltpu.VMEM((units, 2 * wide), bf16),
            pltpu.VMEM((2, 2 * units, half), bf16),
            pltpu.VMEM((4 * nz * tok, 2 * units), bf16),
            pltpu.VMEM(expert_ids.shape[::-1], expert_ids.dtype),
            pltpu.VMEM(route_weights.shape[::-1], route_weights.dtype),
            pltpu.VMEM((nz, 2, 2, 2, tok, last), bf16),
            pltpu.VMEM((2, 2, 2, tok, last), bf16),
            pltpu.VMEM((2, tok, last), bf16),
            pltpu.VMEM((2, 3, tok, last), bf16),
            sems((pieces + 6,)),
            sems((pieces - 1, nz)),
            sems((pieces, nz)),
            sems((pieces, 2)),
            sems((nz,)),
            sems((pieces, 2)),
            sems((pieces, 3)),
            sems((pieces,)),
            sems((pieces,)),
            sems((pieces, 2)),
            sems((pieces,)),
            sems((2,)),
            sems((2,)),
            sems((2,)),
            sems((2,)),
        ]
        + [sems((splits,)), sems((splits, nz))] * 3
        + [
            sems((splits,)),
            sems((splits,)),
            sems((splits, 3)),
            sems((splits, 2)),
            sems((splits,)),
            sems((3,)),
            sems,
            sems,
            sems,
            sems,
            sems,
            sems,
            sems,
            sems,
            sems((2,)),
        ],
        compiler_params=pltpu.CompilerParams(
            collective_id=0, has_side_effects=True, vmem_limit_bytes=60 * 2**20
        ),
    )(tokens, expert_ids.T, route_weights.T, gate_weight, up_weight, down_weight)


def body(*args):
    every = args[1].shape[1] == lax.axis_size("expert") // 2
    tok, wide = args[0].shape
    even = lax.axis_size("tensor") == 2 and lax.axis_size("expert") == 16
    fits = tok % 16 == 0 and wide % 512 == 0 and 3 * args[1].shape[1] <= LANES
    if every and even and fits:
        return fused_body(*args)
    return sparse_body(*args)


def solution(mesh):
    placed = (
        P("expert", "tensor"),
        P("expert", None),
        P("expert", None),
        P("expert", "tensor", None),
        P("expert", "tensor", None),
        P("expert", "tensor", None),
    )
    return jax.shard_map(
        body, mesh=mesh, in_specs=placed, out_specs=P("expert", "tensor"), check_vma=False
    )
```
